512 devices in a mesh: fsdp: 16 (over z, core), req: 32 (over y, x).
Axes of the slice: x: 4, y: 8, z: 8, core: 2. Of those that a mesh axis runs over, the one named last changes fastest.
Arguments:
- drafts: bfloat16 [32, 16, 2560], P('req'), may hold values from -6 to 6
- x_weight: bfloat16 [2560, 5120], P('req', 'fsdp'), may hold values from -0.125 to 0.125
- z_weight: bfloat16 [2560, 5120], P('req', 'fsdp'), may hold values from -0.125 to 0.125
- bc_weight: bfloat16 [2560, 256], P('req'), may hold values from -0.125 to 0.125
- dt_weight: bfloat16 [2560, 80], P('req', 'fsdp'), may hold values from -0.125 to 0.125
- dt_bias: float32 [80], P('fsdp'), may hold values from -3 to 0
- decay_rate: float32 [80], P('fsdp'), may hold values from 0.01 to 0.5
- conv_x_weight: bfloat16 [4, 5120], P(None, 'fsdp'), may hold values from -3 to 3
- conv_x_bias: bfloat16 [5120], P('fsdp'), may hold values from -2 to 2
- conv_bc_weight: bfloat16 [4, 256], replicated, may hold values from -3 to 3
- conv_bc_bias: bfloat16 [256], replicated, may hold values from -2 to 2
- norm_gain: bfloat16 [5120], P('fsdp'), may hold values from 0.5 to 1.5
- out_weight: bfloat16 [5120, 2560], P('fsdp', 'req'), may hold values from -0.078125 to 0.078125
- conv_x_state: bfloat16 [32, 3, 5120], P('req', None, 'fsdp'), may hold values from -6 to 6
- conv_bc_state: bfloat16 [32, 3, 256], P('req'), may hold values from -6 to 6
- ssm_state: float32 [32, 80, 64, 128], P('req', 'fsdp'), may hold values from -6 to 6
- sink_x: bfloat16 [32, 4, 5120], P('req', None, 'fsdp'), may hold values from -12 to 12
- sink_b: bfloat16 [32, 4, 128], P('req'), may hold values from -6 to 6
- page_x: bfloat16 [320, 256, 5120], P('req', None, 'fsdp'), may hold values from -3 to 3
- page_b: bfloat16 [320, 256, 128], P('req'), may hold values from -6 to 6
- page_decay: float32 [320, 80, 256], P('req', 'fsdp')
- slot_req: int32 [320], P('req'), may hold values from -1 to 31, as said below
- slot_page: int32 [320], P('req'), may hold values from 0 to 15, as said below
- page_count: int32 [32], replicated, may hold values from 1 to 16, as said below
- accepted: int32 [32], P('req'), may hold values from 1 to 16
- owner_row: int32 [32], replicated, may hold values from 0 to 31, each once
Outputs:
- mixed: bfloat16 [32, 16, 2560], P('req', None, 'fsdp')
- new_state: float32 [32, 80, 64, 128], P('req', 'fsdp')
- new_conv_x: bfloat16 [32, 3, 5120], P('req', None, 'fsdp')
- new_conv_bc: bfloat16 [32, 3, 256], P('req')
The draws below stay inside these ranges and needn't reach their ends.
Inputs may be any that keep to these rules, and one draw needn't show every extreme that they name: `page_count`: one request has 16 pages. `slot_req`: -1 marks an empty slot. Each page 0 to page_count - 1 of every request stands in exactly one slot; a request with fewer than 16 pages also has its page numbered page_count in one slot. `slot_page`: 0 in empty slots. `owner_row`: each row once.
All inputs are finite; a program needn't handle non-finite values.
Results may differ from the reference program's by a relative error of at most 0.015.
Values may be sent and summed in bfloat16 or wider, within the bound.
A program may use at most 64 MiB of HBM per device.

```python
import math
import jax
import jax.numpy as jnp
from jax import lax

D = 2560
ATTENDER_COUNT = 80
HD = 64
NS = 128
KC = 4
E = 5120
DRAFT = 16
PAGE = 256
WPAGES = 16
SINKS = 4
QUERY_SEQ_COUNT = 32
SLOTS = 320


def page_layout(key):
    count_key, largest_key, layout_random_start = jax.random.split(jax.random.fold_in(key, 11), 3)
    shifts = jax.random.randint(count_key, (QUERY_SEQ_COUNT,), 1, 5).astype(jnp.int32)
    counts = jnp.maximum(jnp.right_shift(jnp.full((QUERY_SEQ_COUNT,), WPAGES, jnp.int32), shifts), 1)
    largest = jax.random.randint(largest_key, (), 0, QUERY_SEQ_COUNT)
    counts = jnp.where(jnp.arange(QUERY_SEQ_COUNT) == largest, WPAGES, counts).astype(jnp.int32)
    placed = counts + (counts < WPAGES).astype(jnp.int32)
    range_ends = jnp.cumsum(placed)
    starts = range_ends - placed
    slot_order = jnp.arange(SLOTS, dtype=jnp.int32)
    request_of = jnp.sum((slot_order[:, None] >= range_ends[None, :]).astype(jnp.int32), axis=1)
    in_use = slot_order < range_ends[-1]
    clipped = jnp.minimum(request_of, QUERY_SEQ_COUNT - 1)
    page_index = slot_order - starts[clipped]
    req_value = jnp.where(in_use, clipped, -1).astype(jnp.int32)
    page_value = jnp.where(in_use, page_index, 0).astype(jnp.int32)
    shuffle = jax.random.permutation(layout_random_start, SLOTS)
    slot_req = jnp.zeros((SLOTS,), jnp.int32).at[shuffle].set(req_value)
    slot_page = jnp.zeros((SLOTS,), jnp.int32).at[shuffle].set(page_value)
    return (counts, slot_req, slot_page)


def draw_page_count(key, part):
    return page_layout(key)[0]


def draw_slot_req(key, part):
    return page_layout(key)[1]


def draw_slot_page(key, part):
    return page_layout(key)[2]


def draw_page_decay(key, part):
    counts, slot_req, slot_page = page_layout(key)
    kind_key, slow_key, fast_key, layout_random_start, extent_random_start = jax.random.split(jax.random.fold_in(key, 23), 5)
    span_extent = WPAGES * PAGE
    fast_pick = jax.random.randint(kind_key, (QUERY_SEQ_COUNT, ATTENDER_COUNT), 0, 2) == 1
    slow_rate = jnp.exp(jax.random.uniform(slow_key, (QUERY_SEQ_COUNT, ATTENDER_COUNT), jnp.float32, math.log(0.05 / span_extent), math.log(2.0 / span_extent)))
    fast_rate = jax.random.uniform(fast_key, (QUERY_SEQ_COUNT, ATTENDER_COUNT), jnp.float32, 1.0 / 50.0, 1.0 / 30.0)
    forgetting_factors = jnp.where(fast_pick, fast_rate, slow_rate)
    spurt_location = jax.random.randint(layout_random_start, (QUERY_SEQ_COUNT, ATTENDER_COUNT, 3), 0, span_extent)
    spurt_extent = jax.random.uniform(extent_random_start, (QUERY_SEQ_COUNT, ATTENDER_COUNT, 3), jnp.float32, 0.22, 0.69)
    guarded_query_index = jnp.maximum(slot_req, 0)
    symbol_separation = (counts[guarded_query_index] - 1 - slot_page)[:, None] * PAGE + (PAGE - 1 - jnp.arange(PAGE))[None, :]
    symbol_separation = jnp.abs(symbol_separation)
    elapsed_symbols = (symbol_separation[:, None, :, None] > spurt_location[guarded_query_index][:, :, None, :]).astype(jnp.float32)
    spurt_clusters = jnp.sum(elapsed_symbols * spurt_extent[guarded_query_index][:, :, None, :], axis=-1)
    return forgetting_factors[guarded_query_index][:, :, None] * symbol_separation[:, None, :].astype(jnp.float32) + spurt_clusters


def touch_ends(values, stream_key, least, top_value):
    place = [jax.random.randint(jax.random.fold_in(stream_key, axis), (), 0, length) for axis, length in enumerate(values.shape)]
    main_axis = values.shape.index(max(values.shape))
    next_to = place[:main_axis] + [(place[main_axis] + 1) % values.shape[main_axis]] + place[main_axis + 1:]
    return values.at[tuple(place)].set(least).at[tuple(next_to)].set(top_value)


def levels(own_key, dims, cuts, low, high):
    def one(position, blocks):
        steps = jax.random.uniform(jax.random.fold_in(jax.random.fold_in(own_key, 6), position), (blocks,), jnp.float32, low / len(cuts), high / len(cuts))
        return jnp.repeat(jnp.exp(steps), dims[position] // blocks).reshape((-1,) + (1,) * (len(dims) - position - 1))

    level = one(*cuts[0])
    for cut in cuts[1:]:
        level = level * one(*cut)
    return level


def noise(key, shape, width, bound, cuts=(), held_as=jnp.bfloat16):
    level = levels(key, shape, cuts, -0.22, 0.18) if cuts else 1.0
    array = jax.random.normal(key, shape, jnp.float32) * width * level
    return jnp.minimum(jnp.maximum(array, -bound), bound).astype(held_as)


def setup_inputs(seed: int = 0) -> dict:
    seeds = jax.random.split(jax.random.key(seed), 27)
    return {
        "drafts": noise(seeds[0], (QUERY_SEQ_COUNT, DRAFT, D), 1.0, 6.0, ((0, 32),)),
        "x_weight": noise(seeds[1], (D, E), D ** -0.5, 0.125, ((0, 32), (1, 16))),
        "z_weight": noise(seeds[2], (D, E), D ** -0.5, 0.125, ((0, 32), (1, 16))),
        "bc_weight": noise(seeds[3], (D, 2 * NS), D ** -0.5, 0.125, ((0, 32),)),
        "dt_weight": noise(seeds[4], (D, ATTENDER_COUNT), D ** -0.5, 0.125, ((0, 32), (1, 16))),
        "dt_bias": jnp.clip(-3.0 + 3.0 * jax.random.uniform(seeds[5], (ATTENDER_COUNT,), jnp.float32) ** levels(seeds[5], (ATTENDER_COUNT,), ((0, 16),), -0.2, 0.2), -3.0, 0.0),
        "decay_rate": jnp.clip(jnp.exp(math.log(0.5) - 3.912023 * jax.random.uniform(seeds[6], (ATTENDER_COUNT,), jnp.float32) ** levels(seeds[6], (ATTENDER_COUNT,), ((0, 16),), -0.2, 0.2)), 0.01, 0.5),
        "conv_x_weight": noise(seeds[7], (KC, E), 0.5, 3.0, ((1, 16),)),
        "conv_x_bias": noise(seeds[8], (E,), 0.3, 2.0, ((0, 16),)),
        "conv_bc_weight": noise(seeds[9], (KC, 2 * NS), 0.5, 3.0),
        "conv_bc_bias": noise(seeds[10], (2 * NS,), 0.3, 2.0),
        "norm_gain": jnp.clip(1.0 + 0.1 * jax.random.normal(seeds[11], (E,), jnp.float32), 0.5, 1.5).astype(jnp.bfloat16),
        "out_weight": noise(seeds[12], (E, D), E ** -0.5, 0.078125, ((0, 16), (1, 32))),
        "conv_x_state": noise(seeds[13], (QUERY_SEQ_COUNT, KC - 1, E), 1.0, 6.0, ((0, 32), (2, 16))),
        "conv_bc_state": noise(seeds[14], (QUERY_SEQ_COUNT, KC - 1, 2 * NS), 1.0, 6.0, ((0, 32),)),
        "ssm_state": noise(seeds[15], (QUERY_SEQ_COUNT, ATTENDER_COUNT, HD, NS), 1.0, 6.0, ((0, 32), (1, 16)), jnp.float32),
        "sink_x": noise(seeds[16], (QUERY_SEQ_COUNT, SINKS, E), 2.0, 12.0, ((0, 32), (2, 16))),
        "sink_b": noise(seeds[17], (QUERY_SEQ_COUNT, SINKS, NS), 1.0, 6.0, ((0, 32),)),
        "page_x": noise(seeds[18], (SLOTS, PAGE, E), 0.5, 3.0, ((0, 32), (2, 16))),
        "page_b": noise(seeds[19], (SLOTS, PAGE, NS), 1.0, 6.0, ((0, 32),)),
        "page_decay": draw_page_decay(jax.random.fold_in(seeds[26], 71), 0),
        "slot_req": draw_slot_req(jax.random.fold_in(seeds[26], 71), 0),
        "slot_page": draw_slot_page(jax.random.fold_in(seeds[26], 71), 0),
        "page_count": draw_page_count(jax.random.fold_in(seeds[26], 71), 0),
        "accepted": touch_ends(jax.random.randint(seeds[24], (QUERY_SEQ_COUNT,), 1, DRAFT + 1), jax.random.fold_in(seeds[24], 1), 1, DRAFT).astype(jnp.int32),
        "owner_row": jax.random.permutation(seeds[25], QUERY_SEQ_COUNT).astype(jnp.int32),
    }


EPSILON = 1e-05

def conv_silu(history, fresh, kernel, offset):
    joined = jnp.concatenate([history, fresh], axis=1).astype(jnp.float32)
    length = fresh.shape[1]
    summed = offset.astype(jnp.float32) + jnp.zeros(fresh.shape, jnp.float32)
    for kernel_tap in range(KC):
        summed = summed + kernel[kernel_tap].astype(jnp.float32) * joined[:, kernel_tap:kernel_tap + length]
    return jax.nn.silu(summed).astype(jnp.bfloat16)

def rounded(values):
    return lax.optimization_barrier(values.astype(jnp.bfloat16)).astype(jnp.float32)

def reference(drafts, x_weight, z_weight, bc_weight, dt_weight, dt_bias, decay_rate, conv_x_weight, conv_x_bias, conv_bc_weight, conv_bc_bias, norm_gain, out_weight, conv_x_state, conv_bc_state, ssm_state, sink_x, sink_b, page_x, page_b, page_decay, slot_req, slot_page, page_count, accepted, owner_row):
    flat_tokens = drafts.reshape(QUERY_SEQ_COUNT * DRAFT, D)
    x_raw = jnp.dot(flat_tokens, x_weight, preferred_element_type=jnp.float32).astype(jnp.bfloat16).reshape(QUERY_SEQ_COUNT, DRAFT, E)
    z_raw = jnp.dot(flat_tokens, z_weight, preferred_element_type=jnp.float32).astype(jnp.bfloat16).reshape(QUERY_SEQ_COUNT, DRAFT, E)
    bc_raw = jnp.dot(flat_tokens, bc_weight, preferred_element_type=jnp.float32).astype(jnp.bfloat16).reshape(QUERY_SEQ_COUNT, DRAFT, 2 * NS)
    dt_raw = jnp.dot(flat_tokens, dt_weight, preferred_element_type=jnp.float32).reshape(QUERY_SEQ_COUNT, DRAFT, ATTENDER_COUNT)
    x_act = conv_silu(conv_x_state, x_raw, conv_x_weight, conv_x_bias)
    bc_act = conv_silu(conv_bc_state, bc_raw, conv_bc_weight, conv_bc_bias)
    b_mat = bc_act[:, :, :NS]
    c_mat = bc_act[:, :, NS:]
    dtime = jax.nn.softplus(dt_raw + dt_bias)
    cumul = jnp.cumsum(-decay_rate * dtime, axis=1)
    guarded_query_index = jnp.maximum(slot_req, 0)
    slot_live = (slot_req >= 0) & (slot_page < page_count[guarded_query_index])
    slot_rows = owner_row[guarded_query_index].astype(jnp.int32)

    def visit(carry, items):
        row_id, alive, values, keys_b, decay_k = items
        scores = jnp.dot(c_mat[row_id], keys_b.T, preferred_element_type=jnp.float32)
        weights = scores[None] * jnp.exp(cumul[row_id].T[:, :, None] - decay_k[:, None, :])
        term = jnp.einsum('htp,phd->thd', rounded(weights), values.reshape(PAGE, ATTENDER_COUNT, HD).astype(jnp.float32))
        term = jnp.where(alive, term, 0.0).reshape(DRAFT, E)
        return (carry.at[row_id].add(term), None)
    page_sum = lax.scan(visit, jnp.zeros((QUERY_SEQ_COUNT, DRAFT, E), jnp.float32), (slot_rows, slot_live, page_x, page_b, page_decay))[0]
    inner = jnp.einsum('rtn,run->rtu', c_mat.astype(jnp.float32), b_mat.astype(jnp.float32))
    later = jnp.arange(DRAFT)[:, None] >= jnp.arange(DRAFT)[None, :]
    spread = jnp.where(later[None, :, :, None], cumul[:, :, None, :] - cumul[:, None, :, :], 0.0)
    draft_weight = jnp.where(later[None, :, :, None], inner[..., None] * jnp.exp(spread) * dtime[:, None, :, :], 0.0)
    head_values = x_act.reshape(QUERY_SEQ_COUNT, DRAFT, ATTENDER_COUNT, HD).astype(jnp.float32)
    own_terms = jnp.einsum('rtuh,ruhp->rthp', rounded(draft_weight), head_values).reshape(QUERY_SEQ_COUNT, DRAFT, E)
    sink_weight = jnp.einsum('rtn,rsn->rts', c_mat.astype(jnp.float32), sink_b.astype(jnp.float32))
    sink_terms = jnp.einsum('rts,rse->rte', rounded(sink_weight), sink_x.astype(jnp.float32))
    mixer_out = page_sum + own_terms + sink_terms
    gated = mixer_out * jax.nn.silu(z_raw.astype(jnp.float32))
    square_mean = lax.optimization_barrier(jnp.sum(gated * gated, axis=-1)) / E
    normed = (gated * lax.rsqrt(square_mean + EPSILON)[..., None] * norm_gain.astype(jnp.float32)).astype(jnp.bfloat16)
    mixed = jnp.dot(normed.reshape(QUERY_SEQ_COUNT * DRAFT, E), out_weight, preferred_element_type=jnp.float32).astype(jnp.bfloat16).reshape(QUERY_SEQ_COUNT, DRAFT, D)
    positions = jnp.arange(DRAFT)
    chosen = positions[None, :] == accepted[:, None] - 1
    cumul_last = lax.optimization_barrier(jnp.sum(jnp.where(chosen[:, :, None], cumul, 0.0), axis=1))
    kept = positions[None, :] < accepted[:, None]
    state_spread = jnp.where(kept[:, :, None], cumul_last[:, None, :] - cumul, 0.0)
    coeff = jnp.where(kept[:, :, None], jnp.exp(state_spread) * dtime, 0.0)
    fresh_state = jnp.einsum('ruh,ruhp,run->rhpn', coeff, head_values, b_mat.astype(jnp.float32), precision=lax.Precision.HIGHEST)
    new_state = jnp.exp(cumul_last)[:, :, None, None] * ssm_state + fresh_state

    def tail_rows(history, fresh_rows):
        joined = jnp.concatenate([history, fresh_rows], axis=1)
        return jax.vmap(lambda seq_rows, first_pos: lax.dynamic_slice_in_dim(seq_rows, first_pos, KC - 1, 0))(joined, accepted.astype(jnp.int32))
    new_conv_x = tail_rows(conv_x_state, x_raw)
    new_conv_bc = tail_rows(conv_bc_state, bc_raw)
    return (mixed, new_state, new_conv_x, new_conv_bc)
```

```python
import functools

import jax
import jax.numpy as jnp
from jax import lax
from jax.experimental import pallas as pl
from jax.experimental.pallas import tpu as pltpu
from jax.sharding import PartitionSpec as P

MESH = pl.DeviceIdType.MESH
T = 16
KC = 4
HD = 64
LN = 128
EPSILON = 1e-05
f32 = jnp.float32
bf16 = jnp.bfloat16
EXACT = lax.Precision.HIGHEST


def nt(a, b, precision=None):
    return lax.dot_general(
        a, b, (((1,), (1,)), ((), ())), preferred_element_type=f32, precision=precision
    )


def iota(shape, axis):
    return lax.broadcasted_iota(jnp.int32, shape, axis)


def silu(v):
    return v * jax.nn.sigmoid(v)


def pieces3(v):
    hi = v.astype(bf16).astype(f32)
    rest = v - hi
    mid = rest.astype(bf16).astype(f32)
    low = (rest - mid).astype(bf16).astype(f32)
    return hi, mid, low


def kernel(
    R,
    F,
    drafts_ref,
    xw_ref,
    zw_ref,
    bcw_ref,
    dtw_ref,
    dt_bias_ref,
    decay_ref,
    cxw_ref,
    cxb_ref,
    cbw_ref,
    cbb_ref,
    gain_ref,
    ow_ref,
    cxs_ref,
    cbs_ref,
    ssm_ref,
    sink_x_ref,
    sink_b_ref,
    page_x_ref,
    page_b_ref,
    page_decay_ref,
    slot_req_ref,
    slot_page_ref,
    page_count_ref,
    accepted_ref,
    owner_row_ref,
    mixed_ref,
    state_ref,
    ncx_ref,
    ncb_ref,
    a_buf,
    w_own,
    w_all,
    d_all,
    wxz,
    xz_send,
    xz_recv,
    z_own,
    z_all,
    head_buf,
    s_bc,
    cc_own,
    cc_all,
    q_buf,
    cum_buf,
    w5,
    terms,
    p_send,
    p_recv,
    s_x,
    xs_buf,
    bs_buf,
    g_own,
    g_all,
    w_ext,
    f_send,
    f_recv,
    send_sem,
    recv_sem,
):
    me = lax.axis_index("req")
    mf = lax.axis_index("fsdp")
    ks, inner = xw_ref.shape
    half = ks // 2
    heads = dtw_ref.shape[1]
    ns = bcw_ref.shape[1] // 2
    slots = page_x_ref.shape[0]
    page = page_x_ref.shape[1]
    total_inner = inner * F
    ocols = ow_ref.shape[1]
    pad_in = p_send.shape[1]
    mine = lax.div(me, 2)
    is_self = mine == mf

    barrier = pltpu.get_barrier_semaphore()

    @pl.loop(1, R)
    def _(i):
        pl.semaphore_signal(
            barrier, inc=1, device_id={"req": lax.rem(me + i, R)}, device_id_type=MESH
        )

    @pl.loop(1, F)
    def _(i):
        pl.semaphore_signal(
            barrier, inc=1, device_id={"fsdp": lax.rem(mf + i, F)}, device_id_type=MESH
        )

    @pl.loop(0, F)
    def _(i):
        g = lax.rem(mf + i, F)

        @pl.when(jnp.logical_or(g != mf, 2 * mf != me))
        def _():
            pl.semaphore_signal(
                barrier, inc=1, device_id={"req": 2 * mf, "fsdp": g}, device_id_type=MESH
            )

        @pl.when(jnp.logical_or(g != mf, 2 * mf + 1 != me))
        def _():
            pl.semaphore_signal(
                barrier, inc=1, device_id={"req": 2 * mf + 1, "fsdp": g}, device_id_type=MESH
            )

    wpad = jnp.concatenate([bcw_ref[...], jnp.zeros((LN - ks, 2 * ns), bf16)], axis=0)
    pick = (iota((T, 2 * ns), 1) == T * mf + iota((T, 2 * ns), 0)).astype(bf16)
    bc_rows = nt(pick, wpad)
    dpad = jnp.concatenate([dtw_ref[...], jnp.zeros((LN - ks, heads), bf16)], axis=0)
    row5 = iota((T, heads), 0)
    col5 = iota((T, heads), 1)
    pick5 = ((row5 == col5) | (row5 == col5 + heads)).astype(bf16)
    dt_rows = nt(pick5, dpad)
    row = iota((T, LN), 0)
    lane = iota((T, LN), 1)
    dt_rows = jnp.where(
        row < heads, pltpu.roll(dt_rows, ks, 1), pltpu.roll(dt_rows, half, 1)
    )
    dt_zone = (lane >= ks) & (lane < ks + half)
    w_own[...] = jnp.where(
        lane < ks, bc_rows, jnp.where(dt_zone & (row < 2 * heads), dt_rows, 0.0)
    ).astype(bf16)
    w_all[:, pl.ds(pl.multiple_of(me * LN, LN), LN)] = w_own[...]

    a_buf[pl.ds(48, LN - 48), :] = jnp.zeros((LN - 48, R * LN), bf16)
    for j in range(R):
        start = ks * j
        base = start // LN * LN
        off = start - base
        if off + ks <= LN:
            window = drafts_ref[0, :, pl.ds(base, LN)].astype(f32)
            if off:
                window = pltpu.roll(window, LN - off, 1)
        else:
            window = drafts_ref[0, :, pl.ds(base, 2 * LN)].astype(f32)
            window = pltpu.roll(window, 2 * LN - off, 1)[:, :LN]
        a_buf[pl.ds(0, T), pl.ds(LN * j, LN)] = jnp.where(lane < ks, window, 0.0).astype(bf16)
        a_buf[pl.ds(T, T), pl.ds(LN * j, LN)] = jnp.where(
            dt_zone, pltpu.roll(window, ks, 1), 0.0
        ).astype(bf16)
        a_buf[pl.ds(2 * T, T), pl.ds(LN * j, LN)] = jnp.where(
            dt_zone, pltpu.roll(window, half, 1), 0.0
        ).astype(bf16)
    own_rows = pl.ds(pl.multiple_of(me * T, T), T)
    d_all[own_rows, :] = a_buf[pl.ds(0, T), pl.ds(pl.multiple_of(me * LN, LN), LN)]

    pl.semaphore_wait(barrier, (R - 1) + (F - 1) + R - is_self.astype(jnp.int32))

    def put(src, dst, phase, device):
        pltpu.make_async_remote_copy(
            src_ref=src,
            dst_ref=dst,
            send_sem=send_sem.at[phase],
            recv_sem=recv_sem.at[phase],
            device_id=device,
            device_id_type=MESH,
        ).start()

    def wait_bytes(ref, sem):
        pltpu.make_async_copy(ref, ref, sem).wait()

    own_lanes = pl.ds(pl.multiple_of(me * LN, LN), LN)

    @pl.loop(1, R)
    def _(i):
        put(w_own, w_all.at[:, own_lanes], 0, {"req": lax.rem(me + i, R)})

    @pl.loop(1, R)
    def _(i):
        r = lax.rem(me + i, R)
        put(
            a_buf.at[pl.ds(0, T), pl.ds(pl.multiple_of(r * LN, LN), LN)],
            d_all.at[own_rows, :],
            1,
            {"req": r},
        )

    wxz[pl.ds(0, ks), pl.ds(0, inner)] = xw_ref[...]
    wxz[pl.ds(0, ks), pl.ds(inner, inner)] = zw_ref[...]
    wxz[pl.ds(ks, LN - ks), :] = jnp.zeros((LN - ks, 2 * inner), bf16)
    head_buf[...] = jnp.zeros(head_buf.shape, f32)
    head_buf[pl.ds(0, 1), pl.ds(0, heads)] = dt_bias_ref[...]
    head_buf[pl.ds(1, 1), pl.ds(0, heads)] = decay_ref[...]
    s_bc[...] = jnp.zeros(s_bc.shape, f32)
    s_bc[pl.ds(T - KC + 1, KC - 1), :] = cbs_ref[0].astype(f32)
    s_x[...] = jnp.zeros(s_x.shape, f32)
    s_x[pl.ds(T - KC + 1, KC - 1), :] = cxs_ref[0].astype(f32)
    bs_buf[...] = jnp.zeros(bs_buf.shape, f32)
    bs_buf[pl.ds(T, 4), :] = sink_b_ref[0].astype(f32)
    xs_buf[...] = jnp.zeros(xs_buf.shape, f32)
    xs_buf[pl.ds(T, 4), :] = sink_x_ref[0].astype(f32)
    w_ext[...] = jnp.zeros(w_ext.shape, bf16)
    w_ext[pl.ds(0, inner), pl.ds(0, ocols)] = ow_ref[...]
    tail = pad_in - inner
    er = iota((tail, LN), 0)
    el = iota((tail, LN), 1)
    w_ext[pl.ds(inner, tail), :] = jnp.where(
        (el >= ocols) & (el < ocols + 3) & (el - ocols == er), 1.0, w_ext[pl.ds(inner, tail), :].astype(f32)
    ).astype(bf16)

    rows_of = []
    live_of = []
    for s in range(slots):
        req = slot_req_ref[s]
        guarded = jnp.maximum(req, 0)
        live_of.append((req >= 0) & (slot_page_ref[s] < page_count_ref[guarded]))
        rows_of.append(owner_row_ref[guarded])
    by_sub = jnp.zeros((slots * T, 1), jnp.int32)
    by_lane = jnp.zeros((1, slots * T), jnp.int32)
    live_sub = jnp.zeros((slots * T, 1), jnp.int32)
    for s in range(slots):
        in_sub = lax.div(iota((slots * T, 1), 0), T) == s
        in_lane = lax.div(iota((1, slots * T), 1), T) == s
        by_sub = jnp.where(in_sub, T * (rows_of[s] - s), by_sub)
        live_sub = jnp.where(in_sub, live_of[s].astype(jnp.int32), live_sub)
        by_lane = jnp.where(
            in_lane, jnp.where(live_of[s], T * (rows_of[s] - s), -(1 << 20)), by_lane
        )
    gather_rows = (
        iota((slots * T, R * T), 1) == iota((slots * T, R * T), 0) + by_sub
    ).astype(bf16)
    scatter_rows = (
        iota((R * T, slots * T), 0) == iota((R * T, slots * T), 1) + by_lane
    ).astype(bf16)

    wait_bytes(w_all.at[:, pl.ds(0, (R - 1) * LN)], recv_sem.at[0])
    proj = nt(a_buf[...], w_all[...])
    z_own[...] = nt((iota((T, T), 0) == iota((T, T), 1)).astype(bf16), proj.astype(bf16)).astype(bf16)
    z_rows = pl.ds(pl.multiple_of(mf * T, T), T)
    z_all[z_rows, :] = z_own[...]

    @pl.loop(1, F)
    def _(i):
        put(z_own, z_all.at[z_rows, :], 2, {"fsdp": lax.rem(mf + i, F)})

    er = iota((T, LN), 0)
    el = iota((T, LN), 1)
    first = ((er == el) & (el < heads)).astype(f32)
    second = ((er == el + heads) & (el < heads)).astype(f32)
    dt_raw = jnp.dot(proj[T : 2 * T], first, precision=EXACT, preferred_element_type=f32) + jnp.dot(
        proj[2 * T : 3 * T], second, precision=EXACT, preferred_element_type=f32
    )
    v = dt_raw + head_buf[pl.ds(0, 1), :]
    dtime = jnp.maximum(v, 0.0) + jnp.log1p(jnp.exp(-jnp.abs(v)))
    upto = (iota((T, T), 1) <= iota((T, T), 0)).astype(f32)
    cumul = -jnp.dot(
        upto, dtime * head_buf[pl.ds(1, 1), :], precision=EXACT, preferred_element_type=f32
    )
    hi, mid, low = pieces3(cumul)
    packed = hi + pltpu.roll(mid, 16, 1) + pltpu.roll(low, 32, 1)

    wait_bytes(z_all.at[pl.ds(0, (F - 1) * T), :], recv_sem.at[2])
    bc_raw = nt((iota((T, LN), 0) == iota((T, LN), 1)).astype(bf16), z_all[...])
    s_bc[pl.ds(T, T), :] = bc_raw
    acc = jnp.zeros((T, 2 * ns), f32) + cbb_ref[...].astype(f32)
    for k in range(KC):
        acc = acc + cbw_ref[pl.ds(k, 1), :].astype(f32) * s_bc[pl.ds(T - KC + 1 + k, T), :]
    bc_act = silu(acc)
    b_mat = bc_act[:, :ns].astype(bf16)
    c_mat = bc_act[:, ns:].astype(bf16)
    cc_own[:, pl.ds(0, ns)] = c_mat
    cc_own[:, pl.ds(ns, LN)] = packed.astype(bf16)
    cc_all[own_rows, :] = cc_own[...]

    @pl.loop(1, R)
    def _(i):
        put(cc_own, cc_all.at[own_rows, :], 3, {"req": lax.rem(me + i, R)})

    wait_bytes(d_all.at[pl.ds(0, (R - 1) * T), :], recv_sem.at[1])
    xz_send[...] = jnp.dot(d_all[...], wxz[...], preferred_element_type=f32).astype(bf16)
    xz_recv[me] = xz_send[own_rows, :]

    @pl.loop(1, R)
    def _(i):
        r = lax.rem(me + i, R)
        put(
            xz_send.at[pl.ds(pl.multiple_of(r * T, T), T), :], xz_recv.at[me], 4, {"req": r}
        )

    head_lane = lax.div(iota((T, inner), 1), HD)

    def own_heads(stacked):
        out = jnp.where(head_lane == 0, stacked[0:T], 0.0)
        for h in range(1, heads):
            out = jnp.where(head_lane == h, stacked[h * T : (h + 1) * T], out)
        return out

    wait_bytes(cc_all.at[pl.ds(0, (R - 1) * T), :], recv_sem.at[3])
    picked = jnp.dot(gather_rows, cc_all[...], preferred_element_type=f32)
    q_buf[...] = picked[:, :ns].astype(bf16)
    cum3 = picked[:, ns:]
    cum_buf[...] = cum3 + pltpu.roll(cum3, LN - 16, 1) + pltpu.roll(cum3, LN - 32, 1)

    @pl.loop(0, slots)
    def _(s):
        rows = pl.ds(pl.multiple_of(s * T, T), T)
        scores = nt(q_buf[rows, :], page_b_ref[s])
        cum = cum_buf[rows, :]
        decays = page_decay_ref[s]
        for h in range(heads):
            factor = jnp.exp(cum[:, h : h + 1] - decays[h : h + 1, :])
            w5[pl.ds(h * T, T), :] = (scores * factor).astype(bf16)
        stacked = jnp.dot(w5[...], page_x_ref[s], preferred_element_type=f32)
        terms[rows, :] = own_heads(stacked)

    kept_terms = jnp.where(live_sub != 0, terms[...], 0.0).astype(bf16)
    summed = jnp.dot(scatter_rows, kept_terms, preferred_element_type=f32)
    p_send[:, pl.ds(0, inner)] = summed.astype(bf16)
    p_send[:, pl.ds(inner, tail)] = jnp.zeros((R * T, tail), bf16)
    p_recv[me] = p_send[own_rows, :]

    @pl.loop(1, R)
    def _(i):
        r = lax.rem(me + i, R)
        put(p_send.at[pl.ds(pl.multiple_of(r * T, T), T), :], p_recv.at[me], 5, {"req": r})

    wait_bytes(xz_recv.at[pl.ds(0, R - 1)], recv_sem.at[4])
    xz = lax.fori_loop(
        1, R, lambda i, total: total + xz_recv[i].astype(f32), xz_recv[0].astype(f32)
    )
    x_raw = xz[:, :inner].astype(bf16).astype(f32)
    z_raw = xz[:, inner:].astype(bf16).astype(f32)
    s_x[pl.ds(T, T), :] = x_raw
    acc = jnp.zeros((T, inner), f32) + cxb_ref[...].astype(f32)
    for k in range(KC):
        acc = acc + cxw_ref[pl.ds(k, 1), :].astype(f32) * s_x[pl.ds(T - KC + 1 + k, T), :]
    x_act = silu(acc).astype(bf16).astype(f32)
    xs_buf[pl.ds(0, T), :] = x_act
    bs_buf[pl.ds(0, T), :] = b_mat.astype(f32)
    scores = nt(c_mat, bs_buf[...].astype(bf16))
    zeros_t = jnp.zeros((T, LN), f32)
    eye8 = (iota((8, LN), 0) == iota((8, LN), 1)).astype(f32)
    cumul_t = nt(eye8, jnp.concatenate([cumul, zeros_t], axis=0), EXACT)
    dtime_t = nt(eye8, jnp.concatenate([dtime, zeros_t], axis=0), EXACT)
    at = iota((T, 2 * T), 0)
    au = iota((T, 2 * T), 1)
    for h in range(heads):
        spread = jnp.where(au <= at, cumul[:, h : h + 1] - cumul_t[h : h + 1, :], 0.0)
        factor = jnp.exp(spread) * dtime_t[h : h + 1, :]
        factor = jnp.where(au >= T, 1.0, jnp.where(au <= at, factor, 0.0))
        w5[pl.ds(h * T, T), pl.ds(0, 2 * T)] = (scores * factor).astype(bf16)
    local = own_heads(
        jnp.dot(
            w5[:, pl.ds(0, 2 * T)], xs_buf[...].astype(bf16), preferred_element_type=f32
        )
    )

    taken = accepted_ref[0]
    at = iota((T, LN), 0)
    last = jnp.sum(jnp.where(at == taken - 1, cumul, 0.0), axis=0, keepdims=True)
    spread = jnp.where(at < taken, last - cumul, 0.0)
    coeff = jnp.where(at < taken, jnp.exp(spread) * dtime, 0.0)
    coeff_x = jnp.zeros((T, inner), f32)
    for h in range(heads):
        coeff_x = jnp.where(head_lane == h, coeff[:, h : h + 1], coeff_x)
    y = coeff_x * x_act
    y_hi = y.astype(bf16).astype(f32)
    y2 = jnp.concatenate([y_hi, y - y_hi], axis=0).astype(bf16)
    b2 = jnp.concatenate([b_mat, b_mat], axis=0)
    fresh = lax.dot_general(
        y2, b2, (((0,), (0,)), ((), ())), preferred_element_type=f32
    )
    keep = jnp.exp(last)
    for h in range(heads):
        state_ref[0, h] = keep[:, h : h + 1] * ssm_ref[0, h] + fresh[h * HD : (h + 1) * HD]
    tail_pick = (
        iota((8, 2 * T), 1) == T - KC + 1 + taken + iota((8, 2 * T), 0)
    ).astype(bf16)
    ncx = jnp.dot(tail_pick, s_x[...].astype(bf16), preferred_element_type=f32)
    ncx_ref[0] = ncx[: KC - 1].astype(bf16)
    ncb = jnp.dot(tail_pick, s_bc[...].astype(bf16), preferred_element_type=f32)
    ncb_ref[0] = ncb[: KC - 1].astype(bf16)
    gate = silu(z_raw)

    wait_bytes(p_recv.at[pl.ds(0, R - 1)], recv_sem.at[5])
    page_sum = lax.fori_loop(
        1, R, lambda i, total: total + p_recv[i].astype(f32), p_recv[0].astype(f32)
    )[:, :inner]
    gated = (page_sum + local) * gate
    squares = jnp.sum(gated * gated, axis=1, keepdims=True)
    hi, mid, low = pieces3(squares)
    el = iota((T, tail), 1)
    g_own[:, pl.ds(0, inner)] = (gated * gain_ref[...].astype(f32)).astype(bf16)
    g_own[:, pl.ds(inner, tail)] = jnp.where(
        el == 0, hi, jnp.where(el == 1, mid, jnp.where(el == 2, low, 0.0))
    ).astype(bf16)
    g_all[own_rows, :] = g_own[...]

    @pl.loop(1, R)
    def _(i):
        put(g_own, g_all.at[own_rows, :], 6, {"req": lax.rem(me + i, R)})

    wait_bytes(g_all.at[pl.ds(0, (R - 1) * T), :], recv_sem.at[6])
    f_send[...] = jnp.dot(g_all[...], w_ext[...], preferred_element_type=f32).astype(bf16)
    slot = lax.rem(me, 2) * F + mf

    @pl.when(is_self)
    def _():
        f_recv[slot] = f_send[own_rows, :]

    @pl.when(jnp.logical_not(is_self))
    def _():
        put(f_send.at[own_rows, :], f_recv.at[slot], 7, {"req": me, "fsdp": mine})

    @pl.loop(1, R)
    def _(i):
        r = lax.rem(me + i, R)
        put(
            f_send.at[pl.ds(pl.multiple_of(r * T, T), T), :],
            f_recv.at[slot],
            7,
            {"req": r, "fsdp": mine},
        )

    @pl.when(is_self)
    def _():
        wait_bytes(f_recv.at[pl.ds(0, R - 1)], recv_sem.at[7])

    @pl.when(jnp.logical_not(is_self))
    def _():
        wait_bytes(f_recv, recv_sem.at[7])

    even = lax.fori_loop(
        1, F, lambda i, total: total + f_recv[i].astype(f32), f_recv[0].astype(f32)
    )
    odd = lax.fori_loop(
        1, F, lambda i, total: total + f_recv[F + i].astype(f32), f_recv[F].astype(f32)
    )
    total_squares = (
        even[:, ocols : ocols + 1]
        + even[:, ocols + 1 : ocols + 2]
        + even[:, ocols + 2 : ocols + 3]
    )
    scale = lax.rsqrt(total_squares / total_inner + EPSILON)
    moved = pltpu.roll(odd, ocols, 1)
    mixed_ref[0, :, pl.ds(0, LN)] = (jnp.where(lane < ocols, even, moved) * scale).astype(bf16)
    mixed_ref[0, :, pl.ds(LN, 2 * ocols - LN)] = (moved * scale)[:, : 2 * ocols - LN].astype(bf16)

    wait_bytes(w_all.at[:, pl.ds(0, (R - 1) * LN)], send_sem.at[0])
    wait_bytes(d_all.at[pl.ds(0, (R - 1) * T), :], send_sem.at[1])
    wait_bytes(z_all.at[pl.ds(0, (F - 1) * T), :], send_sem.at[2])
    wait_bytes(cc_all.at[pl.ds(0, (R - 1) * T), :], send_sem.at[3])
    wait_bytes(xz_recv.at[pl.ds(0, R - 1)], send_sem.at[4])
    wait_bytes(p_recv.at[pl.ds(0, R - 1)], send_sem.at[5])
    wait_bytes(g_all.at[pl.ds(0, (R - 1) * T), :], send_sem.at[6])

    @pl.when(is_self)
    def _():
        wait_bytes(f_recv.at[pl.ds(0, R - 1)], send_sem.at[7])

    @pl.when(jnp.logical_not(is_self))
    def _():
        wait_bytes(f_recv, send_sem.at[7])


def per_device(
    R,
    F,
    drafts,
    x_weight,
    z_weight,
    bc_weight,
    dt_weight,
    dt_bias,
    decay_rate,
    conv_x_weight,
    conv_x_bias,
    conv_bc_weight,
    conv_bc_bias,
    norm_gain,
    out_weight,
    conv_x_state,
    conv_bc_state,
    ssm_state,
    sink_x,
    sink_b,
    page_x,
    page_b,
    page_decay,
    slot_req,
    slot_page,
    page_count,
    accepted,
    owner_row,
):
    inner = x_weight.shape[1]
    ns = bc_weight.shape[1] // 2
    slots, page, _ = page_x.shape
    heads = dt_weight.shape[1]
    ocols = out_weight.shape[1]
    pad_in = -(-inner // LN) * LN
    vmem = pl.BlockSpec(memory_space=pltpu.VMEM)
    smem = pl.BlockSpec(memory_space=pltpu.SMEM)
    shape = jax.ShapeDtypeStruct
    scratch = [
        pltpu.VMEM((LN, R * LN), bf16),
        pltpu.VMEM((T, LN), bf16),
        pltpu.VMEM((T, R * LN), bf16),
        pltpu.VMEM((R * T, LN), bf16),
        pltpu.VMEM((LN, 2 * inner), bf16),
        pltpu.VMEM((R * T, 2 * inner), bf16),
        pltpu.VMEM((R, T, 2 * inner), bf16),
        pltpu.VMEM((T, LN), bf16),
        pltpu.VMEM((F * T, LN), bf16),
        pltpu.VMEM((8, LN), f32),
        pltpu.VMEM((2 * T, 2 * ns), f32),
        pltpu.VMEM((T, ns + LN), bf16),
        pltpu.VMEM((R * T, ns + LN), bf16),
        pltpu.VMEM((slots * T, ns), bf16),
        pltpu.VMEM((slots * T, LN), f32),
        pltpu.VMEM((heads * T, page), bf16),
        pltpu.VMEM((slots * T, inner), f32),
        pltpu.VMEM((R * T, pad_in), bf16),
        pltpu.VMEM((R, T, pad_in), bf16),
        pltpu.VMEM((2 * T, inner), f32),
        pltpu.VMEM((2 * T, inner), f32),
        pltpu.VMEM((2 * T, ns), f32),
        pltpu.VMEM((T, pad_in), bf16),
        pltpu.VMEM((R * T, pad_in), bf16),
        pltpu.VMEM((pad_in, LN), bf16),
        pltpu.VMEM((R * T, LN), bf16),
        pltpu.VMEM((2 * F, T, LN), bf16),
        pltpu.SemaphoreType.DMA((8,)),
        pltpu.SemaphoreType.DMA((8,)),
    ]
    return pl.pallas_call(
        functools.partial(kernel, R, F),
        out_shape=(
            shape((1, T, 2 * ocols), bf16),
            shape(ssm_state.shape, f32),
            shape(conv_x_state.shape, bf16),
            shape(conv_bc_state.shape, bf16),
        ),
        in_specs=[vmem] * 21 + [smem] * 5,
        out_specs=(vmem,) * 4,
        scratch_shapes=scratch,
        compiler_params=pltpu.CompilerParams(
            collective_id=0, has_side_effects=True, vmem_limit_bytes=48 << 20
        ),
        name="mixer",
    )(
        drafts,
        x_weight,
        z_weight,
        bc_weight,
        dt_weight,
        dt_bias.reshape(1, -1),
        decay_rate.reshape(1, -1),
        conv_x_weight,
        conv_x_bias.reshape(1, -1),
        conv_bc_weight,
        conv_bc_bias.reshape(1, -1),
        norm_gain.reshape(1, -1),
        out_weight,
        conv_x_state,
        conv_bc_state,
        ssm_state,
        sink_x,
        sink_b,
        page_x,
        page_b,
        page_decay,
        slot_req,
        slot_page,
        page_count,
        accepted,
        owner_row,
    )


def solution(mesh):
    in_specs = (
        P("req", None, None),
        P("req", "fsdp"),
        P("req", "fsdp"),
        P("req", None),
        P("req", "fsdp"),
        P("fsdp"),
        P("fsdp"),
        P(None, "fsdp"),
        P("fsdp"),
        P(),
        P(),
        P("fsdp"),
        P("fsdp", "req"),
        P("req", None, "fsdp"),
        P("req", None, None),
        P("req", "fsdp", None, None),
        P("req", None, "fsdp"),
        P("req", None, None),
        P("req", None, "fsdp"),
        P("req", None, None),
        P("req", "fsdp", None),
        P("req"),
        P("req"),
        P(),
        P("req"),
        P(),
    )
    out_specs = (
        P("req", None, "fsdp"),
        P("req", "fsdp", None, None),
        P("req", None, "fsdp"),
        P("req", None, None),
    )
    return jax.shard_map(
        functools.partial(per_device, mesh.shape["req"], mesh.shape["fsdp"]),
        mesh=mesh,
        in_specs=in_specs,
        out_specs=out_specs,
        check_vma=False,
    )
```

```python
import functools

import jax
import jax.numpy as jnp
from jax import lax
from jax.experimental import pallas as pl
from jax.experimental.pallas import tpu as pltpu
from jax.sharding import PartitionSpec as P

MESH = pl.DeviceIdType.MESH
T = 16
X = 4
KC = 4
HD = 64
LN = 128
EPSILON = 1e-05
f32 = jnp.float32
bf16 = jnp.bfloat16
EXACT = lax.Precision.HIGHEST


def nt(a, b, precision=None):
    return lax.dot_general(
        a, b, (((1,), (1,)), ((), ())), preferred_element_type=f32, precision=precision
    )


def iota(shape, axis):
    return lax.broadcasted_iota(jnp.int32, shape, axis)


def silu(v):
    return v * jax.nn.sigmoid(v)


def pieces3(v):
    hi = v.astype(bf16).astype(f32)
    rest = v - hi
    mid = rest.astype(bf16).astype(f32)
    low = (rest - mid).astype(bf16).astype(f32)
    return hi, mid, low


def kernel(
    R,
    F,
    drafts_ref,
    xw_ref,
    zw_ref,
    bcw_ref,
    dtw_ref,
    dt_bias_ref,
    decay_ref,
    cxw_ref,
    cxb_ref,
    cbw_ref,
    cbb_ref,
    gain_ref,
    ow_ref,
    cxs_ref,
    cbs_ref,
    ssm_ref,
    sink_x_ref,
    sink_b_ref,
    page_x_ref,
    page_b_ref,
    page_decay_ref,
    slot_req_ref,
    slot_page_ref,
    page_count_ref,
    accepted_ref,
    owner_row_ref,
    mixed_ref,
    state_ref,
    ncx_ref,
    ncb_ref,
    dt_buf,
    a_buf,
    w_own,
    w_all,
    d_all,
    wxz,
    xz_send,
    xz_recv,
    z_own,
    z_all,
    head_buf,
    s_bc,
    cc_own,
    cc_all,
    q_buf,
    cum_buf,
    w5,
    terms,
    p_send,
    p_recv,
    s_x,
    xs_buf,
    bs_buf,
    g_own,
    g_all,
    w_ext,
    f_send,
    f_recv,
    send_sem,
    recv_sem,
):
    me = lax.axis_index("req")
    mf = lax.axis_index("fsdp")
    ks, inner = xw_ref.shape
    half = ks // 2
    heads = dtw_ref.shape[0]
    ns = bcw_ref.shape[1] // 2
    slots = page_x_ref.shape[0]
    total_inner = inner * F
    ocols = ow_ref.shape[0]
    pad_in = g_own.shape[1]
    Y = R // X
    per_row = X // 2
    my = lax.div(me, X)
    mx = lax.rem(me, X)
    is_self = lax.div(mf, per_row) == my

    barrier = pltpu.get_barrier_semaphore()

    @pl.loop(1, R)
    def _(i):
        pl.semaphore_signal(
            barrier, inc=1, device_id={"req": lax.rem(me + i, R)}, device_id_type=MESH
        )

    @pl.loop(1, F)
    def _(i):
        pl.semaphore_signal(
            barrier, inc=1, device_id={"fsdp": lax.rem(mf + i, F)}, device_id_type=MESH
        )

    source = lax.div(mf, per_row) * X + mx

    @pl.loop(0, F)
    def _(i):
        g = lax.rem(mf + i, F)

        @pl.when(jnp.logical_or(g != mf, source != me))
        def _():
            pl.semaphore_signal(
                barrier, inc=1, device_id={"req": source, "fsdp": g}, device_id_type=MESH
            )

    wpad = jnp.concatenate([bcw_ref[...], jnp.zeros((LN - ks, 2 * ns), bf16)], axis=0)
    pick = (iota((T, 2 * ns), 1) == T * mf + iota((T, 2 * ns), 0)).astype(bf16)
    bc_rows = nt(pick, wpad)
    row = iota((T, LN), 0)
    lane = iota((T, LN), 1)
    dt_buf[...] = jnp.zeros(dt_buf.shape, f32)
    dt_buf[pl.ds(0, heads), pl.ds(0, ks)] = dtw_ref[...].astype(f32)
    dt_buf[pl.ds(heads, heads), pl.ds(0, ks)] = dtw_ref[...].astype(f32)
    dt_rows = dt_buf[...]
    dt_rows = jnp.where(
        row < heads, pltpu.roll(dt_rows, ks, 1), pltpu.roll(dt_rows, half, 1)
    )
    dt_zone = (lane >= ks) & (lane < ks + half)
    w_own[...] = jnp.where(
        lane < ks, bc_rows, jnp.where(dt_zone & (row < 2 * heads), dt_rows, 0.0)
    ).astype(bf16)
    w_all[:, pl.ds(pl.multiple_of(me * LN, LN), LN)] = w_own[...]

    own_rows = pl.ds(pl.multiple_of(me * T, T), T)
    y_rows = pl.ds(pl.multiple_of(my * T, T), T)
    pl.semaphore_wait(
        barrier, (R - 1) + (F - 1) + Y * per_row - is_self.astype(jnp.int32)
    )

    def put(src, dst, phase, device):
        pltpu.make_async_remote_copy(
            src_ref=src,
            dst_ref=dst,
            send_sem=send_sem.at[phase],
            recv_sem=recv_sem.at[phase],
            device_id=device,
            device_id_type=MESH,
        ).start()

    def wait_bytes(ref, sem):
        pltpu.make_async_copy(ref, ref, sem).wait()

    own_lanes = pl.ds(pl.multiple_of(me * LN, LN), LN)
    w_bytes = wxz.at[pl.ds(0, (X - 1) * ks), :]
    o_bytes = w_ext.at[pl.ds(0, (X - 1) * ocols), :]

    @pl.loop(1, R)
    def _(i):
        put(w_own, w_all.at[:, own_lanes], 0, {"req": lax.rem(me + i, R)})

    own_block = pl.ds(pl.multiple_of(mx * LN, LN), ks)
    own_outs = pl.ds(
        pl.multiple_of(lax.div(mx, 2) * 2 * LN + lax.rem(mx, 2) * ocols, 16), ocols
    )
    tail = pad_in - inner
    for i in range(X):
        wxz[pl.ds(LN * i + ks, LN - ks), :] = jnp.zeros((LN - ks, 2 * inner), bf16)
    wxz[own_block, pl.ds(0, inner)] = xw_ref[...]
    wxz[own_block, pl.ds(inner, inner)] = zw_ref[...]
    w_ext[own_outs, pl.ds(0, inner)] = ow_ref[...]
    w_ext[own_outs, pl.ds(inner, tail)] = jnp.zeros((ocols, tail), bf16)
    rest = 2 * LN - 2 * ocols
    er = iota((rest, tail), 0)
    el = iota((rest, tail), 1)
    for i in range(per_row):
        top = pl.ds(2 * LN * i + 2 * ocols, rest)
        w_ext[top, pl.ds(0, inner)] = jnp.zeros((rest, inner), bf16)
        w_ext[top, pl.ds(inner, tail)] = ((er == el) & (el < 3)).astype(bf16)

    @pl.loop(1, X)
    def _(i):
        r = my * X + lax.rem(mx + i, X)
        put(wxz.at[own_block, :], wxz.at[own_block, :], 8, {"req": r})

    a_buf[pl.ds(48, LN - 48), :] = jnp.zeros((LN - 48, R * LN), bf16)
    for j in range(R):
        start = ks * j
        base = start // LN * LN
        off = start - base
        if off + ks <= LN:
            window = drafts_ref[0, :, pl.ds(base, LN)].astype(f32)
            if off:
                window = pltpu.roll(window, LN - off, 1)
        else:
            window = drafts_ref[0, :, pl.ds(base, 2 * LN)].astype(f32)
            window = pltpu.roll(window, 2 * LN - off, 1)[:, :LN]
        a_buf[pl.ds(0, T), pl.ds(LN * j, LN)] = jnp.where(lane < ks, window, 0.0).astype(bf16)
        a_buf[pl.ds(T, T), pl.ds(LN * j, LN)] = jnp.where(
            dt_zone, pltpu.roll(window, ks, 1), 0.0
        ).astype(bf16)
        a_buf[pl.ds(2 * T, T), pl.ds(LN * j, LN)] = jnp.where(
            dt_zone, pltpu.roll(window, half, 1), 0.0
        ).astype(bf16)
    d_all[y_rows, :] = a_buf[pl.ds(0, T), pl.ds(pl.multiple_of(my * X * LN, X * LN), X * LN)]

    @pl.loop(1, Y)
    def _(i):
        yy = lax.rem(my + i, Y)
        put(
            a_buf.at[pl.ds(0, T), pl.ds(pl.multiple_of(yy * X * LN, X * LN), X * LN)],
            d_all.at[y_rows, :],
            1,
            {"req": yy * X + mx},
        )

    @pl.loop(1, X)
    def _(i):
        r = my * X + lax.rem(mx + i, X)
        put(w_ext.at[own_outs, :], w_ext.at[own_outs, :], 9, {"req": r})

    head_buf[...] = jnp.zeros(head_buf.shape, f32)
    head_buf[pl.ds(0, 1), pl.ds(0, heads)] = dt_bias_ref[...]
    head_buf[pl.ds(1, 1), pl.ds(0, heads)] = decay_ref[...]
    s_bc[...] = jnp.zeros(s_bc.shape, f32)
    s_bc[pl.ds(T - KC + 1, KC - 1), :] = cbs_ref[0].astype(f32)
    s_x[...] = jnp.zeros(s_x.shape, f32)
    s_x[pl.ds(T - KC + 1, KC - 1), :] = cxs_ref[0].astype(f32)
    bs_buf[...] = jnp.zeros(bs_buf.shape, f32)
    bs_buf[pl.ds(T, 4), :] = sink_b_ref[0].astype(f32)
    xs_buf[...] = jnp.zeros(xs_buf.shape, f32)
    xs_buf[pl.ds(T, 4), :] = sink_x_ref[0].astype(f32)
    rows_of = []
    live_of = []
    for s in range(slots):
        req = slot_req_ref[s]
        guarded = jnp.maximum(req, 0)
        live_of.append((req >= 0) & (slot_page_ref[s] < page_count_ref[guarded]))
        rows_of.append(owner_row_ref[guarded])
    by_sub = jnp.zeros((slots * T, 1), jnp.int32)
    by_lane = jnp.zeros((1, slots * T), jnp.int32)
    live_sub = jnp.zeros((slots * T, 1), jnp.int32)
    for s in range(slots):
        in_sub = lax.div(iota((slots * T, 1), 0), T) == s
        in_lane = lax.div(iota((1, slots * T), 1), T) == s
        by_sub = jnp.where(in_sub, T * (rows_of[s] - s), by_sub)
        live_sub = jnp.where(in_sub, live_of[s].astype(jnp.int32), live_sub)
        by_lane = jnp.where(
            in_lane, jnp.where(live_of[s], T * (rows_of[s] - s), -(1 << 20)), by_lane
        )
    gather_rows = (
        iota((slots * T, R * T), 1) == iota((slots * T, R * T), 0) + by_sub
    ).astype(bf16)
    scatter_rows = (
        iota((R * T, slots * T), 0) == iota((R * T, slots * T), 1) + by_lane
    ).astype(bf16)

    wait_bytes(w_all.at[:, pl.ds(0, (R - 1) * LN)], recv_sem.at[0])
    proj = nt(a_buf[...], w_all[...])
    z_own[...] = nt((iota((T, T), 0) == iota((T, T), 1)).astype(bf16), proj.astype(bf16)).astype(bf16)
    z_rows = pl.ds(pl.multiple_of(mf * T, T), T)
    z_all[z_rows, :] = z_own[...]

    @pl.loop(1, F)
    def _(i):
        put(z_own, z_all.at[z_rows, :], 2, {"fsdp": lax.rem(mf + i, F)})

    er = iota((T, LN), 0)
    el = iota((T, LN), 1)
    first = ((er == el) & (el < heads)).astype(f32)
    second = ((er == el + heads) & (el < heads)).astype(f32)
    dt_raw = jnp.dot(proj[T : 2 * T], first, precision=EXACT, preferred_element_type=f32) + jnp.dot(
        proj[2 * T : 3 * T], second, precision=EXACT, preferred_element_type=f32
    )
    v = dt_raw + head_buf[pl.ds(0, 1), :]
    dtime = jnp.maximum(v, 0.0) + jnp.log1p(jnp.exp(-jnp.abs(v)))
    upto = (iota((T, T), 1) <= iota((T, T), 0)).astype(f32)
    cumul = -jnp.dot(
        upto, dtime * head_buf[pl.ds(1, 1), :], precision=EXACT, preferred_element_type=f32
    )
    hi, mid, low = pieces3(cumul)
    packed = hi + pltpu.roll(mid, 16, 1) + pltpu.roll(low, 32, 1)

    wait_bytes(z_all.at[pl.ds(0, (F - 1) * T), :], recv_sem.at[2])
    bc_raw = nt((iota((T, LN), 0) == iota((T, LN), 1)).astype(bf16), z_all[...])
    s_bc[pl.ds(T, T), :] = bc_raw
    acc = jnp.zeros((T, 2 * ns), f32) + cbb_ref[...].astype(f32).reshape(1, 2 * ns)
    for k in range(KC):
        acc = acc + cbw_ref[pl.ds(k, 1), :].astype(f32) * s_bc[pl.ds(T - KC + 1 + k, T), :]
    bc_act = silu(acc)
    b_mat = bc_act[:, :ns].astype(bf16)
    c_mat = bc_act[:, ns:].astype(bf16)
    cc_own[:, pl.ds(0, ns)] = c_mat
    cc_own[:, pl.ds(ns, LN)] = packed.astype(bf16)
    cc_all[own_rows, :] = cc_own[...]

    @pl.loop(1, R)
    def _(i):
        put(cc_own, cc_all.at[own_rows, :], 3, {"req": lax.rem(me + i, R)})

    wait_bytes(d_all.at[pl.ds(0, (Y - 1) * T), :], recv_sem.at[1])
    wait_bytes(w_bytes, recv_sem.at[8])
    xz_send[...] = jnp.dot(d_all[...], wxz[...], preferred_element_type=f32).astype(bf16)
    xz_recv[my] = xz_send[y_rows, :]

    @pl.loop(1, Y)
    def _(i):
        yy = lax.rem(my + i, Y)
        put(
            xz_send.at[pl.ds(pl.multiple_of(yy * T, T), T), :],
            xz_recv.at[my],
            4,
            {"req": yy * X + mx},
        )

    head_lane = lax.div(iota((T, inner), 1), HD)

    def own_heads(stacked):
        out = jnp.where(head_lane == 0, stacked[0:T], 0.0)
        for h in range(1, heads):
            out = jnp.where(head_lane == h, stacked[h * T : (h + 1) * T], out)
        return out

    wait_bytes(cc_all.at[pl.ds(0, (R - 1) * T), :], recv_sem.at[3])
    picked = jnp.dot(gather_rows, cc_all[...], preferred_element_type=f32)
    q_buf[...] = picked[:, :ns].astype(bf16)
    cum3 = picked[:, ns:]
    cum_buf[...] = cum3 + pltpu.roll(cum3, LN - 16, 1) + pltpu.roll(cum3, LN - 32, 1)

    @pl.loop(0, slots)
    def _(s):
        rows = pl.ds(pl.multiple_of(s * T, T), T)
        scores = nt(q_buf[rows, :], page_b_ref[s])
        cum = cum_buf[rows, :]
        decays = page_decay_ref[s]
        for h in range(heads):
            factor = jnp.exp(cum[:, h : h + 1] - decays[h : h + 1, :])
            w5[pl.ds(h * T, T), :] = (scores * factor).astype(bf16)
        stacked = nt(w5[...], page_x_ref[s])
        terms[rows, :] = own_heads(stacked)

    kept_terms = jnp.where(live_sub != 0, terms[...], 0.0).astype(bf16)
    summed = jnp.dot(scatter_rows, kept_terms, preferred_element_type=f32)
    p_send[:, pl.ds(0, inner)] = summed.astype(bf16)
    p_send[:, pl.ds(inner, tail)] = jnp.zeros((R * T, tail), bf16)
    p_recv[me] = p_send[own_rows, :]

    @pl.loop(1, R)
    def _(i):
        r = lax.rem(me + i, R)
        put(p_send.at[pl.ds(pl.multiple_of(r * T, T), T), :], p_recv.at[me], 5, {"req": r})

    wait_bytes(xz_recv.at[pl.ds(0, Y - 1)], recv_sem.at[4])
    xz = lax.fori_loop(
        1, Y, lambda i, total: total + xz_recv[i].astype(f32), xz_recv[0].astype(f32)
    )
    x_raw = xz[:, :inner].astype(bf16).astype(f32)
    z_raw = xz[:, inner:].astype(bf16).astype(f32)
    s_x[pl.ds(T, T), :] = x_raw
    acc = jnp.zeros((T, inner), f32) + cxb_ref[...].astype(f32).reshape(1, inner)
    for k in range(KC):
        acc = acc + cxw_ref[pl.ds(k, 1), :].astype(f32) * s_x[pl.ds(T - KC + 1 + k, T), :]
    x_act = silu(acc).astype(bf16).astype(f32)
    xs_buf[pl.ds(0, T), :] = x_act
    bs_buf[pl.ds(0, T), :] = b_mat.astype(f32)
    scores = nt(c_mat, bs_buf[...].astype(bf16))
    zeros_t = jnp.zeros((T, LN), f32)
    eye8 = (iota((8, LN), 0) == iota((8, LN), 1)).astype(f32)
    cumul_t = nt(eye8, jnp.concatenate([cumul, zeros_t], axis=0), EXACT)
    dtime_t = nt(eye8, jnp.concatenate([dtime, zeros_t], axis=0), EXACT)
    at = iota((T, 2 * T), 0)
    au = iota((T, 2 * T), 1)
    for h in range(heads):
        spread = jnp.where(au <= at, cumul[:, h : h + 1] - cumul_t[h : h + 1, :], 0.0)
        factor = jnp.exp(spread) * dtime_t[h : h + 1, :]
        factor = jnp.where(au >= T, 1.0, jnp.where(au <= at, factor, 0.0))
        w5[pl.ds(h * T, T), pl.ds(0, 2 * T)] = (scores * factor).astype(bf16)
    local = own_heads(
        jnp.dot(
            w5[:, pl.ds(0, 2 * T)], xs_buf[...].astype(bf16), preferred_element_type=f32
        )
    )

    taken = accepted_ref[0]
    at = iota((T, LN), 0)
    last = jnp.sum(jnp.where(at == taken - 1, cumul, 0.0), axis=0, keepdims=True)
    spread = jnp.where(at < taken, last - cumul, 0.0)
    coeff = jnp.where(at < taken, jnp.exp(spread) * dtime, 0.0)
    coeff_x = jnp.zeros((T, inner), f32)
    for h in range(heads):
        coeff_x = jnp.where(head_lane == h, coeff[:, h : h + 1], coeff_x)
    y = coeff_x * x_act
    y_hi = y.astype(bf16).astype(f32)
    y2 = jnp.concatenate([y_hi, y - y_hi], axis=0).astype(bf16)
    b2 = jnp.concatenate([b_mat, b_mat], axis=0)
    fresh = lax.dot_general(
        y2, b2, (((0,), (0,)), ((), ())), preferred_element_type=f32
    )
    keep = jnp.exp(last)
    for h in range(heads):
        state_ref[0, h] = keep[:, h : h + 1] * ssm_ref[0, h] + fresh[h * HD : (h + 1) * HD]
    tail_pick = (
        iota((8, 2 * T), 1) == T - KC + 1 + taken + iota((8, 2 * T), 0)
    ).astype(bf16)
    ncx = jnp.dot(tail_pick, s_x[...].astype(bf16), preferred_element_type=f32)
    ncx_ref[0] = ncx[: KC - 1].astype(bf16)
    ncb = jnp.dot(tail_pick, s_bc[...].astype(bf16), preferred_element_type=f32)
    ncb_ref[0] = ncb[: KC - 1].astype(bf16)
    gate = silu(z_raw)

    wait_bytes(p_recv.at[pl.ds(0, R - 1)], recv_sem.at[5])
    page_sum = lax.fori_loop(
        1, R, lambda i, total: total + p_recv[i].astype(f32), p_recv[0].astype(f32)
    )[:, :inner]
    gated = (page_sum + local) * gate
    squares = jnp.sum(gated * gated, axis=1, keepdims=True)
    hi, mid, low = pieces3(squares)
    el = iota((T, tail), 1)
    g_own[:, pl.ds(0, inner)] = (gated * gain_ref[...].astype(f32).reshape(1, inner)).astype(bf16)
    g_own[:, pl.ds(inner, tail)] = jnp.where(
        el == 0, hi, jnp.where(el == 1, mid, jnp.where(el == 2, low, 0.0))
    ).astype(bf16)
    g_all[y_rows, :] = g_own[...]

    @pl.loop(1, Y)
    def _(i):
        put(g_own, g_all.at[y_rows, :], 6, {"req": lax.rem(my + i, Y) * X + mx})

    wait_bytes(o_bytes, recv_sem.at[9])
    wait_bytes(g_all.at[pl.ds(0, (Y - 1) * T), :], recv_sem.at[6])
    f_send[...] = nt(g_all[...], w_ext[...]).astype(bf16)

    for b in range(per_row):
        lanes = pl.ds(2 * LN * b, 2 * LN)
        target = per_row * my + b

        @pl.when(target == mf)
        def _():
            f_recv[mf] = f_send[y_rows, lanes]

        @pl.when(target != mf)
        def _():
            put(f_send.at[y_rows, lanes], f_recv.at[mf], 7, {"fsdp": target})

        @pl.loop(1, Y)
        def _(i):
            yy = lax.rem(my + i, Y)
            put(
                f_send.at[pl.ds(pl.multiple_of(yy * T, T), T), lanes],
                f_recv.at[mf],
                7,
                {"req": yy * X + mx, "fsdp": target},
            )

    @pl.when(is_self)
    def _():
        wait_bytes(f_recv.at[pl.ds(0, F - 1)], recv_sem.at[7])

    @pl.when(jnp.logical_not(is_self))
    def _():
        wait_bytes(f_recv, recv_sem.at[7])

    out = lax.fori_loop(
        1, F, lambda i, total: total + f_recv[i].astype(f32), f_recv[0].astype(f32)
    )
    wide = 2 * ocols
    total_squares = (
        out[:, wide : wide + 1] + out[:, wide + 1 : wide + 2] + out[:, wide + 2 : wide + 3]
    )
    scale = lax.rsqrt(total_squares / total_inner + EPSILON)
    mixed_ref[0] = (out * scale)[:, :wide].astype(bf16)

    wait_bytes(w_all.at[:, pl.ds(0, (R - 1) * LN)], send_sem.at[0])
    wait_bytes(d_all.at[pl.ds(0, (Y - 1) * T), :], send_sem.at[1])
    wait_bytes(z_all.at[pl.ds(0, (F - 1) * T), :], send_sem.at[2])
    wait_bytes(cc_all.at[pl.ds(0, (R - 1) * T), :], send_sem.at[3])
    wait_bytes(xz_recv.at[pl.ds(0, Y - 1)], send_sem.at[4])
    wait_bytes(w_bytes, send_sem.at[8])
    wait_bytes(o_bytes, send_sem.at[9])
    wait_bytes(p_recv.at[pl.ds(0, R - 1)], send_sem.at[5])
    wait_bytes(g_all.at[pl.ds(0, (Y - 1) * T), :], send_sem.at[6])

    @pl.when(is_self)
    def _():
        wait_bytes(f_recv.at[pl.ds(0, F - 1)], send_sem.at[7])

    @pl.when(jnp.logical_not(is_self))
    def _():
        wait_bytes(f_recv, send_sem.at[7])


def per_device(
    R,
    F,
    drafts,
    x_weight,
    z_weight,
    bc_weight,
    dt_weight,
    dt_bias,
    decay_rate,
    conv_x_weight,
    conv_x_bias,
    conv_bc_weight,
    conv_bc_bias,
    norm_gain,
    out_weight,
    conv_x_state,
    conv_bc_state,
    ssm_state,
    sink_x,
    sink_b,
    page_x,
    page_b,
    page_decay,
    slot_req,
    slot_page,
    page_count,
    accepted,
    owner_row,
):
    inner = x_weight.shape[1]
    ns = bc_weight.shape[1] // 2
    slots, page, _ = page_x.shape
    heads = dt_weight.shape[1]
    ocols = out_weight.shape[1]
    pad_in = -(-inner // LN) * LN
    Y = R // X
    vmem = pl.BlockSpec(memory_space=pltpu.VMEM)
    smem = pl.BlockSpec(memory_space=pltpu.SMEM)
    shape = jax.ShapeDtypeStruct
    scratch = [
        pltpu.VMEM((T, LN), f32),
        pltpu.VMEM((LN, R * LN), bf16),
        pltpu.VMEM((T, LN), bf16),
        pltpu.VMEM((T, R * LN), bf16),
        pltpu.VMEM((Y * T, X * LN), bf16),
        pltpu.VMEM((X * LN, 2 * inner), bf16),
        pltpu.VMEM((Y * T, 2 * inner), bf16),
        pltpu.VMEM((Y, T, 2 * inner), bf16),
        pltpu.VMEM((T, LN), bf16),
        pltpu.VMEM((F * T, LN), bf16),
        pltpu.VMEM((8, LN), f32),
        pltpu.VMEM((2 * T, 2 * ns), f32),
        pltpu.VMEM((T, ns + LN), bf16),
        pltpu.VMEM((R * T, ns + LN), bf16),
        pltpu.VMEM((slots * T, ns), bf16),
        pltpu.VMEM((slots * T, LN), f32),
        pltpu.VMEM((heads * T, page), bf16),
        pltpu.VMEM((slots * T, inner), f32),
        pltpu.VMEM((R * T, pad_in), bf16),
        pltpu.VMEM((R, T, pad_in), bf16),
        pltpu.VMEM((2 * T, inner), f32),
        pltpu.VMEM((2 * T, inner), f32),
        pltpu.VMEM((2 * T, ns), f32),
        pltpu.VMEM((T, pad_in), bf16),
        pltpu.VMEM((Y * T, pad_in), bf16),
        pltpu.VMEM((X * LN, pad_in), bf16),
        pltpu.VMEM((Y * T, X * LN), bf16),
        pltpu.VMEM((F, T, 2 * LN), bf16),
        pltpu.SemaphoreType.DMA((10,)),
        pltpu.SemaphoreType.DMA((10,)),
    ]
    return pl.pallas_call(
        functools.partial(kernel, R, F),
        out_shape=(
            shape((1, T, 2 * ocols), bf16),
            shape(ssm_state.shape, f32),
            shape(conv_x_state.shape, bf16),
            shape(conv_bc_state.shape, bf16),
        ),
        in_specs=[vmem] * 21 + [smem] * 5,
        out_specs=(vmem,) * 4,
        scratch_shapes=scratch,
        compiler_params=pltpu.CompilerParams(
            collective_id=0, has_side_effects=True, vmem_limit_bytes=48 << 20
        ),
        name="mixer",
    )(
        drafts,
        x_weight,
        z_weight,
        bc_weight,
        dt_weight.T,
        dt_bias.reshape(1, -1),
        decay_rate.reshape(1, -1),
        conv_x_weight,
        conv_x_bias,
        conv_bc_weight,
        conv_bc_bias,
        norm_gain,
        out_weight.T,
        conv_x_state,
        conv_bc_state,
        ssm_state,
        sink_x,
        sink_b,
        jnp.swapaxes(page_x, 1, 2),
        page_b,
        page_decay,
        slot_req,
        slot_page,
        page_count,
        accepted,
        owner_row,
    )


def solution(mesh):
    in_specs = (
        P("req", None, None),
        P("req", "fsdp"),
        P("req", "fsdp"),
        P("req", None),
        P("req", "fsdp"),
        P("fsdp"),
        P("fsdp"),
        P(None, "fsdp"),
        P("fsdp"),
        P(),
        P(),
        P("fsdp"),
        P("fsdp", "req"),
        P("req", None, "fsdp"),
        P("req", None, None),
        P("req", "fsdp", None, None),
        P("req", None, "fsdp"),
        P("req", None, None),
        P("req", None, "fsdp"),
        P("req", None, None),
        P("req", "fsdp", None),
        P("req"),
        P("req"),
        P(),
        P("req"),
        P(),
    )
    out_specs = (
        P("req", None, "fsdp"),
        P("req", "fsdp", None, None),
        P("req", None, "fsdp"),
        P("req", None, None),
    )
    return jax.shard_map(
        functools.partial(per_device, mesh.shape["req"], mesh.shape["fsdp"]),
        mesh=mesh,
        in_specs=in_specs,
        out_specs=out_specs,
        check_vma=False,
    )
```

```python
import functools

import jax
import jax.numpy as jnp
from jax import lax
from jax.experimental import pallas as pl
from jax.experimental.pallas import tpu as pltpu
from jax.sharding import PartitionSpec as P

MESH = pl.DeviceIdType.MESH
T = 16
CROWS = 24
X = 4
KC = 4
HD = 64
LN = 128
EPSILON = 1e-05
f32 = jnp.float32
bf16 = jnp.bfloat16
EXACT = lax.Precision.HIGHEST
NAMES = (
    "drafts",
    "xw",
    "zw",
    "bcw",
    "dtw",
    "dt_bias",
    "decay",
    "cxw",
    "cxb",
    "cbw",
    "cbb",
    "gain",
    "ow",
    "cxs",
    "cbs",
    "ssm",
    "sink_x",
    "sink_b",
    "page_x",
    "page_b",
    "page_decay",
    "slot_req",
    "slot_page",
    "page_count",
    "accepted",
    "owner_row",
)
SCALARS = ("slot_req", "slot_page", "page_count", "owner_row")
FIRST = ("bcw", "dtw")
SECOND = ("xw", "zw", "drafts", "ow", "page_decay", "page_x", "page_b")
OTHERS = tuple(n for n in NAMES if n not in FIRST + SECOND)


def nt(a, b, precision=None):
    return lax.dot_general(
        a, b, (((1,), (1,)), ((), ())), preferred_element_type=f32, precision=precision
    )


def iota(shape, axis):
    return lax.broadcasted_iota(jnp.int32, shape, axis)


def silu(v):
    return v * jax.nn.sigmoid(v)


def pieces3(v):
    hi = v.astype(bf16).astype(f32)
    rest = v - hi
    mid = rest.astype(bf16).astype(f32)
    low = (rest - mid).astype(bf16).astype(f32)
    return hi, mid, low


def kernel(R, F, *refs):
    sources, outs, held, rest = refs[:26], refs[26:30], refs[30:56], refs[56:-1]
    load_sem = refs[-1]
    copies = [
        pltpu.make_async_copy(source, target, load_sem.at[i])
        for i, (source, target) in enumerate(zip(sources, held))
    ]

    def load(*names):
        for name in names:
            copies[NAMES.index(name)].start()

    def arrive(*names):
        for name in names:
            copies[NAMES.index(name)].wait()

    body(R, F, load, arrive, *held, *outs, *rest)


def body(
    R,
    F,
    load,
    arrive,
    drafts_ref,
    xw_ref,
    zw_ref,
    bcw_ref,
    dtw_ref,
    dt_bias_ref,
    decay_ref,
    cxw_ref,
    cxb_ref,
    cbw_ref,
    cbb_ref,
    gain_ref,
    ow_ref,
    cxs_ref,
    cbs_ref,
    ssm_ref,
    sink_x_ref,
    sink_b_ref,
    page_x_ref,
    page_b_ref,
    page_decay_ref,
    slot_req_ref,
    slot_page_ref,
    page_count_ref,
    accepted_ref,
    owner_row_ref,
    mixed_ref,
    state_ref,
    ncx_ref,
    ncb_ref,
    dt_buf,
    a_buf,
    w_own,
    w_all,
    d_all,
    wxz,
    xz_send,
    xz_recv,
    z_own,
    z_all,
    head_buf,
    s_bc,
    cc_own,
    cc_all,
    state_buf,
    least_buf,
    q_buf,
    cum_buf,
    w5,
    terms,
    p_send,
    p_recv,
    s_x,
    xs_buf,
    bs_buf,
    g_own,
    g_all,
    w_ext,
    f_send,
    f_recv,
    send_sem,
    recv_sem,
):
    me = lax.axis_index("req")
    mf = lax.axis_index("fsdp")
    ks, inner = xw_ref.shape
    half = ks // 2
    heads = dtw_ref.shape[0]
    ns = bcw_ref.shape[1] // 2
    slots = page_x_ref.shape[0]
    total_inner = inner * F
    ocols = ow_ref.shape[0]
    pad_in = g_own.shape[1]
    Y = R // X
    per_row = X // 2
    my = lax.div(me, X)
    mx = lax.rem(me, X)
    is_self = lax.div(mf, per_row) == my

    load(*FIRST)
    barrier = pltpu.get_barrier_semaphore()

    @pl.loop(1, R)
    def _(i):
        pl.semaphore_signal(
            barrier, inc=1, device_id={"req": lax.rem(me + i, R)}, device_id_type=MESH
        )

    @pl.loop(1, F)
    def _(i):
        pl.semaphore_signal(
            barrier, inc=1, device_id={"fsdp": lax.rem(mf + i, F)}, device_id_type=MESH
        )

    source = lax.div(mf, per_row) * X + mx

    @pl.loop(0, F)
    def _(i):
        g = lax.rem(mf + i, F)

        @pl.when(jnp.logical_or(g != mf, source != me))
        def _():
            pl.semaphore_signal(
                barrier, inc=1, device_id={"req": source, "fsdp": g}, device_id_type=MESH
            )

    load(*SECOND)
    load(*OTHERS)
    arrive("bcw", "dtw")
    wpad = jnp.concatenate([bcw_ref[...], jnp.zeros((LN - ks, 2 * ns), bf16)], axis=0)
    pick = (iota((T, 2 * ns), 1) == T * mf + iota((T, 2 * ns), 0)).astype(bf16)
    bc_rows = nt(pick, wpad)
    row = iota((T, LN), 0)
    lane = iota((T, LN), 1)
    dt_buf[...] = jnp.zeros(dt_buf.shape, f32)
    dt_buf[pl.ds(0, heads), pl.ds(0, ks)] = dtw_ref[...].astype(f32)
    dt_buf[pl.ds(heads, heads), pl.ds(0, ks)] = dtw_ref[...].astype(f32)
    dt_rows = dt_buf[...]
    dt_rows = jnp.where(
        row < heads, pltpu.roll(dt_rows, ks, 1), pltpu.roll(dt_rows, half, 1)
    )
    dt_zone = (lane >= ks) & (lane < ks + half)
    w_own[...] = jnp.where(
        lane < ks, bc_rows, jnp.where(dt_zone & (row < 2 * heads), dt_rows, 0.0)
    ).astype(bf16)
    w_all[:, pl.ds(pl.multiple_of(me * LN, LN), LN)] = w_own[...]

    own_rows = pl.ds(pl.multiple_of(me * T, T), T)
    y_rows = pl.ds(pl.multiple_of(my * T, T), T)
    pl.semaphore_wait(
        barrier, (R - 1) + (F - 1) + Y * per_row - is_self.astype(jnp.int32)
    )

    def put(src, dst, phase, device):
        pltpu.make_async_remote_copy(
            src_ref=src,
            dst_ref=dst,
            send_sem=send_sem.at[phase],
            recv_sem=recv_sem.at[phase],
            device_id=device,
            device_id_type=MESH,
        ).start()

    def wait_bytes(ref, sem):
        pltpu.make_async_copy(ref, ref, sem).wait()

    own_lanes = pl.ds(pl.multiple_of(me * LN, LN), LN)
    w_bytes = wxz.at[pl.ds(0, (X - 1) * ks), :]
    o_bytes = w_ext.at[pl.ds(0, (X - 1) * ocols), :]

    @pl.loop(1, R)
    def _(i):
        put(w_own, w_all.at[:, own_lanes], 0, {"req": lax.rem(me + i, R)})

    own_block = pl.ds(pl.multiple_of(mx * LN, LN), ks)
    own_outs = pl.ds(
        pl.multiple_of(lax.div(mx, 2) * 2 * LN + lax.rem(mx, 2) * ocols, 16), ocols
    )
    tail = pad_in - inner
    for i in range(X):
        wxz[pl.ds(LN * i + ks, LN - ks), :] = jnp.zeros((LN - ks, 2 * inner), bf16)
    arrive("xw", "zw")
    wxz[own_block, pl.ds(0, inner)] = xw_ref[...]
    wxz[own_block, pl.ds(inner, inner)] = zw_ref[...]
    arrive("ow")
    w_ext[own_outs, pl.ds(0, inner)] = ow_ref[...]
    w_ext[own_outs, pl.ds(inner, tail)] = jnp.zeros((ocols, tail), bf16)
    rest = 2 * LN - 2 * ocols
    er = iota((rest, tail), 0)
    el = iota((rest, tail), 1)
    for i in range(per_row):
        top = pl.ds(2 * LN * i + 2 * ocols, rest)
        w_ext[top, pl.ds(0, inner)] = jnp.zeros((rest, inner), bf16)
        w_ext[top, pl.ds(inner, tail)] = ((er == el) & (el < 3)).astype(bf16)

    @pl.loop(1, X)
    def _(i):
        r = my * X + lax.rem(mx + i, X)
        put(wxz.at[own_block, :], wxz.at[own_block, :], 8, {"req": r})

    arrive("drafts")
    a_buf[pl.ds(48, LN - 48), :] = jnp.zeros((LN - 48, R * LN), bf16)
    for j in range(R):
        start = ks * j
        base = start // LN * LN
        off = start - base
        if off + ks <= LN:
            window = drafts_ref[0, :, pl.ds(base, LN)].astype(f32)
            if off:
                window = pltpu.roll(window, LN - off, 1)
        else:
            window = drafts_ref[0, :, pl.ds(base, 2 * LN)].astype(f32)
            window = pltpu.roll(window, 2 * LN - off, 1)[:, :LN]
        a_buf[pl.ds(0, T), pl.ds(LN * j, LN)] = jnp.where(lane < ks, window, 0.0).astype(bf16)
        a_buf[pl.ds(T, T), pl.ds(LN * j, LN)] = jnp.where(
            dt_zone, pltpu.roll(window, ks, 1), 0.0
        ).astype(bf16)
        a_buf[pl.ds(2 * T, T), pl.ds(LN * j, LN)] = jnp.where(
            dt_zone, pltpu.roll(window, half, 1), 0.0
        ).astype(bf16)
    d_all[y_rows, :] = a_buf[pl.ds(0, T), pl.ds(pl.multiple_of(my * X * LN, X * LN), X * LN)]

    @pl.loop(1, Y)
    def _(i):
        yy = lax.rem(my + i, Y)
        put(
            a_buf.at[pl.ds(0, T), pl.ds(pl.multiple_of(yy * X * LN, X * LN), X * LN)],
            d_all.at[y_rows, :],
            1,
            {"req": yy * X + mx},
        )

    @pl.loop(1, X)
    def _(i):
        r = my * X + lax.rem(mx + i, X)
        put(w_ext.at[own_outs, :], w_ext.at[own_outs, :], 9, {"req": r})

    arrive("dt_bias", "decay", "cbs", "cxs", "sink_b", "sink_x")
    head_buf[...] = jnp.zeros(head_buf.shape, f32)
    head_buf[pl.ds(0, 1), pl.ds(0, heads)] = dt_bias_ref[...].reshape(1, heads)
    head_buf[pl.ds(1, 1), pl.ds(0, heads)] = decay_ref[...].reshape(1, heads)
    s_bc[...] = jnp.zeros(s_bc.shape, f32)
    s_bc[pl.ds(T - KC + 1, KC - 1), :] = cbs_ref[0].astype(f32)
    s_x[...] = jnp.zeros(s_x.shape, f32)
    s_x[pl.ds(T - KC + 1, KC - 1), :] = cxs_ref[0].astype(f32)
    bs_buf[...] = jnp.zeros(bs_buf.shape, f32)
    bs_buf[pl.ds(T, 4), :] = sink_b_ref[0].astype(f32)
    xs_buf[...] = jnp.zeros(xs_buf.shape, f32)
    xs_buf[pl.ds(T, 4), :] = sink_x_ref[0].astype(f32)
    arrive("slot_req", "slot_page", "page_count", "owner_row", "accepted")
    rows_of = []
    live_of = []
    for s in range(slots):
        req = slot_req_ref[s]
        guarded = jnp.maximum(req, 0)
        live_of.append((req >= 0) & (slot_page_ref[s] < page_count_ref[guarded]))
        rows_of.append(owner_row_ref[guarded])
    by_sub = jnp.zeros((slots * T, 1), jnp.int32)
    by_lane = jnp.zeros((1, slots * T), jnp.int32)
    live_sub = jnp.zeros((slots * T, 1), jnp.int32)
    for s in range(slots):
        in_sub = lax.div(iota((slots * T, 1), 0), T) == s
        in_lane = lax.div(iota((1, slots * T), 1), T) == s
        by_sub = jnp.where(in_sub, rows_of[s], by_sub)
        live_sub = jnp.where(in_sub, live_of[s].astype(jnp.int32), live_sub)
        by_lane = jnp.where(
            in_lane, jnp.where(live_of[s], rows_of[s], -(1 << 20)), by_lane
        )
    wide_lane = iota((slots * T, R * CROWS), 1)
    at = lax.rem(iota((slots * T, 1), 0), T)
    gather_c = (wide_lane == CROWS * by_sub + at).astype(bf16)
    gather_cum = (wide_lane == CROWS * by_sub + T + lax.div(at, 8)).astype(bf16)
    at = lax.rem(iota((1, slots * T), 1), T)
    tall_sub = iota((R * 8, slots * T), 0)
    scatter_low = ((tall_sub == 8 * by_lane + at) & (at < 8)).astype(bf16)
    scatter_high = ((tall_sub == 8 * by_lane + at - 8) & (at >= 8)).astype(bf16)

    arrive("cbb", "cbw", "cxb", "cxw", "gain", "ssm", "page_x", "page_b", "page_decay")

    eye_h = iota((heads, LN), 0) == iota((heads, LN), 1)

    @pl.loop(0, slots)
    def _(s):
        decays = page_decay_ref[s]
        least = jnp.min(decays, axis=1, keepdims=True)
        least_buf[s] = jnp.sum(jnp.where(eye_h, least, 0.0), axis=0, keepdims=True)
        factor = jnp.exp(least - decays)
        for h in range(heads):
            rows = pl.ds(h * HD, HD)
            faded = page_x_ref[s, rows, :].astype(f32) * factor[h : h + 1, :]
            state_buf[s, rows, :] = jnp.dot(
                faded.astype(bf16), page_b_ref[s], preferred_element_type=f32
            ).astype(bf16)


    wait_bytes(w_all.at[:, pl.ds(0, (R - 1) * LN)], recv_sem.at[0])
    proj = nt(a_buf[...], w_all[...])
    z_own[...] = nt((iota((T, T), 0) == iota((T, T), 1)).astype(bf16), proj.astype(bf16)).astype(bf16)
    z_rows = pl.ds(pl.multiple_of(mf * T, T), T)
    z_all[z_rows, :] = z_own[...]

    @pl.loop(1, F)
    def _(i):
        put(z_own, z_all.at[z_rows, :], 2, {"fsdp": lax.rem(mf + i, F)})

    er = iota((T, LN), 0)
    el = iota((T, LN), 1)
    first = ((er == el) & (el < heads)).astype(f32)
    second = ((er == el + heads) & (el < heads)).astype(f32)
    dt_raw = jnp.dot(proj[T : 2 * T], first, precision=EXACT, preferred_element_type=f32) + jnp.dot(
        proj[2 * T : 3 * T], second, precision=EXACT, preferred_element_type=f32
    )
    v = dt_raw + head_buf[pl.ds(0, 1), :]
    dtime = jnp.maximum(v, 0.0) + jnp.log1p(jnp.exp(-jnp.abs(v)))
    upto = (iota((T, T), 1) <= iota((T, T), 0)).astype(f32)
    cumul = -jnp.dot(
        upto, dtime * head_buf[pl.ds(1, 1), :], precision=EXACT, preferred_element_type=f32
    )
    hi, mid, low = pieces3(cumul)
    packed = hi + pltpu.roll(mid, 5, 1) + pltpu.roll(low, 10, 1)
    for step in (16, 32, 64):
        packed = packed + pltpu.roll(packed, step, 1)
    packed = jnp.where(lax.div(el, T) == lax.rem(er, 8), packed, 0.0)
    packed_low = jnp.sum(jnp.where(er < 8, packed, 0.0), axis=0, keepdims=True)
    packed_high = jnp.sum(jnp.where(er >= 8, packed, 0.0), axis=0, keepdims=True)
    row8 = iota((8, LN), 0)
    packed = jnp.where(row8 == 0, packed_low, jnp.where(row8 == 1, packed_high, 0.0))

    wait_bytes(z_all.at[pl.ds(0, (F - 1) * T), :], recv_sem.at[2])
    bc_raw = nt((iota((T, LN), 0) == iota((T, LN), 1)).astype(bf16), z_all[...])
    s_bc[pl.ds(T, T), :] = bc_raw
    acc = jnp.zeros((T, 2 * ns), f32) + cbb_ref[...].astype(f32).reshape(1, 2 * ns)
    for k in range(KC):
        acc = acc + cbw_ref[pl.ds(k, 1), :].astype(f32) * s_bc[pl.ds(T - KC + 1 + k, T), :]
    bc_act = silu(acc)
    b_mat = bc_act[:, :ns].astype(bf16)
    c_mat = bc_act[:, ns:].astype(bf16)
    if ns < LN:
        cc_own[...] = jnp.zeros(cc_own.shape, bf16)
    cc_own[pl.ds(0, T), pl.ds(0, ns)] = c_mat
    cc_own[pl.ds(T, 8), :] = packed.astype(bf16)
    cc_all[me] = cc_own[...]

    @pl.loop(1, R)
    def _(i):
        put(cc_own, cc_all.at[me], 3, {"req": lax.rem(me + i, R)})

    wait_bytes(d_all.at[pl.ds(0, (Y - 1) * T), :], recv_sem.at[1])
    wait_bytes(w_bytes, recv_sem.at[8])
    xz_send[...] = jnp.dot(d_all[...], wxz[...], preferred_element_type=f32).astype(bf16)
    xz_recv[my] = xz_send[y_rows, :]

    @pl.loop(1, Y)
    def _(i):
        yy = lax.rem(my + i, Y)
        put(
            xz_send.at[pl.ds(pl.multiple_of(yy * T, T), T), :],
            xz_recv.at[my],
            4,
            {"req": yy * X + mx},
        )

    head_lane = lax.div(iota((T, inner), 1), HD)

    def own_heads(stacked):
        out = jnp.where(head_lane == 0, stacked[0:T], 0.0)
        for h in range(1, heads):
            out = jnp.where(head_lane == h, stacked[h * T : (h + 1) * T], out)
        return out

    wait_bytes(cc_all.at[pl.ds(0, R - 1)], recv_sem.at[3])
    cc = cc_all[...].reshape(R * CROWS, LN)
    q_buf[...] = jnp.dot(gather_c, cc, preferred_element_type=f32)[:, :ns].astype(bf16)
    cum3 = jnp.dot(gather_cum, cc, preferred_element_type=f32)
    at = lax.rem(iota((slots * T, LN), 0), T)
    el = iota((slots * T, LN), 1)
    cum3 = jnp.where(lax.div(el, T) == lax.rem(at, 8), cum3, 0.0)
    for step in (64, 32, 16):
        cum3 = cum3 + pltpu.roll(cum3, step, 1)
    cum = cum3 + pltpu.roll(cum3, LN - 5, 1) + pltpu.roll(cum3, LN - 10, 1)
    cum_buf[...] = cum

    for s in range(slots):
        rows = pl.ds(s * T, T)
        factor = jnp.exp(cum_buf[rows, :] - least_buf[s])
        spread = jnp.zeros((T, inner), f32)
        for h in range(heads):
            spread = jnp.where(head_lane == h, factor[:, h : h + 1], spread)
        terms[rows, :] = nt(q_buf[rows, :], state_buf[s]) * spread

    kept_terms = jnp.where(live_sub != 0, terms[...], 0.0).astype(bf16)
    low = jnp.dot(scatter_low, kept_terms, preferred_element_type=f32)
    high = jnp.dot(scatter_high, kept_terms, preferred_element_type=f32)
    p_send[:, :, pl.ds(0, inner)] = low.astype(bf16).reshape(R, 8, inner)
    p_send[:, :, pl.ds(inner, inner)] = high.astype(bf16).reshape(R, 8, inner)
    p_recv[me] = p_send[me]

    @pl.loop(1, R)
    def _(i):
        r = lax.rem(me + i, R)
        put(p_send.at[r], p_recv.at[me], 5, {"req": r})

    wait_bytes(xz_recv.at[pl.ds(0, Y - 1)], recv_sem.at[4])
    xz = lax.fori_loop(
        1, Y, lambda i, total: total + xz_recv[i].astype(f32), xz_recv[0].astype(f32)
    )
    x_raw = xz[:, :inner].astype(bf16).astype(f32)
    z_raw = xz[:, inner:].astype(bf16).astype(f32)
    s_x[pl.ds(T, T), :] = x_raw
    acc = jnp.zeros((T, inner), f32) + cxb_ref[...].astype(f32).reshape(1, inner)
    for k in range(KC):
        acc = acc + cxw_ref[pl.ds(k, 1), :].astype(f32) * s_x[pl.ds(T - KC + 1 + k, T), :]
    x_act = silu(acc).astype(bf16).astype(f32)
    xs_buf[pl.ds(0, T), :] = x_act
    bs_buf[pl.ds(0, T), :] = b_mat.astype(f32)
    scores = nt(c_mat, bs_buf[...].astype(bf16))
    zeros_t = jnp.zeros((T, LN), f32)
    eye8 = (iota((8, LN), 0) == iota((8, LN), 1)).astype(f32)
    cumul_t = nt(eye8, jnp.concatenate([cumul, zeros_t], axis=0), EXACT)
    dtime_t = nt(eye8, jnp.concatenate([dtime, zeros_t], axis=0), EXACT)
    at = iota((T, 2 * T), 0)
    au = iota((T, 2 * T), 1)
    for h in range(heads):
        spread = jnp.where(au <= at, cumul[:, h : h + 1] - cumul_t[h : h + 1, :], 0.0)
        factor = jnp.exp(spread) * dtime_t[h : h + 1, :]
        factor = jnp.where(au >= T, 1.0, jnp.where(au <= at, factor, 0.0))
        w5[pl.ds(h * T, T), pl.ds(0, 2 * T)] = (scores * factor).astype(bf16)
    local = own_heads(
        jnp.dot(
            w5[:, pl.ds(0, 2 * T)], xs_buf[...].astype(bf16), preferred_element_type=f32
        )
    )

    taken = accepted_ref[...]
    at = iota((T, LN), 0)
    last = jnp.sum(jnp.where(at == taken - 1, cumul, 0.0), axis=0, keepdims=True)
    spread = jnp.where(at < taken, last - cumul, 0.0)
    coeff = jnp.where(at < taken, jnp.exp(spread) * dtime, 0.0)
    coeff_x = jnp.zeros((T, inner), f32)
    for h in range(heads):
        coeff_x = jnp.where(head_lane == h, coeff[:, h : h + 1], coeff_x)
    y = coeff_x * x_act
    y_hi = y.astype(bf16).astype(f32)
    y2 = jnp.concatenate([y_hi, y - y_hi], axis=0).astype(bf16)
    b2 = jnp.concatenate([b_mat, b_mat], axis=0)
    fresh = lax.dot_general(
        y2, b2, (((0,), (0,)), ((), ())), preferred_element_type=f32
    )
    keep = jnp.exp(last)
    for h in range(heads):
        state_ref[0, h] = keep[:, h : h + 1] * ssm_ref[0, h] + fresh[h * HD : (h + 1) * HD]
    tail_pick = (
        iota((8, 2 * T), 1) == T - KC + 1 + taken + iota((8, 2 * T), 0)
    ).astype(bf16)
    ncx = jnp.dot(tail_pick, s_x[...].astype(bf16), preferred_element_type=f32)
    ncx_ref[0] = ncx[: KC - 1].astype(bf16)
    ncb = jnp.dot(tail_pick, s_bc[...].astype(bf16), preferred_element_type=f32)
    ncb_ref[0] = ncb[: KC - 1].astype(bf16)
    gate = silu(z_raw)

    wait_bytes(p_recv.at[pl.ds(0, R - 1)], recv_sem.at[5])
    page_sum = lax.fori_loop(
        1, R, lambda i, total: total + p_recv[i].astype(f32), p_recv[0].astype(f32)
    )
    page_sum = jnp.concatenate([page_sum[:, :inner], page_sum[:, inner:]], axis=0)
    gated = (page_sum + local) * gate
    squares = jnp.sum(gated * gated, axis=1, keepdims=True)
    hi, mid, low = pieces3(squares)
    el = iota((T, tail), 1)
    g_own[:, pl.ds(0, inner)] = (gated * gain_ref[...].astype(f32).reshape(1, inner)).astype(bf16)
    g_own[:, pl.ds(inner, tail)] = jnp.where(
        el == 0, hi, jnp.where(el == 1, mid, jnp.where(el == 2, low, 0.0))
    ).astype(bf16)
    g_all[y_rows, :] = g_own[...]

    @pl.loop(1, Y)
    def _(i):
        put(g_own, g_all.at[y_rows, :], 6, {"req": lax.rem(my + i, Y) * X + mx})

    wait_bytes(o_bytes, recv_sem.at[9])
    wait_bytes(g_all.at[pl.ds(0, (Y - 1) * T), :], recv_sem.at[6])
    f_send[...] = nt(g_all[...], w_ext[...]).astype(bf16)

    for b in range(per_row):
        lanes = pl.ds(2 * LN * b, 2 * LN)
        target = per_row * my + b

        @pl.when(target == mf)
        def _():
            f_recv[mf] = f_send[y_rows, lanes]

        @pl.when(target != mf)
        def _():
            put(f_send.at[y_rows, lanes], f_recv.at[mf], 7, {"fsdp": target})

        @pl.loop(1, Y)
        def _(i):
            yy = lax.rem(my + i, Y)
            put(
                f_send.at[pl.ds(pl.multiple_of(yy * T, T), T), lanes],
                f_recv.at[mf],
                7,
                {"req": yy * X + mx, "fsdp": target},
            )

    @pl.when(is_self)
    def _():
        wait_bytes(f_recv.at[pl.ds(0, F - 1)], recv_sem.at[7])

    @pl.when(jnp.logical_not(is_self))
    def _():
        wait_bytes(f_recv, recv_sem.at[7])

    out = lax.fori_loop(
        1, F, lambda i, total: total + f_recv[i].astype(f32), f_recv[0].astype(f32)
    )
    wide = 2 * ocols
    total_squares = (
        out[:, wide : wide + 1] + out[:, wide + 1 : wide + 2] + out[:, wide + 2 : wide + 3]
    )
    scale = lax.rsqrt(total_squares / total_inner + EPSILON)
    mixed_ref[0] = (out * scale)[:, :wide].astype(bf16)

    wait_bytes(w_all.at[:, pl.ds(0, (R - 1) * LN)], send_sem.at[0])
    wait_bytes(d_all.at[pl.ds(0, (Y - 1) * T), :], send_sem.at[1])
    wait_bytes(z_all.at[pl.ds(0, (F - 1) * T), :], send_sem.at[2])
    wait_bytes(cc_all.at[pl.ds(0, R - 1)], send_sem.at[3])
    wait_bytes(xz_recv.at[pl.ds(0, Y - 1)], send_sem.at[4])
    wait_bytes(w_bytes, send_sem.at[8])
    wait_bytes(o_bytes, send_sem.at[9])
    wait_bytes(p_recv.at[pl.ds(0, R - 1)], send_sem.at[5])
    wait_bytes(g_all.at[pl.ds(0, (Y - 1) * T), :], send_sem.at[6])

    @pl.when(is_self)
    def _():
        wait_bytes(f_recv.at[pl.ds(0, F - 1)], send_sem.at[7])

    @pl.when(jnp.logical_not(is_self))
    def _():
        wait_bytes(f_recv, send_sem.at[7])


def hand_over(*refs):
    sem = refs[8]
    copies = [pltpu.make_async_copy(refs[i], refs[4 + i], sem.at[i]) for i in range(4)]
    for copy in copies:
        copy.start()
    for copy in copies:
        copy.wait()


def per_device(
    R,
    F,
    drafts,
    x_weight,
    z_weight,
    bc_weight,
    dt_weight,
    dt_bias,
    decay_rate,
    conv_x_weight,
    conv_x_bias,
    conv_bc_weight,
    conv_bc_bias,
    norm_gain,
    out_weight,
    conv_x_state,
    conv_bc_state,
    ssm_state,
    sink_x,
    sink_b,
    page_x,
    page_b,
    page_decay,
    slot_req,
    slot_page,
    page_count,
    accepted,
    owner_row,
):
    inner = x_weight.shape[1]
    ns = bc_weight.shape[1] // 2
    slots, page, _ = page_x.shape
    heads = dt_weight.shape[1]
    ocols = out_weight.shape[1]
    pad_in = -(-inner // LN) * LN
    Y = R // X
    vmem = pl.BlockSpec(memory_space=pltpu.VMEM)
    shape = jax.ShapeDtypeStruct
    operands = (
        drafts,
        x_weight,
        z_weight,
        bc_weight,
        dt_weight.T,
        dt_bias,
        decay_rate,
        conv_x_weight,
        conv_x_bias,
        conv_bc_weight,
        conv_bc_bias,
        norm_gain,
        out_weight.T,
        conv_x_state,
        conv_bc_state,
        ssm_state,
        sink_x,
        sink_b,
        jnp.swapaxes(page_x, 1, 2),
        page_b,
        page_decay,
        slot_req,
        slot_page,
        page_count,
        accepted.reshape(1, 1),
        owner_row,
    )
    held = [
        (pltpu.SMEM if name in SCALARS else pltpu.VMEM)(a.shape, a.dtype)
        for name, a in zip(NAMES, operands)
    ]
    scratch = held + [
        pltpu.VMEM((T, LN), f32),
        pltpu.VMEM((LN, R * LN), bf16),
        pltpu.VMEM((T, LN), bf16),
        pltpu.VMEM((T, R * LN), bf16),
        pltpu.VMEM((Y * T, X * LN), bf16),
        pltpu.VMEM((X * LN, 2 * inner), bf16),
        pltpu.VMEM((Y * T, 2 * inner), bf16),
        pltpu.VMEM((Y, T, 2 * inner), bf16),
        pltpu.VMEM((T, LN), bf16),
        pltpu.VMEM((F * T, LN), bf16),
        pltpu.VMEM((8, LN), f32),
        pltpu.VMEM((2 * T, 2 * ns), f32),
        pltpu.VMEM((CROWS, LN), bf16),
        pltpu.VMEM((R, CROWS, LN), bf16),
        pltpu.VMEM((slots, inner, ns), bf16),
        pltpu.VMEM((slots, 1, LN), f32),
        pltpu.VMEM((slots * T, ns), bf16),
        pltpu.VMEM((slots * T, LN), f32),
        pltpu.VMEM((heads * T, page), bf16),
        pltpu.VMEM((slots * T, inner), f32),
        pltpu.VMEM((R, 8, 2 * inner), bf16),
        pltpu.VMEM((R, 8, 2 * inner), bf16),
        pltpu.VMEM((2 * T, inner), f32),
        pltpu.VMEM((2 * T, inner), f32),
        pltpu.VMEM((2 * T, ns), f32),
        pltpu.VMEM((T, pad_in), bf16),
        pltpu.VMEM((Y * T, pad_in), bf16),
        pltpu.VMEM((X * LN, pad_in), bf16),
        pltpu.VMEM((Y * T, X * LN), bf16),
        pltpu.VMEM((F, T, 2 * LN), bf16),
        pltpu.SemaphoreType.DMA((10,)),
        pltpu.SemaphoreType.DMA((10,)),
        pltpu.SemaphoreType.DMA((26,)),
    ]
    results = pl.pallas_call(
        functools.partial(kernel, R, F),
        out_shape=(
            shape((1, T, 2 * ocols), bf16),
            shape(ssm_state.shape, f32),
            shape(conv_x_state.shape, bf16),
            shape(conv_bc_state.shape, bf16),
        ),
        in_specs=[pl.BlockSpec(memory_space=pltpu.HBM)] * 26,
        out_specs=(vmem,) * 4,
        scratch_shapes=scratch,
        compiler_params=pltpu.CompilerParams(
            collective_id=0, has_side_effects=True
        ),
        name="mixer",
    )(*operands)
    hbm = pl.BlockSpec(memory_space=pltpu.HBM)
    return pl.pallas_call(
        hand_over,
        out_shape=tuple(shape(a.shape, a.dtype) for a in results),
        in_specs=[hbm] * 4,
        out_specs=(hbm,) * 4,
        scratch_shapes=[pltpu.SemaphoreType.DMA((4,))],
        name="hand_over",
    )(*results)


def solution(mesh):
    in_specs = (
        P("req", None, None),
        P("req", "fsdp"),
        P("req", "fsdp"),
        P("req", None),
        P("req", "fsdp"),
        P("fsdp"),
        P("fsdp"),
        P(None, "fsdp"),
        P("fsdp"),
        P(),
        P(),
        P("fsdp"),
        P("fsdp", "req"),
        P("req", None, "fsdp"),
        P("req", None, None),
        P("req", "fsdp", None, None),
        P("req", None, "fsdp"),
        P("req", None, None),
        P("req", None, "fsdp"),
        P("req", None, None),
        P("req", "fsdp", None),
        P("req"),
        P("req"),
        P(),
        P("req"),
        P(),
    )
    out_specs = (
        P("req", None, "fsdp"),
        P("req", "fsdp", None, None),
        P("req", None, "fsdp"),
        P("req", None, None),
    )
    return jax.shard_map(
        functools.partial(per_device, mesh.shape["req"], mesh.shape["fsdp"]),
        mesh=mesh,
        in_specs=in_specs,
        out_specs=out_specs,
        check_vma=False,
    )
```

```python
import functools

import jax
import jax.numpy as jnp
from jax import lax
from jax.experimental import pallas as pl
from jax.experimental.pallas import tpu as pltpu
from jax.sharding import PartitionSpec as P

MESH = pl.DeviceIdType.MESH
T = 16
CROWS = 24
X = 4
KC = 4
HD = 64
LN = 128
EPSILON = 1e-05
f32 = jnp.float32
bf16 = jnp.bfloat16
EXACT = lax.Precision.HIGHEST
NAMES = (
    "drafts",
    "xw",
    "zw",
    "bcw",
    "dtw",
    "dt_bias",
    "decay",
    "cxw",
    "cxb",
    "cbw",
    "cbb",
    "gain",
    "ow",
    "cxs",
    "cbs",
    "ssm",
    "sink_x",
    "sink_b",
    "page_x",
    "page_b",
    "page_decay",
    "slot_req",
    "slot_page",
    "page_count",
    "accepted",
    "owner_row",
)
SCALARS = ("slot_req", "slot_page", "page_count", "owner_row")
FIRST = ("bcw", "dtw")
SECOND = ("drafts", "xw", "zw", "ow")
OTHERS = tuple(n for n in NAMES if n not in FIRST + SECOND)


def nt(a, b, precision=None):
    return lax.dot_general(
        a, b, (((1,), (1,)), ((), ())), preferred_element_type=f32, precision=precision
    )


def iota(shape, axis):
    return lax.broadcasted_iota(jnp.int32, shape, axis)


def silu(v):
    return v * jax.nn.sigmoid(v)


def pieces3(v):
    hi = v.astype(bf16).astype(f32)
    rest = v - hi
    mid = rest.astype(bf16).astype(f32)
    low = (rest - mid).astype(bf16).astype(f32)
    return hi, mid, low


def kernel(R, F, *refs):
    sources, outs, held, rest = refs[:26], refs[26:30], refs[30:56], refs[56:-6]
    ready, load_sem, store_sem = refs[-6:-2], refs[-2], refs[-1]
    stores = [
        pltpu.make_async_copy(source, target, store_sem.at[i])
        for i, (source, target) in enumerate(zip(ready, outs))
    ]
    copies = [
        pltpu.make_async_copy(source, target, load_sem.at[i])
        for i, (source, target) in enumerate(zip(sources, held))
    ]

    def load(*names):
        for name in names:
            copies[NAMES.index(name)].start()

    def arrive(*names):
        for name in names:
            copies[NAMES.index(name)].wait()

    body(R, F, load, arrive, stores, *held, *ready, *rest)
    for store in stores:
        store.wait()


def body(
    R,
    F,
    load,
    arrive,
    stores,
    drafts_ref,
    xw_ref,
    zw_ref,
    bcw_ref,
    dtw_ref,
    dt_bias_ref,
    decay_ref,
    cxw_ref,
    cxb_ref,
    cbw_ref,
    cbb_ref,
    gain_ref,
    ow_ref,
    cxs_ref,
    cbs_ref,
    ssm_ref,
    sink_x_ref,
    sink_b_ref,
    page_x_ref,
    page_b_ref,
    page_decay_ref,
    slot_req_ref,
    slot_page_ref,
    page_count_ref,
    accepted_ref,
    owner_row_ref,
    mixed_ref,
    state_ref,
    ncx_ref,
    ncb_ref,
    dt_buf,
    a_buf,
    w_own,
    w_all,
    d_all,
    wxz,
    xz_send,
    xz_recv,
    z_own,
    z_all,
    head_buf,
    s_bc,
    cc_own,
    cc_all,
    state_buf,
    least_buf,
    q_buf,
    cum_buf,
    w5,
    pa_send,
    pa_recv,
    pb_send,
    pb_recv,
    s_x,
    xs_buf,
    bs_buf,
    g_own,
    g_all,
    w_ext,
    f_send,
    f_recv,
    send_sem,
    recv_sem,
):
    me = lax.axis_index("req")
    mf = lax.axis_index("fsdp")
    ks, inner = xw_ref.shape
    half = ks // 2
    heads = dtw_ref.shape[0]
    ns = bcw_ref.shape[1] // 2
    slots = page_x_ref.shape[0]
    total_inner = inner * F
    ocols = ow_ref.shape[0]
    pad_in = g_own.shape[1]
    Y = R // X
    per_row = X // 2
    my = lax.div(me, X)
    mx = lax.rem(me, X)
    is_self = lax.div(mf, per_row) == my

    load(*FIRST)
    barrier = pltpu.get_barrier_semaphore()

    @pl.loop(1, R)
    def _(i):
        pl.semaphore_signal(
            barrier, inc=1, device_id={"req": lax.rem(me + i, R)}, device_id_type=MESH
        )

    @pl.loop(1, F)
    def _(i):
        pl.semaphore_signal(
            barrier, inc=1, device_id={"fsdp": lax.rem(mf + i, F)}, device_id_type=MESH
        )

    source = lax.div(mf, per_row) * X + mx

    @pl.loop(0, F)
    def _(i):
        g = lax.rem(mf + i, F)

        @pl.when(jnp.logical_or(g != mf, source != me))
        def _():
            pl.semaphore_signal(
                barrier, inc=1, device_id={"req": source, "fsdp": g}, device_id_type=MESH
            )

    load(*SECOND)
    arrive("bcw", "dtw")
    wpad = jnp.concatenate([bcw_ref[...], jnp.zeros((LN - ks, 2 * ns), bf16)], axis=0)
    pick = (iota((T, 2 * ns), 1) == T * mf + iota((T, 2 * ns), 0)).astype(bf16)
    bc_rows = nt(pick, wpad)
    row = iota((T, LN), 0)
    lane = iota((T, LN), 1)
    dt_buf[...] = jnp.zeros(dt_buf.shape, f32)
    dt_buf[pl.ds(0, heads), pl.ds(0, ks)] = dtw_ref[...].astype(f32)
    dt_buf[pl.ds(heads, heads), pl.ds(0, ks)] = dtw_ref[...].astype(f32)
    dt_rows = dt_buf[...]
    dt_rows = jnp.where(
        row < heads, pltpu.roll(dt_rows, ks, 1), pltpu.roll(dt_rows, half, 1)
    )
    dt_zone = (lane >= ks) & (lane < ks + half)
    w_own[...] = jnp.where(
        lane < ks, bc_rows, jnp.where(dt_zone & (row < 2 * heads), dt_rows, 0.0)
    ).astype(bf16)
    w_all[:, pl.ds(pl.multiple_of(me * LN, LN), LN)] = w_own[...]

    own_rows = pl.ds(pl.multiple_of(me * T, T), T)
    y_rows = pl.ds(pl.multiple_of(my * T, T), T)
    pl.semaphore_wait(
        barrier, (R - 1) + (F - 1) + Y * per_row - is_self.astype(jnp.int32)
    )

    def put(src, dst, phase, device):
        pltpu.make_async_remote_copy(
            src_ref=src,
            dst_ref=dst,
            send_sem=send_sem.at[phase],
            recv_sem=recv_sem.at[phase],
            device_id=device,
            device_id_type=MESH,
        ).start()

    def wait_bytes(ref, sem):
        pltpu.make_async_copy(ref, ref, sem).wait()

    own_lanes = pl.ds(pl.multiple_of(me * LN, LN), LN)
    w_bytes = wxz.at[pl.ds(0, (X - 1) * ks), :]
    o_bytes = w_ext.at[pl.ds(0, (X - 1) * ocols), :]

    @pl.loop(1, R)
    def _(i):
        put(w_own, w_all.at[:, own_lanes], 0, {"req": lax.rem(me + i, R)})

    load(*OTHERS)

    own_block = pl.ds(pl.multiple_of(mx * LN, LN), ks)
    own_outs = pl.ds(
        pl.multiple_of(lax.div(mx, 2) * 2 * LN + lax.rem(mx, 2) * ocols, 16), ocols
    )
    tail = pad_in - inner
    for i in range(X):
        wxz[pl.ds(LN * i + ks, LN - ks), :] = jnp.zeros((LN - ks, 2 * inner), bf16)
    arrive("xw", "zw")
    wxz[own_block, pl.ds(0, inner)] = xw_ref[...]
    wxz[own_block, pl.ds(inner, inner)] = zw_ref[...]
    arrive("ow")
    w_ext[own_outs, pl.ds(0, inner)] = ow_ref[...]
    w_ext[own_outs, pl.ds(inner, tail)] = jnp.zeros((ocols, tail), bf16)
    rest = 2 * LN - 2 * ocols
    er = iota((rest, tail), 0)
    el = iota((rest, tail), 1)
    for i in range(per_row):
        top = pl.ds(2 * LN * i + 2 * ocols, rest)
        w_ext[top, pl.ds(0, inner)] = jnp.zeros((rest, inner), bf16)
        w_ext[top, pl.ds(inner, tail)] = ((er == el) & (el < 3)).astype(bf16)

    @pl.loop(1, X)
    def _(i):
        r = my * X + lax.rem(mx + i, X)
        put(wxz.at[own_block, :], wxz.at[own_block, :], 8, {"req": r})

    arrive("drafts")
    z_own[...] = jnp.zeros(z_own.shape, bf16)
    for j in range(R):
        start = ks * j
        base = start // LN * LN
        off = start - base
        if off + ks <= LN:
            window = drafts_ref[0, :, pl.ds(base, LN)].astype(f32)
            if off:
                window = pltpu.roll(window, LN - off, 1)
        else:
            window = drafts_ref[0, :, pl.ds(base, 2 * LN)].astype(f32)
            window = pltpu.roll(window, 2 * LN - off, 1)[:, :LN]
        a_buf[pl.ds(0, T), pl.ds(LN * j, LN)] = jnp.where(lane < ks, window, 0.0).astype(bf16)
        a_buf[pl.ds(T, T), pl.ds(LN * j, LN)] = jnp.where(
            dt_zone, pltpu.roll(window, ks, 1), 0.0
        ).astype(bf16)
        a_buf[pl.ds(2 * T, T), pl.ds(LN * j, LN)] = jnp.where(
            dt_zone, pltpu.roll(window, half, 1), 0.0
        ).astype(bf16)
    d_all[y_rows, :] = a_buf[pl.ds(0, T), pl.ds(pl.multiple_of(my * X * LN, X * LN), X * LN)]

    @pl.loop(1, Y)
    def _(i):
        yy = lax.rem(my + i, Y)
        put(
            a_buf.at[pl.ds(0, T), pl.ds(pl.multiple_of(yy * X * LN, X * LN), X * LN)],
            d_all.at[y_rows, :],
            1,
            {"req": yy * X + mx},
        )

    @pl.loop(1, X)
    def _(i):
        r = my * X + lax.rem(mx + i, X)
        put(w_ext.at[own_outs, :], w_ext.at[own_outs, :], 9, {"req": r})

    arrive("dt_bias", "decay", "cbs", "cxs", "sink_b", "sink_x")
    head_buf[...] = jnp.zeros(head_buf.shape, f32)
    head_buf[pl.ds(0, 1), pl.ds(0, heads)] = dt_bias_ref[...].reshape(1, heads)
    head_buf[pl.ds(1, 1), pl.ds(0, heads)] = decay_ref[...].reshape(1, heads)
    s_bc[...] = jnp.zeros(s_bc.shape, f32)
    s_bc[pl.ds(T - KC + 1, KC - 1), :] = cbs_ref[0].astype(f32)
    s_x[...] = jnp.zeros(s_x.shape, f32)
    s_x[pl.ds(T - KC + 1, KC - 1), :] = cxs_ref[0].astype(f32)
    bs_buf[...] = jnp.zeros(bs_buf.shape, f32)
    bs_buf[pl.ds(T, 4), :] = sink_b_ref[0].astype(f32)
    xs_buf[...] = jnp.zeros(xs_buf.shape, f32)
    xs_buf[pl.ds(T, 4), :] = sink_x_ref[0].astype(f32)
    arrive("cbb", "cbw", "cxb", "cxw", "gain", "ssm", "page_x", "page_b", "page_decay")

    wait_bytes(w_all.at[:, pl.ds(0, (R - 1) * LN)], recv_sem.at[0])
    proj = nt(a_buf[pl.ds(0, 3 * T), :], w_all[...])
    z_own[:, pl.ds(0, 3 * T)] = nt((iota((T, T), 0) == iota((T, T), 1)).astype(bf16), proj.astype(bf16)).astype(bf16)
    z_rows = pl.ds(pl.multiple_of(mf * T, T), T)
    z_all[z_rows, :] = z_own[...]

    @pl.loop(1, F)
    def _(i):
        put(z_own, z_all.at[z_rows, :], 2, {"fsdp": lax.rem(mf + i, F)})

    wait_bytes(d_all.at[pl.ds(0, (Y - 1) * T), :], recv_sem.at[1])
    wait_bytes(w_bytes, recv_sem.at[8])
    xz_send[...] = jnp.dot(d_all[...], wxz[...], preferred_element_type=f32).astype(bf16)
    xz_recv[my] = xz_send[y_rows, :]

    @pl.loop(1, Y)
    def _(i):
        yy = lax.rem(my + i, Y)
        put(
            xz_send.at[pl.ds(pl.multiple_of(yy * T, T), T), :],
            xz_recv.at[my],
            4,
            {"req": yy * X + mx},
        )

    er = iota((T, LN), 0)
    el = iota((T, LN), 1)
    first = ((er == el) & (el < heads)).astype(f32)
    second = ((er == el + heads) & (el < heads)).astype(f32)
    dt_raw = jnp.dot(proj[T : 2 * T], first, precision=EXACT, preferred_element_type=f32) + jnp.dot(
        proj[2 * T : 3 * T], second, precision=EXACT, preferred_element_type=f32
    )
    v = dt_raw + head_buf[pl.ds(0, 1), :]
    dtime = jnp.maximum(v, 0.0) + jnp.log1p(jnp.exp(-jnp.abs(v)))
    upto = (iota((T, T), 1) <= iota((T, T), 0)).astype(f32)
    cumul = -jnp.dot(
        upto, dtime * head_buf[pl.ds(1, 1), :], precision=EXACT, preferred_element_type=f32
    )
    hi, mid, low = pieces3(cumul)
    packed = hi + pltpu.roll(mid, 5, 1) + pltpu.roll(low, 10, 1)
    for step in (16, 32, 64):
        packed = packed + pltpu.roll(packed, step, 1)
    packed = jnp.where(lax.div(el, T) == lax.rem(er, 8), packed, 0.0)
    packed_low = jnp.sum(jnp.where(er < 8, packed, 0.0), axis=0, keepdims=True)
    packed_high = jnp.sum(jnp.where(er >= 8, packed, 0.0), axis=0, keepdims=True)
    row8 = iota((8, LN), 0)
    packed = jnp.where(row8 == 0, packed_low, jnp.where(row8 == 1, packed_high, 0.0))

    wait_bytes(z_all.at[pl.ds(0, (F - 1) * T), :], recv_sem.at[2])
    bc_raw = nt((iota((T, LN), 0) == iota((T, LN), 1)).astype(bf16), z_all[...])
    s_bc[pl.ds(T, T), :] = bc_raw
    acc = jnp.zeros((T, 2 * ns), f32) + cbb_ref[...].astype(f32).reshape(1, 2 * ns)
    for k in range(KC):
        acc = acc + cbw_ref[pl.ds(k, 1), :].astype(f32) * s_bc[pl.ds(T - KC + 1 + k, T), :]
    bc_act = silu(acc)
    b_mat = bc_act[:, :ns].astype(bf16)
    c_mat = bc_act[:, ns:].astype(bf16)
    if ns < LN:
        cc_own[...] = jnp.zeros(cc_own.shape, bf16)
    cc_own[pl.ds(0, T), pl.ds(0, ns)] = c_mat
    cc_own[pl.ds(T, 8), :] = packed.astype(bf16)
    cc_all[me] = cc_own[...]

    @pl.loop(1, R)
    def _(i):
        put(cc_own, cc_all.at[me], 3, {"req": lax.rem(me + i, R)})

    eye_h = iota((heads, LN), 0) == iota((heads, LN), 1)

    @pl.loop(0, slots)
    def _(s):
        decays = page_decay_ref[s]
        least = jnp.min(decays, axis=1, keepdims=True)
        least_buf[s] = jnp.sum(jnp.where(eye_h, least, 0.0), axis=0, keepdims=True)
        factor = jnp.exp(least - decays)
        for h in range(heads):
            rows = pl.ds(h * HD, HD)
            faded = page_x_ref[s, rows, :].astype(f32) * factor[h : h + 1, :]
            state_buf[s, rows, :] = jnp.dot(
                faded.astype(bf16), page_b_ref[s], preferred_element_type=f32
            ).astype(bf16)


    arrive("slot_req", "slot_page", "page_count", "owner_row", "accepted")
    rows_of = []
    live_of = []
    for s in range(slots):
        req = slot_req_ref[s]
        guarded = jnp.maximum(req, 0)
        live_of.append((req >= 0) & (slot_page_ref[s] < page_count_ref[guarded]))
        rows_of.append(owner_row_ref[guarded])
    by_sub = jnp.zeros((slots * T, 1), jnp.int32)
    by_lane = jnp.zeros((1, slots * T), jnp.int32)
    live_sub = jnp.zeros((slots * T, 1), jnp.int32)
    for s in range(slots):
        in_sub = lax.div(iota((slots * T, 1), 0), T) == s
        in_lane = lax.div(iota((1, slots * T), 1), T) == s
        by_sub = jnp.where(in_sub, rows_of[s], by_sub)
        live_sub = jnp.where(in_sub, live_of[s].astype(jnp.int32), live_sub)
        by_lane = jnp.where(
            in_lane, jnp.where(live_of[s], rows_of[s], -(1 << 20)), by_lane
        )
    wide_lane = iota((slots * T, R * CROWS), 1)
    at = lax.rem(iota((slots * T, 1), 0), T)
    gather_c = (wide_lane == CROWS * by_sub + at).astype(bf16)
    gather_cum = (wide_lane == CROWS * by_sub + T + lax.div(at, 8)).astype(bf16)
    at = lax.rem(iota((1, slots * T), 1), T)
    tall_sub = iota((R * 8, slots * T), 0)
    scatter_low = ((tall_sub == 8 * by_lane + at) & (at < 8)).astype(bf16)
    scatter_high = ((tall_sub == 8 * by_lane + at - 8) & (at >= 8)).astype(bf16)

    head_lane = lax.div(iota((T, inner), 1), HD)

    def own_heads(stacked):
        out = jnp.where(head_lane == 0, stacked[0:T], 0.0)
        for h in range(1, heads):
            out = jnp.where(head_lane == h, stacked[h * T : (h + 1) * T], out)
        return out

    wait_bytes(cc_all.at[pl.ds(0, R - 1)], recv_sem.at[3])
    cc = cc_all[...].reshape(R * CROWS, LN)
    q_buf[...] = jnp.dot(gather_c, cc, preferred_element_type=f32)[:, :ns].astype(bf16)
    cum3 = jnp.dot(gather_cum, cc, preferred_element_type=f32)
    at = lax.rem(iota((slots * T, LN), 0), T)
    el = iota((slots * T, LN), 1)
    cum3 = jnp.where(lax.div(el, T) == lax.rem(at, 8), cum3, 0.0)
    for step in (64, 32, 16):
        cum3 = cum3 + pltpu.roll(cum3, step, 1)
    cum = cum3 + pltpu.roll(cum3, LN - 5, 1) + pltpu.roll(cum3, LN - 10, 1)
    cum_buf[...] = cum

    cut = 2 * HD
    for first_head, send, recv, phase in ((0, pa_send, pa_recv, 5), (2, pb_send, pb_recv, 10)):
        lanes = cut if first_head == 0 else inner - cut
        part = pl.ds(first_head * HD, lanes)
        lane_head = lax.div(iota((T, lanes), 1), HD) + first_head
        chosen = []
        for s in range(slots):
            rows = pl.ds(s * T, T)
            factor = jnp.exp(cum_buf[rows, :] - least_buf[s])
            spread = jnp.zeros((T, lanes), f32)
            for h in range(first_head, first_head + lanes // HD):
                spread = jnp.where(lane_head == h, factor[:, h : h + 1], spread)
            chosen.append(nt(q_buf[rows, :], state_buf[s, part, :]) * spread)
        kept = jnp.where(live_sub != 0, jnp.concatenate(chosen, axis=0), 0.0).astype(bf16)
        low = jnp.dot(scatter_low, kept, preferred_element_type=f32)
        high = jnp.dot(scatter_high, kept, preferred_element_type=f32)
        send[:, :, pl.ds(0, lanes)] = low.astype(bf16).reshape(R, 8, lanes)
        send[:, :, pl.ds(lanes, lanes)] = high.astype(bf16).reshape(R, 8, lanes)
        recv[me] = send[me]

        @pl.loop(1, R)
        def _(i, send=send, recv=recv, phase=phase):
            r = lax.rem(me + i, R)
            put(send.at[r], recv.at[me], phase, {"req": r})

    wait_bytes(xz_recv.at[pl.ds(0, Y - 1)], recv_sem.at[4])
    xz = lax.fori_loop(
        1, Y, lambda i, total: total + xz_recv[i].astype(f32), xz_recv[0].astype(f32)
    )
    x_raw = xz[:, :inner].astype(bf16).astype(f32)
    z_raw = xz[:, inner:].astype(bf16).astype(f32)
    s_x[pl.ds(T, T), :] = x_raw
    acc = jnp.zeros((T, inner), f32) + cxb_ref[...].astype(f32).reshape(1, inner)
    for k in range(KC):
        acc = acc + cxw_ref[pl.ds(k, 1), :].astype(f32) * s_x[pl.ds(T - KC + 1 + k, T), :]
    x_act = silu(acc).astype(bf16).astype(f32)
    xs_buf[pl.ds(0, T), :] = x_act
    bs_buf[pl.ds(0, T), :] = b_mat.astype(f32)
    scores = nt(c_mat, bs_buf[...].astype(bf16))
    zeros_t = jnp.zeros((T, LN), f32)
    eye8 = (iota((8, LN), 0) == iota((8, LN), 1)).astype(f32)
    cumul_t = nt(eye8, jnp.concatenate([cumul, zeros_t], axis=0), EXACT)
    dtime_t = nt(eye8, jnp.concatenate([dtime, zeros_t], axis=0), EXACT)
    at = iota((T, 2 * T), 0)
    au = iota((T, 2 * T), 1)
    for h in range(heads):
        spread = jnp.where(au <= at, cumul[:, h : h + 1] - cumul_t[h : h + 1, :], 0.0)
        factor = jnp.exp(spread) * dtime_t[h : h + 1, :]
        factor = jnp.where(au >= T, 1.0, jnp.where(au <= at, factor, 0.0))
        w5[pl.ds(h * T, T), pl.ds(0, 2 * T)] = (scores * factor).astype(bf16)
    local = own_heads(
        jnp.dot(
            w5[:, pl.ds(0, 2 * T)], xs_buf[...].astype(bf16), preferred_element_type=f32
        )
    )

    taken = accepted_ref[...]
    at = iota((T, LN), 0)
    last = jnp.sum(jnp.where(at == taken - 1, cumul, 0.0), axis=0, keepdims=True)
    spread = jnp.where(at < taken, last - cumul, 0.0)
    coeff = jnp.where(at < taken, jnp.exp(spread) * dtime, 0.0)
    coeff_x = jnp.zeros((T, inner), f32)
    for h in range(heads):
        coeff_x = jnp.where(head_lane == h, coeff[:, h : h + 1], coeff_x)
    y = coeff_x * x_act
    y_hi = y.astype(bf16).astype(f32)
    y2 = jnp.concatenate([y_hi, y - y_hi], axis=0).astype(bf16)
    b2 = jnp.concatenate([b_mat, b_mat], axis=0)
    fresh = lax.dot_general(
        y2, b2, (((0,), (0,)), ((), ())), preferred_element_type=f32
    )
    keep = jnp.exp(last)
    for h in range(heads):
        state_ref[0, h] = keep[:, h : h + 1] * ssm_ref[0, h] + fresh[h * HD : (h + 1) * HD]
    tail_pick = (
        iota((8, 2 * T), 1) == T - KC + 1 + taken + iota((8, 2 * T), 0)
    ).astype(bf16)
    ncx = jnp.dot(tail_pick, s_x[...].astype(bf16), preferred_element_type=f32)
    ncx_ref[0] = ncx[: KC - 1].astype(bf16)
    ncb = jnp.dot(tail_pick, s_bc[...].astype(bf16), preferred_element_type=f32)
    ncb_ref[0] = ncb[: KC - 1].astype(bf16)
    for store in stores[1:]:
        store.start()
    gate = silu(z_raw)

    parts = []
    for recv, phase in ((pa_recv, 5), (pb_recv, 10)):
        wait_bytes(recv.at[pl.ds(0, R - 1)], recv_sem.at[phase])
        part = lax.fori_loop(
            1, R, lambda i, total, recv=recv: total + recv[i].astype(f32), recv[0].astype(f32)
        )
        lanes = part.shape[1] // 2
        parts.append(jnp.concatenate([part[:, :lanes], part[:, lanes:]], axis=0))
    page_sum = jnp.concatenate(parts, axis=1)
    gated = (page_sum + local) * gate
    squares = jnp.sum(gated * gated, axis=1, keepdims=True)
    hi, mid, low = pieces3(squares)
    el = iota((T, tail), 1)
    g_own[:, pl.ds(0, inner)] = (gated * gain_ref[...].astype(f32).reshape(1, inner)).astype(bf16)
    g_own[:, pl.ds(inner, tail)] = jnp.where(
        el == 0, hi, jnp.where(el == 1, mid, jnp.where(el == 2, low, 0.0))
    ).astype(bf16)
    g_all[y_rows, :] = g_own[...]

    @pl.loop(1, Y)
    def _(i):
        put(g_own, g_all.at[y_rows, :], 6, {"req": lax.rem(my + i, Y) * X + mx})

    wait_bytes(o_bytes, recv_sem.at[9])
    wait_bytes(g_all.at[pl.ds(0, (Y - 1) * T), :], recv_sem.at[6])
    f_send[...] = nt(g_all[...], w_ext[...]).astype(bf16)

    for b in range(per_row):
        lanes = pl.ds(2 * LN * b, 2 * LN)
        target = per_row * my + b

        @pl.when(target == mf)
        def _():
            f_recv[mf] = f_send[y_rows, lanes]

        @pl.when(target != mf)
        def _():
            put(f_send.at[y_rows, lanes], f_recv.at[mf], 7, {"fsdp": target})

        @pl.loop(1, Y)
        def _(i):
            yy = lax.rem(my + i, Y)
            put(
                f_send.at[pl.ds(pl.multiple_of(yy * T, T), T), lanes],
                f_recv.at[mf],
                7,
                {"req": yy * X + mx, "fsdp": target},
            )

    @pl.when(is_self)
    def _():
        wait_bytes(f_recv.at[pl.ds(0, F - 1)], recv_sem.at[7])

    @pl.when(jnp.logical_not(is_self))
    def _():
        wait_bytes(f_recv, recv_sem.at[7])

    out = lax.fori_loop(
        1, F, lambda i, total: total + f_recv[i].astype(f32), f_recv[0].astype(f32)
    )
    wide = 2 * ocols
    total_squares = (
        out[:, wide : wide + 1] + out[:, wide + 1 : wide + 2] + out[:, wide + 2 : wide + 3]
    )
    scale = lax.rsqrt(total_squares / total_inner + EPSILON)
    mixed_ref[0] = (out * scale)[:, :wide].astype(bf16)
    stores[0].start()

    wait_bytes(w_all.at[:, pl.ds(0, (R - 1) * LN)], send_sem.at[0])
    wait_bytes(d_all.at[pl.ds(0, (Y - 1) * T), :], send_sem.at[1])
    wait_bytes(z_all.at[pl.ds(0, (F - 1) * T), :], send_sem.at[2])
    wait_bytes(cc_all.at[pl.ds(0, R - 1)], send_sem.at[3])
    wait_bytes(xz_recv.at[pl.ds(0, Y - 1)], send_sem.at[4])
    wait_bytes(w_bytes, send_sem.at[8])
    wait_bytes(o_bytes, send_sem.at[9])
    wait_bytes(pa_recv.at[pl.ds(0, R - 1)], send_sem.at[5])
    wait_bytes(pb_recv.at[pl.ds(0, R - 1)], send_sem.at[10])
    wait_bytes(g_all.at[pl.ds(0, (Y - 1) * T), :], send_sem.at[6])

    @pl.when(is_self)
    def _():
        wait_bytes(f_recv.at[pl.ds(0, F - 1)], send_sem.at[7])

    @pl.when(jnp.logical_not(is_self))
    def _():
        wait_bytes(f_recv, send_sem.at[7])


def hand_over(*refs):
    held, sem = refs[8:12], refs[12]
    reads = [pltpu.make_async_copy(refs[i], held[i], sem.at[i]) for i in range(4)]
    writes = [pltpu.make_async_copy(held[i], refs[4 + i], sem.at[4 + i]) for i in range(4)]
    for read in reads:
        read.start()
    for read, write in zip(reads, writes):
        read.wait()
        write.start()
    for write in writes:
        write.wait()


def per_device(
    R,
    F,
    drafts,
    x_weight,
    z_weight,
    bc_weight,
    dt_weight,
    dt_bias,
    decay_rate,
    conv_x_weight,
    conv_x_bias,
    conv_bc_weight,
    conv_bc_bias,
    norm_gain,
    out_weight,
    conv_x_state,
    conv_bc_state,
    ssm_state,
    sink_x,
    sink_b,
    page_x,
    page_b,
    page_decay,
    slot_req,
    slot_page,
    page_count,
    accepted,
    owner_row,
):
    inner = x_weight.shape[1]
    ns = bc_weight.shape[1] // 2
    slots, page, _ = page_x.shape
    heads = dt_weight.shape[1]
    ocols = out_weight.shape[1]
    pad_in = -(-inner // LN) * LN
    Y = R // X
    shape = jax.ShapeDtypeStruct
    operands = (
        drafts,
        x_weight,
        z_weight,
        bc_weight,
        dt_weight.T,
        dt_bias,
        decay_rate,
        conv_x_weight,
        conv_x_bias,
        conv_bc_weight,
        conv_bc_bias,
        norm_gain,
        out_weight.T,
        conv_x_state,
        conv_bc_state,
        ssm_state,
        sink_x,
        sink_b,
        jnp.swapaxes(page_x, 1, 2),
        page_b,
        page_decay,
        slot_req,
        slot_page,
        page_count,
        accepted.reshape(1, 1),
        owner_row,
    )
    out_shapes = (
        shape((1, T, 2 * ocols), bf16),
        shape(ssm_state.shape, f32),
        shape(conv_x_state.shape, bf16),
        shape(conv_bc_state.shape, bf16),
    )
    held = [
        (pltpu.SMEM if name in SCALARS else pltpu.VMEM)(a.shape, a.dtype)
        for name, a in zip(NAMES, operands)
    ]
    scratch = held + [
        pltpu.VMEM((T, LN), f32),
        pltpu.VMEM((3 * T, R * LN), bf16),
        pltpu.VMEM((T, LN), bf16),
        pltpu.VMEM((T, R * LN), bf16),
        pltpu.VMEM((Y * T, X * LN), bf16),
        pltpu.VMEM((X * LN, 2 * inner), bf16),
        pltpu.VMEM((Y * T, 2 * inner), bf16),
        pltpu.VMEM((Y, T, 2 * inner), bf16),
        pltpu.VMEM((T, LN), bf16),
        pltpu.VMEM((F * T, LN), bf16),
        pltpu.VMEM((8, LN), f32),
        pltpu.VMEM((2 * T, 2 * ns), f32),
        pltpu.VMEM((CROWS, LN), bf16),
        pltpu.VMEM((R, CROWS, LN), bf16),
        pltpu.VMEM((slots, inner, ns), bf16),
        pltpu.VMEM((slots, 1, LN), f32),
        pltpu.VMEM((slots * T, ns), bf16),
        pltpu.VMEM((slots * T, LN), f32),
        pltpu.VMEM((heads * T, page), bf16),
        pltpu.VMEM((R, 8, 4 * HD), bf16),
        pltpu.VMEM((R, 8, 4 * HD), bf16),
        pltpu.VMEM((R, 8, 2 * inner - 4 * HD), bf16),
        pltpu.VMEM((R, 8, 2 * inner - 4 * HD), bf16),
        pltpu.VMEM((2 * T, inner), f32),
        pltpu.VMEM((2 * T, inner), f32),
        pltpu.VMEM((2 * T, ns), f32),
        pltpu.VMEM((T, pad_in), bf16),
        pltpu.VMEM((Y * T, pad_in), bf16),
        pltpu.VMEM((X * LN, pad_in), bf16),
        pltpu.VMEM((Y * T, X * LN), bf16),
        pltpu.VMEM((F, T, 2 * LN), bf16),
        pltpu.SemaphoreType.DMA((11,)),
        pltpu.SemaphoreType.DMA((11,)),
        *(pltpu.VMEM(a.shape, a.dtype) for a in out_shapes),
        pltpu.SemaphoreType.DMA((26,)),
        pltpu.SemaphoreType.DMA((4,)),
    ]
    results = pl.pallas_call(
        functools.partial(kernel, R, F),
        out_shape=out_shapes,
        in_specs=[pl.BlockSpec(memory_space=pltpu.HBM)] * 26,
        out_specs=(pl.BlockSpec(memory_space=pltpu.HBM),) * 4,
        scratch_shapes=scratch,
        compiler_params=pltpu.CompilerParams(
            collective_id=0, has_side_effects=True
        ),
        name="mixer",
    )(*operands)
    hbm = pl.BlockSpec(memory_space=pltpu.HBM)
    return pl.pallas_call(
        hand_over,
        out_shape=tuple(shape(a.shape, a.dtype) for a in results),
        in_specs=[hbm] * 4,
        out_specs=(hbm,) * 4,
        scratch_shapes=[pltpu.VMEM(a.shape, a.dtype) for a in results]
        + [pltpu.SemaphoreType.DMA((8,))],
        name="hand_over",
    )(*results)


def solution(mesh):
    in_specs = (
        P("req", None, None),
        P("req", "fsdp"),
        P("req", "fsdp"),
        P("req", None),
        P("req", "fsdp"),
        P("fsdp"),
        P("fsdp"),
        P(None, "fsdp"),
        P("fsdp"),
        P(),
        P(),
        P("fsdp"),
        P("fsdp", "req"),
        P("req", None, "fsdp"),
        P("req", None, None),
        P("req", "fsdp", None, None),
        P("req", None, "fsdp"),
        P("req", None, None),
        P("req", None, "fsdp"),
        P("req", None, None),
        P("req", "fsdp", None),
        P("req"),
        P("req"),
        P(),
        P("req"),
        P(),
    )
    out_specs = (
        P("req", None, "fsdp"),
        P("req", "fsdp", None, None),
        P("req", None, "fsdp"),
        P("req", None, None),
    )
    return jax.shard_map(
        functools.partial(per_device, mesh.shape["req"], mesh.shape["fsdp"]),
        mesh=mesh,
        in_specs=in_specs,
        out_specs=out_specs,
        check_vma=False,
    )
```

```python
import functools

import jax
import jax.numpy as jnp
from jax import lax
from jax.experimental import pallas as pl
from jax.experimental.pallas import tpu as pltpu
from jax.sharding import PartitionSpec as P

MESH = pl.DeviceIdType.MESH
T = 16
CROWS = 24
X = 4
KC = 4
HD = 64
LN = 128
EPSILON = 1e-05
f32 = jnp.float32
bf16 = jnp.bfloat16
EXACT = lax.Precision.HIGHEST
NAMES = (
    "drafts",
    "xw",
    "zw",
    "bcw",
    "dtw",
    "dt_bias",
    "decay",
    "cxw",
    "cxb",
    "cbw",
    "cbb",
    "gain",
    "ow",
    "cxs",
    "cbs",
    "ssm",
    "sink_x",
    "sink_b",
    "page_x",
    "page_b",
    "page_decay",
    "slot_req",
    "slot_page",
    "page_count",
    "accepted",
    "owner_row",
)
SCALARS = ("slot_req", "slot_page", "page_count", "owner_row")
FIRST = ("bcw", "dtw")
SECOND = ("drafts", "xw", "zw", "ow")
OTHERS = tuple(n for n in NAMES if n not in FIRST + SECOND)


def nt(a, b, precision=None):
    return lax.dot_general(
        a, b, (((1,), (1,)), ((), ())), preferred_element_type=f32, precision=precision
    )


def iota(shape, axis):
    return lax.broadcasted_iota(jnp.int32, shape, axis)


def silu(v):
    return v * jax.nn.sigmoid(v)


def far_first(k, n):
    return n // 2 + jnp.where(lax.rem(k, 2) == 1, -lax.div(k + 1, 2), lax.div(k, 2))


def sum_blocks(ref):
    n = ref.shape[0]
    group = min(8, n)
    total = None
    for i in range(0, n, group):
        part = ref[i].astype(f32)
        for j in range(i + 1, i + group):
            part = part + ref[j].astype(f32)
        total = part if total is None else total + part
    return total


def pieces3(v):
    hi = v.astype(bf16).astype(f32)
    rest = v - hi
    mid = rest.astype(bf16).astype(f32)
    low = (rest - mid).astype(bf16).astype(f32)
    return hi, mid, low


def kernel(R, F, *refs):
    sources, outs, held, rest = refs[:26], refs[26:30], refs[30:56], refs[56:-6]
    ready, load_sem, store_sem = refs[-6:-2], refs[-2], refs[-1]
    stores = [
        pltpu.make_async_copy(source, target, store_sem.at[i])
        for i, (source, target) in enumerate(zip(ready, outs))
    ]
    copies = [
        pltpu.make_async_copy(source, target, load_sem.at[i])
        for i, (source, target) in enumerate(zip(sources, held))
    ]

    def load(*names):
        for name in names:
            copies[NAMES.index(name)].start()

    def arrive(*names):
        for name in names:
            copies[NAMES.index(name)].wait()

    body(R, F, load, arrive, stores, *held, *ready, *rest)
    for store in stores:
        store.wait()


def body(
    R,
    F,
    load,
    arrive,
    stores,
    drafts_ref,
    xw_ref,
    zw_ref,
    bcw_ref,
    dtw_ref,
    dt_bias_ref,
    decay_ref,
    cxw_ref,
    cxb_ref,
    cbw_ref,
    cbb_ref,
    gain_ref,
    ow_ref,
    cxs_ref,
    cbs_ref,
    ssm_ref,
    sink_x_ref,
    sink_b_ref,
    page_x_ref,
    page_b_ref,
    page_decay_ref,
    slot_req_ref,
    slot_page_ref,
    page_count_ref,
    accepted_ref,
    owner_row_ref,
    mixed_ref,
    state_ref,
    ncx_ref,
    ncb_ref,
    dt_buf,
    a_buf,
    w_own,
    w_all,
    d_all,
    wxz,
    xz_send,
    xz_recv,
    z_own,
    z_all,
    head_buf,
    s_bc,
    cc_own,
    cc_all,
    state_buf,
    least_buf,
    w5,
    pa_send,
    pa_recv,
    pb_send,
    pb_recv,
    s_x,
    xs_buf,
    bs_buf,
    g_own,
    g_all,
    w_ext,
    f_send,
    f_recv,
    send_sem,
    recv_sem,
):
    me = lax.axis_index("req")
    mf = lax.axis_index("fsdp")
    ks, inner = xw_ref.shape
    half = ks // 2
    heads = dtw_ref.shape[0]
    ns = bcw_ref.shape[1] // 2
    slots = page_x_ref.shape[0]
    total_inner = inner * F
    ocols = ow_ref.shape[0]
    pad_in = g_own.shape[1]
    Y = R // X
    per_row = X // 2
    my = lax.div(me, X)
    mx = lax.rem(me, X)
    is_self = lax.div(mf, per_row) == my
    source = lax.div(mf, per_row) * X + mx
    Z = F // 2

    def req_peer(i):
        yy = lax.rem(my + far_first(lax.div(i, X), Y), Y)
        return yy * X + lax.rem(mx + far_first(lax.rem(i, X), X), X)

    def y_peer(i):
        return lax.rem(my + far_first(i, Y), Y)

    def f_peer(i):
        zz = lax.rem(lax.div(mf, 2) + far_first(lax.div(i, 2), Z), Z)
        return zz * 2 + lax.rem(mf + 1 + i, 2)


    load(*FIRST)
    barrier = pltpu.get_barrier_semaphore()

    @pl.loop(0, R - 1)
    def _(i):
        pl.semaphore_signal(
            barrier, inc=1, device_id={"req": req_peer(i)}, device_id_type=MESH
        )

    @pl.loop(0, F - 1)
    def _(i):
        pl.semaphore_signal(barrier, inc=1, device_id={"fsdp": f_peer(i)}, device_id_type=MESH)


    @pl.loop(0, F)
    def _(i):
        g = f_peer(i)

        @pl.when(jnp.logical_or(g != mf, source != me))
        def _():
            pl.semaphore_signal(
                barrier, inc=1, device_id={"req": source, "fsdp": g}, device_id_type=MESH
            )

    load(*SECOND)
    arrive("bcw", "dtw")
    wpad = jnp.concatenate([bcw_ref[...], jnp.zeros((LN - ks, 2 * ns), bf16)], axis=0)
    pick = (iota((T, 2 * ns), 1) == T * mf + iota((T, 2 * ns), 0)).astype(bf16)
    bc_rows = nt(pick, wpad)
    row = iota((T, LN), 0)
    lane = iota((T, LN), 1)
    dt_buf[...] = jnp.zeros(dt_buf.shape, f32)
    dt_buf[pl.ds(0, heads), pl.ds(0, ks)] = dtw_ref[...].astype(f32)
    dt_buf[pl.ds(heads, heads), pl.ds(0, ks)] = dtw_ref[...].astype(f32)
    dt_rows = dt_buf[...]
    dt_rows = jnp.where(
        row < heads, pltpu.roll(dt_rows, ks, 1), pltpu.roll(dt_rows, half, 1)
    )
    dt_zone = (lane >= ks) & (lane < ks + half)
    w_own[...] = jnp.where(
        lane < ks, bc_rows, jnp.where(dt_zone & (row < 2 * heads), dt_rows, 0.0)
    ).astype(bf16)
    w_all[:, pl.ds(pl.multiple_of(me * LN, LN), LN)] = w_own[...]

    own_rows = pl.ds(pl.multiple_of(me * T, T), T)
    y_rows = pl.ds(pl.multiple_of(my * T, T), T)
    pl.semaphore_wait(
        barrier, (R - 1) + (F - 1) + Y * per_row - is_self.astype(jnp.int32)
    )

    def put(src, dst, phase, device):
        pltpu.make_async_remote_copy(
            src_ref=src,
            dst_ref=dst,
            send_sem=send_sem.at[phase],
            recv_sem=recv_sem.at[phase],
            device_id=device,
            device_id_type=MESH,
        ).start()

    def wait_bytes(ref, sem):
        pltpu.make_async_copy(ref, ref, sem).wait()

    own_lanes = pl.ds(pl.multiple_of(me * LN, LN), LN)
    w_bytes = wxz.at[pl.ds(0, (X - 1) * ks), :]
    o_bytes = w_ext.at[pl.ds(0, (X - 1) * ocols), :]

    @pl.loop(0, R - 1)
    def _(i):
        put(w_own, w_all.at[:, own_lanes], 0, {"req": req_peer(i)})

    load(*OTHERS)

    own_block = pl.ds(pl.multiple_of(mx * LN, LN), ks)
    own_outs = pl.ds(
        pl.multiple_of(lax.div(mx, 2) * 2 * LN + lax.rem(mx, 2) * ocols, 16), ocols
    )
    tail = pad_in - inner
    for i in range(X):
        wxz[pl.ds(LN * i + ks, LN - ks), :] = jnp.zeros((LN - ks, 2 * inner), bf16)
    arrive("xw", "zw")
    wxz[own_block, pl.ds(0, inner)] = xw_ref[...]
    wxz[own_block, pl.ds(inner, inner)] = zw_ref[...]
    arrive("ow")
    w_ext[own_outs, pl.ds(0, inner)] = ow_ref[...]
    w_ext[own_outs, pl.ds(inner, tail)] = jnp.zeros((ocols, tail), bf16)
    rest = 2 * LN - 2 * ocols
    er = iota((rest, tail), 0)
    el = iota((rest, tail), 1)
    for i in range(per_row):
        top = pl.ds(2 * LN * i + 2 * ocols, rest)
        w_ext[top, pl.ds(0, inner)] = jnp.zeros((rest, inner), bf16)
        w_ext[top, pl.ds(inner, tail)] = ((er == el) & (el < 3)).astype(bf16)

    @pl.loop(1, X)
    def _(i):
        r = my * X + lax.rem(mx + i, X)
        put(wxz.at[own_block, :], wxz.at[own_block, :], 8, {"req": r})

    arrive("drafts")
    z_own[...] = jnp.zeros(z_own.shape, bf16)
    for j in range(R):
        start = ks * j
        base = start // LN * LN
        off = start - base
        if off + ks <= LN:
            window = drafts_ref[0, :, pl.ds(base, LN)].astype(f32)
            if off:
                window = pltpu.roll(window, LN - off, 1)
        else:
            window = drafts_ref[0, :, pl.ds(base, 2 * LN)].astype(f32)
            window = pltpu.roll(window, 2 * LN - off, 1)[:, :LN]
        a_buf[pl.ds(0, T), pl.ds(LN * j, LN)] = jnp.where(lane < ks, window, 0.0).astype(bf16)
        a_buf[pl.ds(T, T), pl.ds(LN * j, LN)] = jnp.where(
            dt_zone, pltpu.roll(window, ks, 1), 0.0
        ).astype(bf16)
        a_buf[pl.ds(2 * T, T), pl.ds(LN * j, LN)] = jnp.where(
            dt_zone, pltpu.roll(window, half, 1), 0.0
        ).astype(bf16)
    d_all[y_rows, :] = a_buf[pl.ds(0, T), pl.ds(pl.multiple_of(my * X * LN, X * LN), X * LN)]

    @pl.loop(0, Y - 1)
    def _(i):
        yy = y_peer(i)
        put(
            a_buf.at[pl.ds(0, T), pl.ds(pl.multiple_of(yy * X * LN, X * LN), X * LN)],
            d_all.at[y_rows, :],
            1,
            {"req": yy * X + mx},
        )

    @pl.loop(1, X)
    def _(i):
        r = my * X + lax.rem(mx + i, X)
        put(w_ext.at[own_outs, :], w_ext.at[own_outs, :], 9, {"req": r})

    arrive("dt_bias", "decay", "cbs", "cxs", "sink_b", "sink_x")
    head_buf[...] = jnp.zeros(head_buf.shape, f32)
    head_buf[pl.ds(0, 1), pl.ds(0, heads)] = dt_bias_ref[...].reshape(1, heads)
    head_buf[pl.ds(1, 1), pl.ds(0, heads)] = decay_ref[...].reshape(1, heads)
    s_bc[...] = jnp.zeros(s_bc.shape, f32)
    s_bc[pl.ds(T - KC + 1, KC - 1), :] = cbs_ref[0].astype(f32)
    s_x[...] = jnp.zeros(s_x.shape, f32)
    s_x[pl.ds(T - KC + 1, KC - 1), :] = cxs_ref[0].astype(f32)
    bs_buf[...] = jnp.zeros(bs_buf.shape, f32)
    bs_buf[pl.ds(T, 4), :] = sink_b_ref[0].astype(f32)
    xs_buf[...] = jnp.zeros(xs_buf.shape, f32)
    xs_buf[pl.ds(T, 4), :] = sink_x_ref[0].astype(f32)
    arrive("cbb", "cbw", "cxb", "cxw", "gain", "ssm", "page_x", "page_b", "page_decay")

    wait_bytes(w_all.at[:, pl.ds(0, (R - 1) * LN)], recv_sem.at[0])
    z_own[:, pl.ds(0, 3 * T)] = nt(w_all[...], a_buf[...]).astype(bf16)
    z_rows = pl.ds(pl.multiple_of(mf * T, T), T)
    z_all[z_rows, :] = z_own[...]

    @pl.loop(0, F - 1)
    def _(i):
        put(z_own, z_all.at[z_rows, :], 2, {"fsdp": f_peer(i)})

    wait_bytes(d_all.at[pl.ds(0, (Y - 1) * T), :], recv_sem.at[1])
    wait_bytes(w_bytes, recv_sem.at[8])
    xz_send[...] = jnp.dot(d_all[...], wxz[...], preferred_element_type=f32).astype(bf16)
    xz_recv[my] = xz_send[y_rows, :]

    @pl.loop(0, Y - 1)
    def _(i):
        yy = y_peer(i)
        put(
            xz_send.at[pl.ds(pl.multiple_of(yy * T, T), T), :],
            xz_recv.at[my],
            4,
            {"req": yy * X + mx},
        )

    er = iota((T, LN), 0)
    el = iota((T, LN), 1)
    proj = nt(a_buf[pl.ds(T, 2 * T), :], w_all[...])
    first = ((er == el) & (el < heads)).astype(f32)
    second = ((er == el + heads) & (el < heads)).astype(f32)
    dt_raw = jnp.dot(proj[:T], first, precision=EXACT, preferred_element_type=f32) + jnp.dot(
        proj[T:], second, precision=EXACT, preferred_element_type=f32
    )
    v = dt_raw + head_buf[pl.ds(0, 1), :]
    dtime = jnp.maximum(v, 0.0) + jnp.log1p(jnp.exp(-jnp.abs(v)))
    upto = (iota((T, T), 1) <= iota((T, T), 0)).astype(f32)
    cumul = -jnp.dot(
        upto, dtime * head_buf[pl.ds(1, 1), :], precision=EXACT, preferred_element_type=f32
    )
    hi, mid, low = pieces3(cumul)
    packed = hi + pltpu.roll(mid, 5, 1) + pltpu.roll(low, 10, 1)
    for step in (16, 32, 64):
        packed = packed + pltpu.roll(packed, step, 1)
    packed = jnp.where(lax.div(el, T) == lax.rem(er, 8), packed, 0.0)
    packed_low = jnp.sum(jnp.where(er < 8, packed, 0.0), axis=0, keepdims=True)
    packed_high = jnp.sum(jnp.where(er >= 8, packed, 0.0), axis=0, keepdims=True)
    row8 = iota((8, LN), 0)
    packed = jnp.where(row8 == 0, packed_low, jnp.where(row8 == 1, packed_high, 0.0))

    wait_bytes(z_all.at[pl.ds(0, (F - 1) * T), :], recv_sem.at[2])
    bc_raw = nt((iota((T, LN), 0) == iota((T, LN), 1)).astype(bf16), z_all[...])
    s_bc[pl.ds(T, T), :] = bc_raw
    acc = jnp.zeros((T, 2 * ns), f32) + cbb_ref[...].astype(f32).reshape(1, 2 * ns)
    for k in range(KC):
        acc = acc + cbw_ref[pl.ds(k, 1), :].astype(f32) * s_bc[pl.ds(T - KC + 1 + k, T), :]
    bc_act = silu(acc)
    b_mat = bc_act[:, :ns].astype(bf16)
    c_mat = bc_act[:, ns:].astype(bf16)
    if ns < LN:
        cc_own[...] = jnp.zeros(cc_own.shape, bf16)
    cc_own[pl.ds(0, T), pl.ds(0, ns)] = c_mat
    cc_own[pl.ds(T, 8), :] = packed.astype(bf16)
    cc_all[me] = cc_own[...]

    @pl.loop(0, R - 1)
    def _(i):
        put(cc_own, cc_all.at[me], 3, {"req": req_peer(i)})

    eye_h = iota((heads, LN), 0) == iota((heads, LN), 1)

    @pl.loop(0, slots)
    def _(s):
        decays = page_decay_ref[s]
        least = jnp.min(decays, axis=1, keepdims=True)
        least_buf[s] = jnp.sum(jnp.where(eye_h, least, 0.0), axis=0, keepdims=True)
        factor = jnp.exp(least - decays)
        for h in range(heads):
            rows = pl.ds(h * HD, HD)
            faded = page_x_ref[s, rows, :].astype(f32) * factor[h : h + 1, :]
            state_buf[s, rows, :] = jnp.dot(
                faded.astype(bf16), page_b_ref[s], preferred_element_type=f32
            ).astype(bf16)


    arrive("slot_req", "slot_page", "page_count", "owner_row", "accepted")
    rows_of = []
    live_of = []
    for s in range(slots):
        req = slot_req_ref[s]
        guarded = jnp.maximum(req, 0)
        live_of.append((req >= 0) & (slot_page_ref[s] < page_count_ref[guarded]))
        rows_of.append(owner_row_ref[guarded])
    by_lane = jnp.zeros((1, slots * T), jnp.int32)
    live_sub = jnp.zeros((slots * T, 1), jnp.int32)
    for s in range(slots):
        in_sub = lax.div(iota((slots * T, 1), 0), T) == s
        in_lane = lax.div(iota((1, slots * T), 1), T) == s
        live_sub = jnp.where(in_sub, live_of[s].astype(jnp.int32), live_sub)
        by_lane = jnp.where(
            in_lane, jnp.where(live_of[s], rows_of[s], -(1 << 20)), by_lane
        )
    at = lax.rem(iota((1, slots * T), 1), T)
    tall_sub = iota((R * 8, slots * T), 0)
    scatter_low = ((tall_sub == 8 * by_lane + at) & (at < 8)).astype(bf16)
    scatter_high = ((tall_sub == 8 * by_lane + at - 8) & (at >= 8)).astype(bf16)

    head_lane = lax.div(iota((T, inner), 1), HD)

    def own_heads(stacked):
        out = jnp.where(head_lane == 0, stacked[0:T], 0.0)
        for h in range(1, heads):
            out = jnp.where(head_lane == h, stacked[h * T : (h + 1) * T], out)
        return out

    wait_bytes(cc_all.at[pl.ds(0, R - 1)], recv_sem.at[3])
    group = lax.div(lane, T) == lax.rem(row, 8)
    queries = []
    fades = []
    for s in range(slots):
        block = cc_all[rows_of[s]]
        queries.append(block[:T, :ns])
        folded = block[T:].astype(f32)
        folded = jnp.where(group, jnp.where(row < 8, folded[0:1], folded[1:2]), 0.0)
        for step in (64, 32, 16):
            folded = folded + pltpu.roll(folded, step, 1)
        cum = folded + pltpu.roll(folded, LN - 5, 1) + pltpu.roll(folded, LN - 10, 1)
        fades.append(jnp.exp(cum - least_buf[s]))

    cut = 2 * HD
    for first_head, send, recv, phase in ((0, pa_send, pa_recv, 5), (2, pb_send, pb_recv, 10)):
        lanes = cut if first_head == 0 else inner - cut
        part = pl.ds(first_head * HD, lanes)
        lane_head = lax.div(iota((T, lanes), 1), HD) + first_head
        chosen = []
        for s in range(slots):
            factor = fades[s]
            spread = jnp.zeros((T, lanes), f32)
            for h in range(first_head, first_head + lanes // HD):
                spread = jnp.where(lane_head == h, factor[:, h : h + 1], spread)
            chosen.append(nt(queries[s], state_buf[s, part, :]) * spread)
        kept = jnp.where(live_sub != 0, jnp.concatenate(chosen, axis=0), 0.0).astype(bf16)
        low = jnp.dot(scatter_low, kept, preferred_element_type=f32)
        high = jnp.dot(scatter_high, kept, preferred_element_type=f32)
        send[:, :, pl.ds(0, lanes)] = low.astype(bf16).reshape(R, 8, lanes)
        send[:, :, pl.ds(lanes, lanes)] = high.astype(bf16).reshape(R, 8, lanes)
        recv[me] = send[me]

        @pl.loop(0, R - 1)
        def _(i, send=send, recv=recv, phase=phase):
            r = req_peer(i)
            put(send.at[r], recv.at[me], phase, {"req": r})

    wait_bytes(xz_recv.at[pl.ds(0, Y - 1)], recv_sem.at[4])
    xz = sum_blocks(xz_recv)
    x_raw = xz[:, :inner].astype(bf16).astype(f32)
    z_raw = xz[:, inner:].astype(bf16).astype(f32)
    s_x[pl.ds(T, T), :] = x_raw
    acc = jnp.zeros((T, inner), f32) + cxb_ref[...].astype(f32).reshape(1, inner)
    for k in range(KC):
        acc = acc + cxw_ref[pl.ds(k, 1), :].astype(f32) * s_x[pl.ds(T - KC + 1 + k, T), :]
    x_act = silu(acc).astype(bf16).astype(f32)
    xs_buf[pl.ds(0, T), :] = x_act
    bs_buf[pl.ds(0, T), :] = b_mat.astype(f32)
    scores = nt(c_mat, bs_buf[...].astype(bf16))
    zeros_t = jnp.zeros((T, LN), f32)
    eye8 = (iota((8, LN), 0) == iota((8, LN), 1)).astype(f32)
    cumul_t = nt(eye8, jnp.concatenate([cumul, zeros_t], axis=0), EXACT)
    dtime_t = nt(eye8, jnp.concatenate([dtime, zeros_t], axis=0), EXACT)
    at = iota((T, 2 * T), 0)
    au = iota((T, 2 * T), 1)
    for h in range(heads):
        spread = jnp.where(au <= at, cumul[:, h : h + 1] - cumul_t[h : h + 1, :], 0.0)
        factor = jnp.exp(spread) * dtime_t[h : h + 1, :]
        factor = jnp.where(au >= T, 1.0, jnp.where(au <= at, factor, 0.0))
        w5[pl.ds(h * T, T), pl.ds(0, 2 * T)] = (scores * factor).astype(bf16)
    local = own_heads(
        jnp.dot(
            w5[:, pl.ds(0, 2 * T)], xs_buf[...].astype(bf16), preferred_element_type=f32
        )
    )

    taken = accepted_ref[...]
    at = iota((T, LN), 0)
    last = jnp.sum(jnp.where(at == taken - 1, cumul, 0.0), axis=0, keepdims=True)
    spread = jnp.where(at < taken, last - cumul, 0.0)
    coeff = jnp.where(at < taken, jnp.exp(spread) * dtime, 0.0)
    coeff_x = jnp.zeros((T, inner), f32)
    for h in range(heads):
        coeff_x = jnp.where(head_lane == h, coeff[:, h : h + 1], coeff_x)
    y = coeff_x * x_act
    y_hi = y.astype(bf16).astype(f32)
    y2 = jnp.concatenate([y_hi, y - y_hi], axis=0).astype(bf16)
    b2 = jnp.concatenate([b_mat, b_mat], axis=0)
    fresh = lax.dot_general(
        y2, b2, (((0,), (0,)), ((), ())), preferred_element_type=f32
    )
    keep = jnp.exp(last)
    for h in range(heads):
        state_ref[0, h] = keep[:, h : h + 1] * ssm_ref[0, h] + fresh[h * HD : (h + 1) * HD]
    tail_pick = (
        iota((8, 2 * T), 1) == T - KC + 1 + taken + iota((8, 2 * T), 0)
    ).astype(bf16)
    ncx = jnp.dot(tail_pick, s_x[...].astype(bf16), preferred_element_type=f32)
    ncx_ref[0] = ncx[: KC - 1].astype(bf16)
    ncb = jnp.dot(tail_pick, s_bc[...].astype(bf16), preferred_element_type=f32)
    ncb_ref[0] = ncb[: KC - 1].astype(bf16)
    for store in stores[1:]:
        store.start()
    gate = silu(z_raw)

    parts = []
    for recv, phase in ((pa_recv, 5), (pb_recv, 10)):
        wait_bytes(recv.at[pl.ds(0, R - 1)], recv_sem.at[phase])
        part = sum_blocks(recv)
        lanes = part.shape[1] // 2
        parts.append(jnp.concatenate([part[:, :lanes], part[:, lanes:]], axis=0))
    page_sum = jnp.concatenate(parts, axis=1)
    gated = (page_sum + local) * gate
    squares = jnp.sum(gated * gated, axis=1, keepdims=True)
    hi, mid, low = pieces3(squares)
    el = iota((T, tail), 1)
    g_own[:, pl.ds(0, inner)] = (gated * gain_ref[...].astype(f32).reshape(1, inner)).astype(bf16)
    g_own[:, pl.ds(inner, tail)] = jnp.where(
        el == 0, hi, jnp.where(el == 1, mid, jnp.where(el == 2, low, 0.0))
    ).astype(bf16)
    g_all[y_rows, :] = g_own[...]

    @pl.loop(0, Y - 1)
    def _(i):
        put(g_own, g_all.at[y_rows, :], 6, {"req": y_peer(i) * X + mx})

    wait_bytes(o_bytes, recv_sem.at[9])
    wait_bytes(g_all.at[pl.ds(0, (Y - 1) * T), :], recv_sem.at[6])
    f_send[...] = nt(g_all[...], w_ext[...]).astype(bf16)

    for b in range(per_row):
        lanes = pl.ds(2 * LN * b, 2 * LN)
        target = per_row * my + b

        @pl.when(target == mf)
        def _():
            f_recv[mf] = f_send[y_rows, lanes]

        @pl.when(target != mf)
        def _():
            put(f_send.at[y_rows, lanes], f_recv.at[mf], 7, {"fsdp": target})

        @pl.loop(0, Y - 1)
        def _(i):
            yy = y_peer(i)
            put(
                f_send.at[pl.ds(pl.multiple_of(yy * T, T), T), lanes],
                f_recv.at[mf],
                7,
                {"req": yy * X + mx, "fsdp": target},
            )

    @pl.when(is_self)
    def _():
        wait_bytes(f_recv.at[pl.ds(0, F - 1)], recv_sem.at[7])

    @pl.when(jnp.logical_not(is_self))
    def _():
        wait_bytes(f_recv, recv_sem.at[7])

    out = sum_blocks(f_recv)
    wide = 2 * ocols
    total_squares = (
        out[:, wide : wide + 1] + out[:, wide + 1 : wide + 2] + out[:, wide + 2 : wide + 3]
    )
    scale = lax.rsqrt(total_squares / total_inner + EPSILON)
    mixed_ref[0] = (out * scale)[:, :wide].astype(bf16)
    stores[0].start()

    wait_bytes(w_all.at[:, pl.ds(0, (R - 1) * LN)], send_sem.at[0])
    wait_bytes(d_all.at[pl.ds(0, (Y - 1) * T), :], send_sem.at[1])
    wait_bytes(z_all.at[pl.ds(0, (F - 1) * T), :], send_sem.at[2])
    wait_bytes(cc_all.at[pl.ds(0, R - 1)], send_sem.at[3])
    wait_bytes(xz_recv.at[pl.ds(0, Y - 1)], send_sem.at[4])
    wait_bytes(w_bytes, send_sem.at[8])
    wait_bytes(o_bytes, send_sem.at[9])
    wait_bytes(pa_recv.at[pl.ds(0, R - 1)], send_sem.at[5])
    wait_bytes(pb_recv.at[pl.ds(0, R - 1)], send_sem.at[10])
    wait_bytes(g_all.at[pl.ds(0, (Y - 1) * T), :], send_sem.at[6])

    @pl.when(is_self)
    def _():
        wait_bytes(f_recv.at[pl.ds(0, F - 1)], send_sem.at[7])

    @pl.when(jnp.logical_not(is_self))
    def _():
        wait_bytes(f_recv, send_sem.at[7])


def hand_over(*refs):
    held, sem = refs[8:12], refs[12]
    reads = [pltpu.make_async_copy(refs[i], held[i], sem.at[i]) for i in range(4)]
    writes = [pltpu.make_async_copy(held[i], refs[4 + i], sem.at[4 + i]) for i in range(4)]
    for read in reads:
        read.start()
    for read, write in zip(reads, writes):
        read.wait()
        write.start()
    for write in writes:
        write.wait()


def per_device(
    R,
    F,
    drafts,
    x_weight,
    z_weight,
    bc_weight,
    dt_weight,
    dt_bias,
    decay_rate,
    conv_x_weight,
    conv_x_bias,
    conv_bc_weight,
    conv_bc_bias,
    norm_gain,
    out_weight,
    conv_x_state,
    conv_bc_state,
    ssm_state,
    sink_x,
    sink_b,
    page_x,
    page_b,
    page_decay,
    slot_req,
    slot_page,
    page_count,
    accepted,
    owner_row,
):
    inner = x_weight.shape[1]
    ns = bc_weight.shape[1] // 2
    slots, page, _ = page_x.shape
    heads = dt_weight.shape[1]
    ocols = out_weight.shape[1]
    pad_in = -(-inner // LN) * LN
    Y = R // X
    shape = jax.ShapeDtypeStruct
    operands = (
        drafts,
        x_weight,
        z_weight,
        bc_weight,
        dt_weight.T,
        dt_bias,
        decay_rate,
        conv_x_weight,
        conv_x_bias,
        conv_bc_weight,
        conv_bc_bias,
        norm_gain,
        out_weight.T,
        conv_x_state,
        conv_bc_state,
        ssm_state,
        sink_x,
        sink_b,
        jnp.swapaxes(page_x, 1, 2),
        page_b,
        page_decay,
        slot_req,
        slot_page,
        page_count,
        accepted.reshape(1, 1),
        owner_row,
    )
    out_shapes = (
        shape((1, T, 2 * ocols), bf16),
        shape(ssm_state.shape, f32),
        shape(conv_x_state.shape, bf16),
        shape(conv_bc_state.shape, bf16),
    )
    held = [
        (pltpu.SMEM if name in SCALARS else pltpu.VMEM)(a.shape, a.dtype)
        for name, a in zip(NAMES, operands)
    ]
    scratch = held + [
        pltpu.VMEM((T, LN), f32),
        pltpu.VMEM((3 * T, R * LN), bf16),
        pltpu.VMEM((T, LN), bf16),
        pltpu.VMEM((T, R * LN), bf16),
        pltpu.VMEM((Y * T, X * LN), bf16),
        pltpu.VMEM((X * LN, 2 * inner), bf16),
        pltpu.VMEM((Y * T, 2 * inner), bf16),
        pltpu.VMEM((Y, T, 2 * inner), bf16),
        pltpu.VMEM((T, LN), bf16),
        pltpu.VMEM((F * T, LN), bf16),
        pltpu.VMEM((8, LN), f32),
        pltpu.VMEM((2 * T, 2 * ns), f32),
        pltpu.VMEM((CROWS, LN), bf16),
        pltpu.VMEM((R, CROWS, LN), bf16),
        pltpu.VMEM((slots, inner, ns), bf16),
        pltpu.VMEM((slots, 1, LN), f32),
        pltpu.VMEM((heads * T, page), bf16),
        pltpu.VMEM((R, 8, 4 * HD), bf16),
        pltpu.VMEM((R, 8, 4 * HD), bf16),
        pltpu.VMEM((R, 8, 2 * inner - 4 * HD), bf16),
        pltpu.VMEM((R, 8, 2 * inner - 4 * HD), bf16),
        pltpu.VMEM((2 * T, inner), f32),
        pltpu.VMEM((2 * T, inner), f32),
        pltpu.VMEM((2 * T, ns), f32),
        pltpu.VMEM((T, pad_in), bf16),
        pltpu.VMEM((Y * T, pad_in), bf16),
        pltpu.VMEM((X * LN, pad_in), bf16),
        pltpu.VMEM((Y * T, X * LN), bf16),
        pltpu.VMEM((F, T, 2 * LN), bf16),
        pltpu.SemaphoreType.DMA((11,)),
        pltpu.SemaphoreType.DMA((11,)),
        *(pltpu.VMEM(a.shape, a.dtype) for a in out_shapes),
        pltpu.SemaphoreType.DMA((26,)),
        pltpu.SemaphoreType.DMA((4,)),
    ]
    results = pl.pallas_call(
        functools.partial(kernel, R, F),
        out_shape=out_shapes,
        in_specs=[pl.BlockSpec(memory_space=pltpu.HBM)] * 26,
        out_specs=(pl.BlockSpec(memory_space=pltpu.HBM),) * 4,
        scratch_shapes=scratch,
        compiler_params=pltpu.CompilerParams(
            collective_id=0, has_side_effects=True
        ),
        name="mixer",
    )(*operands)
    hbm = pl.BlockSpec(memory_space=pltpu.HBM)
    return pl.pallas_call(
        hand_over,
        out_shape=tuple(shape(a.shape, a.dtype) for a in results),
        in_specs=[hbm] * 4,
        out_specs=(hbm,) * 4,
        scratch_shapes=[pltpu.VMEM(a.shape, a.dtype) for a in results]
        + [pltpu.SemaphoreType.DMA((8,))],
        name="hand_over",
    )(*results)


def solution(mesh):
    in_specs = (
        P("req", None, None),
        P("req", "fsdp"),
        P("req", "fsdp"),
        P("req", None),
        P("req", "fsdp"),
        P("fsdp"),
        P("fsdp"),
        P(None, "fsdp"),
        P("fsdp"),
        P(),
        P(),
        P("fsdp"),
        P("fsdp", "req"),
        P("req", None, "fsdp"),
        P("req", None, None),
        P("req", "fsdp", None, None),
        P("req", None, "fsdp"),
        P("req", None, None),
        P("req", None, "fsdp"),
        P("req", None, None),
        P("req", "fsdp", None),
        P("req"),
        P("req"),
        P(),
        P("req"),
        P(),
    )
    out_specs = (
        P("req", None, "fsdp"),
        P("req", "fsdp", None, None),
        P("req", None, "fsdp"),
        P("req", None, None),
    )
    return jax.shard_map(
        functools.partial(per_device, mesh.shape["req"], mesh.shape["fsdp"]),
        mesh=mesh,
        in_specs=in_specs,
        out_specs=out_specs,
        check_vma=False,
    )
```

```python
import functools

import jax
import jax.numpy as jnp
from jax import lax
from jax.experimental import pallas as pl
from jax.experimental.pallas import tpu as pltpu
from jax.sharding import PartitionSpec as P

MESH = pl.DeviceIdType.MESH
T = 16
CROWS = 18
X = 4
KC = 4
HD = 64
LN = 128
EPSILON = 1e-05
f32 = jnp.float32
bf16 = jnp.bfloat16
EXACT = lax.Precision.HIGHEST
NAMES = (
    "drafts",
    "xw",
    "zw",
    "bcw",
    "dtw",
    "dt_bias",
    "decay",
    "cxw",
    "cxb",
    "cbw",
    "cbb",
    "gain",
    "ow",
    "cxs",
    "cbs",
    "ssm",
    "sink_x",
    "sink_b",
    "page_x",
    "page_b",
    "page_decay",
    "slot_req",
    "slot_page",
    "page_count",
    "accepted",
    "owner_row",
)
SCALARS = ("slot_req", "slot_page", "page_count", "owner_row")
FIRST = ("bcw", "dtw")
SECOND = ("drafts", "xw", "zw", "ow")
OTHERS = tuple(n for n in NAMES if n not in FIRST + SECOND)


def nt(a, b, precision=None):
    return lax.dot_general(
        a, b, (((1,), (1,)), ((), ())), preferred_element_type=f32, precision=precision
    )


def iota(shape, axis):
    return lax.broadcasted_iota(jnp.int32, shape, axis)


def silu(v):
    return v * jax.nn.sigmoid(v)


def far_first(k, n):
    return n // 2 + jnp.where(lax.rem(k, 2) == 1, -lax.div(k + 1, 2), lax.div(k, 2))


def sum_blocks(ref):
    n = ref.shape[0]
    group = min(8, n)
    total = None
    for i in range(0, n, group):
        part = ref[i].astype(f32)
        for j in range(i + 1, i + group):
            part = part + ref[j].astype(f32)
        total = part if total is None else total + part
    return total


def pieces3(v):
    hi = v.astype(bf16).astype(f32)
    rest = v - hi
    mid = rest.astype(bf16).astype(f32)
    low = (rest - mid).astype(bf16).astype(f32)
    return hi, mid, low


def kernel(R, F, *refs):
    sources, outs, held, rest = refs[:26], refs[26:30], refs[30:56], refs[56:-6]
    ready, load_sem, store_sem = refs[-6:-2], refs[-2], refs[-1]
    stores = [
        pltpu.make_async_copy(source, target, store_sem.at[i])
        for i, (source, target) in enumerate(zip(ready, outs))
    ]
    copies = [
        pltpu.make_async_copy(source, target, load_sem.at[i])
        for i, (source, target) in enumerate(zip(sources, held))
    ]

    def load(*names):
        for name in names:
            copies[NAMES.index(name)].start()

    def arrive(*names):
        for name in names:
            copies[NAMES.index(name)].wait()

    body(R, F, load, arrive, stores, *held, *ready, *rest)
    for store in stores:
        store.wait()


def body(
    R,
    F,
    load,
    arrive,
    stores,
    drafts_ref,
    xw_ref,
    zw_ref,
    bcw_ref,
    dtw_ref,
    dt_bias_ref,
    decay_ref,
    cxw_ref,
    cxb_ref,
    cbw_ref,
    cbb_ref,
    gain_ref,
    ow_ref,
    cxs_ref,
    cbs_ref,
    ssm_ref,
    sink_x_ref,
    sink_b_ref,
    page_x_ref,
    page_b_ref,
    page_decay_ref,
    slot_req_ref,
    slot_page_ref,
    page_count_ref,
    accepted_ref,
    owner_row_ref,
    mixed_ref,
    state_ref,
    ncx_ref,
    ncb_ref,
    dt_buf,
    a_buf,
    w_own,
    w_all,
    d_all,
    wxz,
    xz_send,
    xz_recv,
    z_own,
    z_all,
    head_buf,
    s_bc,
    cc_own,
    cc_all,
    state_buf,
    least_buf,
    w5,
    pa_send,
    pa_recv,
    pb_send,
    pb_recv,
    s_x,
    xs_buf,
    bs_buf,
    g_own,
    g_all,
    w_ext,
    f_send,
    f_recv,
    send_sem,
    recv_sem,
):
    me = lax.axis_index("req")
    mf = lax.axis_index("fsdp")
    ks, inner = xw_ref.shape
    half = ks // 2
    heads = dtw_ref.shape[0]
    ns = bcw_ref.shape[1] // 2
    slots = page_x_ref.shape[0]
    total_inner = inner * F
    ocols = ow_ref.shape[0]
    pad_in = g_own.shape[1]
    Y = R // X
    per_row = X // 2
    my = lax.div(me, X)
    mx = lax.rem(me, X)
    is_self = lax.div(mf, per_row) == my
    source = lax.div(mf, per_row) * X + mx
    Z = F // 2

    def req_peer(i):
        yy = lax.rem(my + far_first(lax.div(i, X), Y), Y)
        return yy * X + lax.rem(mx + far_first(lax.rem(i, X), X), X)

    def y_peer(i):
        return lax.rem(my + far_first(i, Y), Y)

    def f_peer(i):
        zz = lax.rem(lax.div(mf, 2) + far_first(lax.div(i, 2), Z), Z)
        return zz * 2 + lax.rem(mf + 1 + i, 2)


    load(*FIRST)
    barrier = pltpu.get_barrier_semaphore()

    @pl.loop(0, R - 1)
    def _(i):
        pl.semaphore_signal(
            barrier, inc=1, device_id={"req": req_peer(i)}, device_id_type=MESH
        )

    @pl.loop(0, F - 1)
    def _(i):
        pl.semaphore_signal(barrier, inc=1, device_id={"fsdp": f_peer(i)}, device_id_type=MESH)


    load(*SECOND)
    arrive("bcw", "dtw")
    wpad = jnp.concatenate([bcw_ref[...], jnp.zeros((LN - ks, 2 * ns), bf16)], axis=0)
    pick = (iota((T, 2 * ns), 1) == T * mf + iota((T, 2 * ns), 0)).astype(bf16)
    bc_rows = nt(pick, wpad)
    row = iota((T, LN), 0)
    lane = iota((T, LN), 1)
    dt_buf[...] = jnp.zeros(dt_buf.shape, f32)
    dt_buf[pl.ds(0, heads), pl.ds(0, ks)] = dtw_ref[...].astype(f32)
    dt_buf[pl.ds(heads, heads), pl.ds(0, ks)] = dtw_ref[...].astype(f32)
    dt_rows = dt_buf[...]
    dt_rows = jnp.where(
        row < heads, pltpu.roll(dt_rows, ks, 1), pltpu.roll(dt_rows, half, 1)
    )
    dt_zone = (lane >= ks) & (lane < ks + half)
    w_own[...] = jnp.where(
        lane < ks, bc_rows, jnp.where(dt_zone & (row < 2 * heads), dt_rows, 0.0)
    ).astype(bf16)
    w_all[:, pl.ds(pl.multiple_of(me * LN, LN), LN)] = w_own[...]

    own_rows = pl.ds(pl.multiple_of(me * T, T), T)
    y_rows = pl.ds(pl.multiple_of(my * T, T), T)
    pl.semaphore_wait(
        barrier, (R - 1) + (F - 1)
    )

    def put(src, dst, phase, device):
        pltpu.make_async_remote_copy(
            src_ref=src,
            dst_ref=dst,
            send_sem=send_sem.at[phase],
            recv_sem=recv_sem.at[phase],
            device_id=device,
            device_id_type=MESH,
        ).start()

    def wait_bytes(ref, sem):
        pltpu.make_async_copy(ref, ref, sem).wait()

    own_lanes = pl.ds(pl.multiple_of(me * LN, LN), LN)
    w_bytes = wxz.at[pl.ds(0, (X - 1) * ks), :]
    o_bytes = w_ext.at[pl.ds(0, (X - 1) * ocols), :]

    @pl.loop(0, R - 1)
    def _(i):
        put(w_own, w_all.at[:, own_lanes], 0, {"req": req_peer(i)})

    load(*OTHERS)

    own_block = pl.ds(pl.multiple_of(mx * LN, LN), ks)
    own_outs = pl.ds(
        pl.multiple_of(lax.div(mx, 2) * 2 * LN + lax.rem(mx, 2) * ocols, 16), ocols
    )
    tail = pad_in - inner
    for i in range(X):
        wxz[pl.ds(LN * i + ks, LN - ks), :] = jnp.zeros((LN - ks, 2 * inner), bf16)
    arrive("xw", "zw")
    wxz[own_block, pl.ds(0, inner)] = xw_ref[...]
    wxz[own_block, pl.ds(inner, inner)] = zw_ref[...]
    arrive("ow")
    w_ext[own_outs, pl.ds(0, inner)] = ow_ref[...]
    w_ext[own_outs, pl.ds(inner, tail)] = jnp.zeros((ocols, tail), bf16)
    rest = 2 * LN - 2 * ocols
    er = iota((rest, tail), 0)
    el = iota((rest, tail), 1)
    for i in range(per_row):
        top = pl.ds(2 * LN * i + 2 * ocols, rest)
        w_ext[top, pl.ds(0, inner)] = jnp.zeros((rest, inner), bf16)
        w_ext[top, pl.ds(inner, tail)] = ((er == el) & (el < 3)).astype(bf16)

    arrive("drafts")
    z_own[...] = jnp.zeros(z_own.shape, bf16)
    for j in range(R):
        start = ks * j
        base = start // LN * LN
        off = start - base
        if off + ks <= LN:
            window = drafts_ref[0, :, pl.ds(base, LN)].astype(f32)
            if off:
                window = pltpu.roll(window, LN - off, 1)
        else:
            window = drafts_ref[0, :, pl.ds(base, 2 * LN)].astype(f32)
            window = pltpu.roll(window, 2 * LN - off, 1)[:, :LN]
        a_buf[pl.ds(0, T), pl.ds(LN * j, LN)] = jnp.where(lane < ks, window, 0.0).astype(bf16)
        a_buf[pl.ds(T, T), pl.ds(LN * j, LN)] = jnp.where(
            dt_zone, pltpu.roll(window, ks, 1), 0.0
        ).astype(bf16)
        a_buf[pl.ds(2 * T, T), pl.ds(LN * j, LN)] = jnp.where(
            dt_zone, pltpu.roll(window, half, 1), 0.0
        ).astype(bf16)
    d_all[y_rows, :] = a_buf[pl.ds(0, T), pl.ds(pl.multiple_of(my * X * LN, X * LN), X * LN)]

    arrive("dt_bias", "decay", "cbs", "cxs", "sink_b", "sink_x")
    head_buf[...] = jnp.zeros(head_buf.shape, f32)
    head_buf[pl.ds(0, 1), pl.ds(0, heads)] = dt_bias_ref[...].reshape(1, heads)
    head_buf[pl.ds(1, 1), pl.ds(0, heads)] = decay_ref[...].reshape(1, heads)
    s_bc[...] = jnp.zeros(s_bc.shape, f32)
    s_bc[pl.ds(T - KC + 1, KC - 1), :] = cbs_ref[0].astype(f32)
    s_x[...] = jnp.zeros(s_x.shape, f32)
    s_x[pl.ds(T - KC + 1, KC - 1), :] = cxs_ref[0].astype(f32)
    bs_buf[...] = jnp.zeros(bs_buf.shape, f32)
    bs_buf[pl.ds(T, 4), :] = sink_b_ref[0].astype(f32)
    xs_buf[...] = jnp.zeros(xs_buf.shape, f32)
    xs_buf[pl.ds(T, 4), :] = sink_x_ref[0].astype(f32)
    arrive("cbb", "cbw", "cxb", "cxw", "gain", "ssm", "page_x", "page_b", "page_decay")

    wait_bytes(w_all.at[:, pl.ds(0, (R - 1) * LN)], recv_sem.at[0])
    z_own[:, pl.ds(0, 3 * T)] = nt(w_all[...], a_buf[...]).astype(bf16)
    z_rows = pl.ds(pl.multiple_of(mf * T, T), T)
    z_all[z_rows, :] = z_own[...]

    @pl.loop(0, F - 1)
    def _(i):
        put(z_own, z_all.at[z_rows, :], 2, {"fsdp": f_peer(i)})

    @pl.loop(1, X)
    def _(i):
        r = my * X + lax.rem(mx + i, X)
        put(wxz.at[own_block, :], wxz.at[own_block, :], 8, {"req": r})

    @pl.loop(0, Y - 1)
    def _(i):
        yy = y_peer(i)
        put(
            a_buf.at[pl.ds(0, T), pl.ds(pl.multiple_of(yy * X * LN, X * LN), X * LN)],
            d_all.at[y_rows, :],
            1,
            {"req": yy * X + mx},
        )

    er = iota((T, LN), 0)
    el = iota((T, LN), 1)
    proj = nt(a_buf[pl.ds(T, 2 * T), :], w_all[...])
    first = ((er == el) & (el < heads)).astype(f32)
    second = ((er == el + heads) & (el < heads)).astype(f32)
    dt_raw = jnp.dot(proj[:T], first, precision=EXACT, preferred_element_type=f32) + jnp.dot(
        proj[T:], second, precision=EXACT, preferred_element_type=f32
    )
    v = dt_raw + head_buf[pl.ds(0, 1), :]
    dtime = jnp.maximum(v, 0.0) + jnp.log1p(jnp.exp(-jnp.abs(v)))
    upto = (iota((T, T), 1) <= iota((T, T), 0)).astype(f32)
    cumul = -jnp.dot(
        upto, dtime * head_buf[pl.ds(1, 1), :], precision=EXACT, preferred_element_type=f32
    )
    hi, mid, low = pieces3(cumul)
    packed = hi + pltpu.roll(mid, 5, 1) + pltpu.roll(low, 10, 1)
    for step in (16, 32, 64):
        packed = packed + pltpu.roll(packed, step, 1)
    packed = jnp.where(lax.div(el, T) == lax.rem(er, 8), packed, 0.0)
    packed_low = jnp.sum(jnp.where(er < 8, packed, 0.0), axis=0, keepdims=True)
    packed_high = jnp.sum(jnp.where(er >= 8, packed, 0.0), axis=0, keepdims=True)
    row8 = iota((8, LN), 0)
    packed = jnp.where(row8 == 0, packed_low, jnp.where(row8 == 1, packed_high, 0.0))

    wait_bytes(z_all.at[pl.ds(0, (F - 1) * T), :], recv_sem.at[2])
    bc_raw = nt((iota((T, LN), 0) == iota((T, LN), 1)).astype(bf16), z_all[...])
    s_bc[pl.ds(T, T), :] = bc_raw
    acc = jnp.zeros((T, 2 * ns), f32) + cbb_ref[...].astype(f32).reshape(1, 2 * ns)
    for k in range(KC):
        acc = acc + cbw_ref[pl.ds(k, 1), :].astype(f32) * s_bc[pl.ds(T - KC + 1 + k, T), :]
    bc_act = silu(acc)
    b_mat = bc_act[:, :ns].astype(bf16)
    c_mat = bc_act[:, ns:].astype(bf16)
    if ns < LN:
        cc_own[...] = jnp.zeros(cc_own.shape, bf16)
    cc_own[pl.ds(0, T), pl.ds(0, ns)] = c_mat
    cc_own[pl.ds(T, CROWS - T), :] = packed[: CROWS - T].astype(bf16)
    cc_all[me] = cc_own[...]

    @pl.loop(0, R - 1)
    def _(i):
        put(cc_own, cc_all.at[me], 3, {"req": req_peer(i)})

    eye_h = iota((heads, LN), 0) == iota((heads, LN), 1)

    @pl.loop(0, slots)
    def _(s):
        decays = page_decay_ref[s]
        least = jnp.min(decays, axis=1, keepdims=True)
        least_buf[s] = jnp.sum(jnp.where(eye_h, least, 0.0), axis=0, keepdims=True)
        factor = jnp.exp(least - decays)
        for h in range(heads):
            rows = pl.ds(h * HD, HD)
            faded = page_x_ref[s, rows, :].astype(f32) * factor[h : h + 1, :]
            state_buf[s, rows, :] = jnp.dot(
                faded.astype(bf16), page_b_ref[s], preferred_element_type=f32
            ).astype(bf16)


    wait_bytes(d_all.at[pl.ds(0, (Y - 1) * T), :], recv_sem.at[1])
    wait_bytes(w_bytes, recv_sem.at[8])
    xz_send[...] = jnp.dot(d_all[...], wxz[...], preferred_element_type=f32).astype(bf16)
    xz_recv[my] = xz_send[y_rows, :]

    @pl.loop(0, Y - 1)
    def _(i):
        yy = y_peer(i)
        put(
            xz_send.at[pl.ds(pl.multiple_of(yy * T, T), T), :],
            xz_recv.at[my],
            4,
            {"req": yy * X + mx},
        )

    @pl.loop(1, X)
    def _(i):
        r = my * X + lax.rem(mx + i, X)
        put(w_ext.at[own_outs, :], w_ext.at[own_outs, :], 9, {"req": r})

    arrive("slot_req", "slot_page", "page_count", "owner_row", "accepted")
    rows_of = []
    live_of = []
    for s in range(slots):
        req = slot_req_ref[s]
        guarded = jnp.maximum(req, 0)
        live_of.append((req >= 0) & (slot_page_ref[s] < page_count_ref[guarded]))
        rows_of.append(owner_row_ref[guarded])
    by_lane = jnp.zeros((1, slots * T), jnp.int32)
    live_sub = jnp.zeros((slots * T, 1), jnp.int32)
    for s in range(slots):
        in_sub = lax.div(iota((slots * T, 1), 0), T) == s
        in_lane = lax.div(iota((1, slots * T), 1), T) == s
        live_sub = jnp.where(in_sub, live_of[s].astype(jnp.int32), live_sub)
        by_lane = jnp.where(
            in_lane, jnp.where(live_of[s], rows_of[s], -(1 << 20)), by_lane
        )
    at = lax.rem(iota((1, slots * T), 1), T)
    tall_sub = iota((R * 8, slots * T), 0)
    scatter_low = ((tall_sub == 8 * by_lane + at) & (at < 8)).astype(bf16)
    scatter_high = ((tall_sub == 8 * by_lane + at - 8) & (at >= 8)).astype(bf16)

    head_lane = lax.div(iota((T, inner), 1), HD)

    def own_heads(stacked):
        out = jnp.where(head_lane == 0, stacked[0:T], 0.0)
        for h in range(1, heads):
            out = jnp.where(head_lane == h, stacked[h * T : (h + 1) * T], out)
        return out

    wait_bytes(cc_all.at[pl.ds(0, R - 1)], recv_sem.at[3])
    group = lax.div(lane, T) == lax.rem(row, 8)
    queries = []
    fades = []
    for s in range(slots):
        block = cc_all[rows_of[s]]
        queries.append(block[:T, :ns])
        folded = block[T:].astype(f32)
        folded = jnp.where(group, jnp.where(row < 8, folded[0:1], folded[1:2]), 0.0)
        for step in (64, 32, 16):
            folded = folded + pltpu.roll(folded, step, 1)
        cum = folded + pltpu.roll(folded, LN - 5, 1) + pltpu.roll(folded, LN - 10, 1)
        fades.append(jnp.exp(cum - least_buf[s]))

    cut = 2 * HD
    for first_head, send, recv, phase in ((0, pa_send, pa_recv, 5), (2, pb_send, pb_recv, 10)):
        lanes = cut if first_head == 0 else inner - cut
        part = pl.ds(first_head * HD, lanes)
        lane_head = lax.div(iota((T, lanes), 1), HD) + first_head
        chosen = []
        for s in range(slots):
            factor = fades[s]
            spread = jnp.zeros((T, lanes), f32)
            for h in range(first_head, first_head + lanes // HD):
                spread = jnp.where(lane_head == h, factor[:, h : h + 1], spread)
            chosen.append(nt(queries[s], state_buf[s, part, :]) * spread)
        kept = jnp.where(live_sub != 0, jnp.concatenate(chosen, axis=0), 0.0).astype(bf16)
        low = jnp.dot(scatter_low, kept, preferred_element_type=f32)
        high = jnp.dot(scatter_high, kept, preferred_element_type=f32)
        send[:, :, pl.ds(0, lanes)] = low.astype(bf16).reshape(R, 8, lanes)
        send[:, :, pl.ds(lanes, lanes)] = high.astype(bf16).reshape(R, 8, lanes)
        recv[me] = send[me]

        @pl.loop(0, R - 1)
        def _(i, send=send, recv=recv, phase=phase):
            r = req_peer(i)
            put(send.at[r], recv.at[me], phase, {"req": r})

    wait_bytes(xz_recv.at[pl.ds(0, Y - 1)], recv_sem.at[4])
    xz = sum_blocks(xz_recv)
    x_raw = xz[:, :inner].astype(bf16).astype(f32)
    z_raw = xz[:, inner:].astype(bf16).astype(f32)
    s_x[pl.ds(T, T), :] = x_raw
    acc = jnp.zeros((T, inner), f32) + cxb_ref[...].astype(f32).reshape(1, inner)
    for k in range(KC):
        acc = acc + cxw_ref[pl.ds(k, 1), :].astype(f32) * s_x[pl.ds(T - KC + 1 + k, T), :]
    x_act = silu(acc).astype(bf16).astype(f32)
    xs_buf[pl.ds(0, T), :] = x_act
    bs_buf[pl.ds(0, T), :] = b_mat.astype(f32)
    scores = nt(c_mat, bs_buf[...].astype(bf16))
    zeros_t = jnp.zeros((T, LN), f32)
    eye8 = (iota((8, LN), 0) == iota((8, LN), 1)).astype(f32)
    cumul_t = nt(eye8, jnp.concatenate([cumul, zeros_t], axis=0), EXACT)
    dtime_t = nt(eye8, jnp.concatenate([dtime, zeros_t], axis=0), EXACT)
    at = iota((T, 2 * T), 0)
    au = iota((T, 2 * T), 1)
    for h in range(heads):
        spread = jnp.where(au <= at, cumul[:, h : h + 1] - cumul_t[h : h + 1, :], 0.0)
        factor = jnp.exp(spread) * dtime_t[h : h + 1, :]
        factor = jnp.where(au >= T, 1.0, jnp.where(au <= at, factor, 0.0))
        w5[pl.ds(h * T, T), pl.ds(0, 2 * T)] = (scores * factor).astype(bf16)
    local = own_heads(
        jnp.dot(
            w5[:, pl.ds(0, 2 * T)], xs_buf[...].astype(bf16), preferred_element_type=f32
        )
    )

    taken = accepted_ref[...]
    at = iota((T, LN), 0)
    last = jnp.sum(jnp.where(at == taken - 1, cumul, 0.0), axis=0, keepdims=True)
    spread = jnp.where(at < taken, last - cumul, 0.0)
    coeff = jnp.where(at < taken, jnp.exp(spread) * dtime, 0.0)
    coeff_x = jnp.zeros((T, inner), f32)
    for h in range(heads):
        coeff_x = jnp.where(head_lane == h, coeff[:, h : h + 1], coeff_x)
    y = coeff_x * x_act
    y_hi = y.astype(bf16).astype(f32)
    y2 = jnp.concatenate([y_hi, y - y_hi], axis=0).astype(bf16)
    b2 = jnp.concatenate([b_mat, b_mat], axis=0)
    fresh = lax.dot_general(
        y2, b2, (((0,), (0,)), ((), ())), preferred_element_type=f32
    )
    keep = jnp.exp(last)
    for h in range(heads):
        state_ref[0, h] = keep[:, h : h + 1] * ssm_ref[0, h] + fresh[h * HD : (h + 1) * HD]
    tail_pick = (
        iota((8, 2 * T), 1) == T - KC + 1 + taken + iota((8, 2 * T), 0)
    ).astype(bf16)
    ncx = jnp.dot(tail_pick, s_x[...].astype(bf16), preferred_element_type=f32)
    ncx_ref[0] = ncx[: KC - 1].astype(bf16)
    ncb = jnp.dot(tail_pick, s_bc[...].astype(bf16), preferred_element_type=f32)
    ncb_ref[0] = ncb[: KC - 1].astype(bf16)
    for store in stores[1:]:
        store.start()
    gate = silu(z_raw)

    parts = []
    for recv, phase in ((pa_recv, 5), (pb_recv, 10)):
        wait_bytes(recv.at[pl.ds(0, R - 1)], recv_sem.at[phase])
        part = sum_blocks(recv)
        lanes = part.shape[1] // 2
        parts.append(jnp.concatenate([part[:, :lanes], part[:, lanes:]], axis=0))
    page_sum = jnp.concatenate(parts, axis=1)
    gated = (page_sum + local) * gate
    squares = jnp.sum(gated * gated, axis=1, keepdims=True)
    hi, mid, low = pieces3(squares)
    el = iota((T, tail), 1)
    g_own[:, pl.ds(0, inner)] = (gated * gain_ref[...].astype(f32).reshape(1, inner)).astype(bf16)
    g_own[:, pl.ds(inner, tail)] = jnp.where(
        el == 0, hi, jnp.where(el == 1, mid, jnp.where(el == 2, low, 0.0))
    ).astype(bf16)
    g_all[y_rows, :] = g_own[...]

    @pl.loop(0, Y - 1)
    def _(i):
        put(g_own, g_all.at[y_rows, :], 6, {"req": y_peer(i) * X + mx})

    wait_bytes(o_bytes, recv_sem.at[9])
    wait_bytes(g_all.at[pl.ds(0, (Y - 1) * T), :], recv_sem.at[6])
    f_send[...] = nt(g_all[...], w_ext[...]).astype(bf16)

    for b in range(per_row):
        lanes = pl.ds(2 * LN * b, 2 * LN)
        target = per_row * my + b

        @pl.when(target == mf)
        def _():
            f_recv[mf] = f_send[y_rows, lanes]

        @pl.when(target != mf)
        def _():
            put(f_send.at[y_rows, lanes], f_recv.at[mf], 7, {"fsdp": target})

        @pl.loop(0, Y - 1)
        def _(i):
            yy = y_peer(i)
            put(
                f_send.at[pl.ds(pl.multiple_of(yy * T, T), T), lanes],
                f_recv.at[mf],
                7,
                {"req": yy * X + mx, "fsdp": target},
            )

    @pl.when(is_self)
    def _():
        wait_bytes(f_recv.at[pl.ds(0, F - 1)], recv_sem.at[7])

    @pl.when(jnp.logical_not(is_self))
    def _():
        wait_bytes(f_recv, recv_sem.at[7])

    out = sum_blocks(f_recv)
    wide = 2 * ocols
    total_squares = (
        out[:, wide : wide + 1] + out[:, wide + 1 : wide + 2] + out[:, wide + 2 : wide + 3]
    )
    scale = lax.rsqrt(total_squares / total_inner + EPSILON)
    mixed_ref[0] = (out * scale)[:, :wide].astype(bf16)
    stores[0].start()

    wait_bytes(w_all.at[:, pl.ds(0, (R - 1) * LN)], send_sem.at[0])
    wait_bytes(d_all.at[pl.ds(0, (Y - 1) * T), :], send_sem.at[1])
    wait_bytes(z_all.at[pl.ds(0, (F - 1) * T), :], send_sem.at[2])
    wait_bytes(cc_all.at[pl.ds(0, R - 1)], send_sem.at[3])
    wait_bytes(xz_recv.at[pl.ds(0, Y - 1)], send_sem.at[4])
    wait_bytes(w_bytes, send_sem.at[8])
    wait_bytes(o_bytes, send_sem.at[9])
    wait_bytes(pa_recv.at[pl.ds(0, R - 1)], send_sem.at[5])
    wait_bytes(pb_recv.at[pl.ds(0, R - 1)], send_sem.at[10])
    wait_bytes(g_all.at[pl.ds(0, (Y - 1) * T), :], send_sem.at[6])

    @pl.when(is_self)
    def _():
        wait_bytes(f_recv.at[pl.ds(0, F - 1)], send_sem.at[7])

    @pl.when(jnp.logical_not(is_self))
    def _():
        wait_bytes(f_recv, send_sem.at[7])


def hand_over(*refs):
    held, sem = refs[8:12], refs[12]
    reads = [pltpu.make_async_copy(refs[i], held[i], sem.at[i]) for i in range(4)]
    writes = [pltpu.make_async_copy(held[i], refs[4 + i], sem.at[4 + i]) for i in range(4)]
    for read in reads:
        read.start()
    for read, write in zip(reads, writes):
        read.wait()
        write.start()
    for write in writes:
        write.wait()


def per_device(
    R,
    F,
    drafts,
    x_weight,
    z_weight,
    bc_weight,
    dt_weight,
    dt_bias,
    decay_rate,
    conv_x_weight,
    conv_x_bias,
    conv_bc_weight,
    conv_bc_bias,
    norm_gain,
    out_weight,
    conv_x_state,
    conv_bc_state,
    ssm_state,
    sink_x,
    sink_b,
    page_x,
    page_b,
    page_decay,
    slot_req,
    slot_page,
    page_count,
    accepted,
    owner_row,
):
    inner = x_weight.shape[1]
    ns = bc_weight.shape[1] // 2
    slots, page, _ = page_x.shape
    heads = dt_weight.shape[1]
    ocols = out_weight.shape[1]
    pad_in = -(-inner // LN) * LN
    Y = R // X
    shape = jax.ShapeDtypeStruct
    operands = (
        drafts,
        x_weight,
        z_weight,
        bc_weight,
        dt_weight.T,
        dt_bias,
        decay_rate,
        conv_x_weight,
        conv_x_bias,
        conv_bc_weight,
        conv_bc_bias,
        norm_gain,
        out_weight.T,
        conv_x_state,
        conv_bc_state,
        ssm_state,
        sink_x,
        sink_b,
        jnp.swapaxes(page_x, 1, 2),
        page_b,
        page_decay,
        slot_req,
        slot_page,
        page_count,
        accepted.reshape(1, 1),
        owner_row,
    )
    out_shapes = (
        shape((1, T, 2 * ocols), bf16),
        shape(ssm_state.shape, f32),
        shape(conv_x_state.shape, bf16),
        shape(conv_bc_state.shape, bf16),
    )
    held = [
        (pltpu.SMEM if name in SCALARS else pltpu.VMEM)(a.shape, a.dtype)
        for name, a in zip(NAMES, operands)
    ]
    scratch = held + [
        pltpu.VMEM((T, LN), f32),
        pltpu.VMEM((3 * T, R * LN), bf16),
        pltpu.VMEM((T, LN), bf16),
        pltpu.VMEM((T, R * LN), bf16),
        pltpu.VMEM((Y * T, X * LN), bf16),
        pltpu.VMEM((X * LN, 2 * inner), bf16),
        pltpu.VMEM((Y * T, 2 * inner), bf16),
        pltpu.VMEM((Y, T, 2 * inner), bf16),
        pltpu.VMEM((T, LN), bf16),
        pltpu.VMEM((F * T, LN), bf16),
        pltpu.VMEM((8, LN), f32),
        pltpu.VMEM((2 * T, 2 * ns), f32),
        pltpu.VMEM((CROWS, LN), bf16),
        pltpu.VMEM((R, CROWS, LN), bf16),
        pltpu.VMEM((slots, inner, ns), bf16),
        pltpu.VMEM((slots, 1, LN), f32),
        pltpu.VMEM((heads * T, page), bf16),
        pltpu.VMEM((R, 8, 4 * HD), bf16),
        pltpu.VMEM((R, 8, 4 * HD), bf16),
        pltpu.VMEM((R, 8, 2 * inner - 4 * HD), bf16),
        pltpu.VMEM((R, 8, 2 * inner - 4 * HD), bf16),
        pltpu.VMEM((2 * T, inner), f32),
        pltpu.VMEM((2 * T, inner), f32),
        pltpu.VMEM((2 * T, ns), f32),
        pltpu.VMEM((T, pad_in), bf16),
        pltpu.VMEM((Y * T, pad_in), bf16),
        pltpu.VMEM((X * LN, pad_in), bf16),
        pltpu.VMEM((Y * T, X * LN), bf16),
        pltpu.VMEM((F, T, 2 * LN), bf16),
        pltpu.SemaphoreType.DMA((11,)),
        pltpu.SemaphoreType.DMA((11,)),
        *(pltpu.VMEM(a.shape, a.dtype) for a in out_shapes),
        pltpu.SemaphoreType.DMA((26,)),
        pltpu.SemaphoreType.DMA((4,)),
    ]
    results = pl.pallas_call(
        functools.partial(kernel, R, F),
        out_shape=out_shapes,
        in_specs=[pl.BlockSpec(memory_space=pltpu.HBM)] * 26,
        out_specs=(pl.BlockSpec(memory_space=pltpu.HBM),) * 4,
        scratch_shapes=scratch,
        compiler_params=pltpu.CompilerParams(
            collective_id=0, has_side_effects=True
        ),
        name="mixer",
    )(*operands)
    hbm = pl.BlockSpec(memory_space=pltpu.HBM)
    return pl.pallas_call(
        hand_over,
        out_shape=tuple(shape(a.shape, a.dtype) for a in results),
        in_specs=[hbm] * 4,
        out_specs=(hbm,) * 4,
        scratch_shapes=[pltpu.VMEM(a.shape, a.dtype) for a in results]
        + [pltpu.SemaphoreType.DMA((8,))],
        name="hand_over",
    )(*results)


def solution(mesh):
    in_specs = (
        P("req", None, None),
        P("req", "fsdp"),
        P("req", "fsdp"),
        P("req", None),
        P("req", "fsdp"),
        P("fsdp"),
        P("fsdp"),
        P(None, "fsdp"),
        P("fsdp"),
        P(),
        P(),
        P("fsdp"),
        P("fsdp", "req"),
        P("req", None, "fsdp"),
        P("req", None, None),
        P("req", "fsdp", None, None),
        P("req", None, "fsdp"),
        P("req", None, None),
        P("req", None, "fsdp"),
        P("req", None, None),
        P("req", "fsdp", None),
        P("req"),
        P("req"),
        P(),
        P("req"),
        P(),
    )
    out_specs = (
        P("req", None, "fsdp"),
        P("req", "fsdp", None, None),
        P("req", None, "fsdp"),
        P("req", None, None),
    )
    return jax.shard_map(
        functools.partial(per_device, mesh.shape["req"], mesh.shape["fsdp"]),
        mesh=mesh,
        in_specs=in_specs,
        out_specs=out_specs,
        check_vma=False,
    )
```

```python
import functools

import jax
import jax.numpy as jnp
from jax import lax
from jax.experimental import pallas as pl
from jax.experimental.pallas import tpu as pltpu
from jax.sharding import PartitionSpec as P

MESH = pl.DeviceIdType.MESH
T = 16
CROWS = 18
X = 4
KC = 4
HD = 64
LN = 128
EPSILON = 1e-05
f32 = jnp.float32
bf16 = jnp.bfloat16
EXACT = lax.Precision.HIGHEST
NAMES = (
    "drafts",
    "xw",
    "zw",
    "bcw",
    "dtw",
    "dt_bias",
    "decay",
    "cxw",
    "cxb",
    "cbw",
    "cbb",
    "gain",
    "ow",
    "cxs",
    "cbs",
    "ssm",
    "sink_x",
    "sink_b",
    "page_x",
    "page_b",
    "page_decay",
    "slot_req",
    "slot_page",
    "page_count",
    "accepted",
    "owner_row",
)
SCALARS = ("slot_req", "slot_page", "page_count", "owner_row")
FIRST = ("bcw", "dtw")
SECOND = ("drafts", "xw", "zw", "ow")
OTHERS = tuple(n for n in NAMES if n not in FIRST + SECOND)


def nt(a, b, precision=None):
    return lax.dot_general(
        a, b, (((1,), (1,)), ((), ())), preferred_element_type=f32, precision=precision
    )


def iota(shape, axis):
    return lax.broadcasted_iota(jnp.int32, shape, axis)


def silu(v):
    return v * jax.nn.sigmoid(v)


def far_first(k, n):
    return n // 2 + jnp.where(lax.rem(k, 2) == 1, -lax.div(k + 1, 2), lax.div(k, 2))


def sum_blocks(ref):
    n = ref.shape[0]
    group = min(8, n)
    total = None
    for i in range(0, n, group):
        part = ref[i].astype(f32)
        for j in range(i + 1, i + group):
            part = part + ref[j].astype(f32)
        total = part if total is None else total + part
    return total


def pieces3(v):
    hi = v.astype(bf16).astype(f32)
    rest = v - hi
    mid = rest.astype(bf16).astype(f32)
    low = (rest - mid).astype(bf16).astype(f32)
    return hi, mid, low


def kernel(R, F, *refs):
    sources, outs, held, rest = refs[:26], refs[26:30], refs[30:56], refs[56:-6]
    ready, load_sem, store_sem = refs[-6:-2], refs[-2], refs[-1]
    stores = [
        pltpu.make_async_copy(source, target, store_sem.at[i])
        for i, (source, target) in enumerate(zip(ready, outs))
    ]
    copies = [
        pltpu.make_async_copy(source, target, load_sem.at[i])
        for i, (source, target) in enumerate(zip(sources, held))
    ]

    def load(*names):
        for name in names:
            copies[NAMES.index(name)].start()

    def arrive(*names):
        for name in names:
            copies[NAMES.index(name)].wait()

    body(R, F, load, arrive, stores, *held, *ready, *rest)
    for store in stores:
        store.wait()


def body(
    R,
    F,
    load,
    arrive,
    stores,
    drafts_ref,
    xw_ref,
    zw_ref,
    bcw_ref,
    dtw_ref,
    dt_bias_ref,
    decay_ref,
    cxw_ref,
    cxb_ref,
    cbw_ref,
    cbb_ref,
    gain_ref,
    ow_ref,
    cxs_ref,
    cbs_ref,
    ssm_ref,
    sink_x_ref,
    sink_b_ref,
    page_x_ref,
    page_b_ref,
    page_decay_ref,
    slot_req_ref,
    slot_page_ref,
    page_count_ref,
    accepted_ref,
    owner_row_ref,
    mixed_ref,
    state_ref,
    ncx_ref,
    ncb_ref,
    dt_buf,
    a_buf,
    w_own,
    w_all,
    d_all,
    wxz,
    xz_send,
    xz_recv,
    z_own,
    z_all,
    head_buf,
    s_bc,
    cc_own,
    cc_all,
    state_buf,
    least_buf,
    w5,
    pa_send,
    pa_recv,
    pb_send,
    pb_recv,
    s_x,
    xs_buf,
    bs_buf,
    g_own,
    g_all,
    w_ext,
    f_send,
    f_recv,
    send_sem,
    recv_sem,
):
    me = lax.axis_index("req")
    mf = lax.axis_index("fsdp")
    ks, inner = xw_ref.shape
    half = ks // 2
    heads = dtw_ref.shape[0]
    ns = bcw_ref.shape[1] // 2
    slots = page_x_ref.shape[0]
    total_inner = inner * F
    ocols = ow_ref.shape[0]
    pad_in = g_own.shape[1]
    Y = R // X
    per_row = X // 2
    my = lax.div(me, X)
    mx = lax.rem(me, X)
    is_self = lax.div(mf, per_row) == my
    source = lax.div(mf, per_row) * X + mx
    Z = F // 2

    def ring(n):
        return [n // 2 + (-(k + 1) // 2 if k % 2 else k // 2) for k in range(n)]

    y_ring = [lax.rem(my + k, Y) * X for k in ring(Y)]
    x_ring = [lax.rem(mx + k, X) for k in ring(X)]
    req_peers = [a + b for a in y_ring for b in x_ring][: R - 1]

    def y_peer(i):
        return lax.rem(my + far_first(i, Y), Y)

    def f_peer(i):
        zz = lax.rem(lax.div(mf, 2) + far_first(lax.div(i, 2), Z), Z)
        return zz * 2 + lax.rem(mf + 1 + i, 2)


    load(*FIRST)
    barrier = pltpu.get_barrier_semaphore()

    for r in req_peers:
        pl.semaphore_signal(barrier, inc=1, device_id={"req": r}, device_id_type=MESH)

    @pl.loop(0, F - 1)
    def _(i):
        pl.semaphore_signal(barrier, inc=1, device_id={"fsdp": f_peer(i)}, device_id_type=MESH)


    load(*SECOND)
    arrive("bcw", "dtw")
    wpad = jnp.concatenate([bcw_ref[...], jnp.zeros((LN - ks, 2 * ns), bf16)], axis=0)
    pick = (iota((T, 2 * ns), 1) == T * mf + iota((T, 2 * ns), 0)).astype(bf16)
    bc_rows = nt(pick, wpad)
    row = iota((T, LN), 0)
    lane = iota((T, LN), 1)
    dt_buf[...] = jnp.zeros(dt_buf.shape, f32)
    dt_buf[pl.ds(0, heads), pl.ds(0, ks)] = dtw_ref[...].astype(f32)
    dt_buf[pl.ds(heads, heads), pl.ds(0, ks)] = dtw_ref[...].astype(f32)
    dt_rows = dt_buf[...]
    dt_rows = jnp.where(
        row < heads, pltpu.roll(dt_rows, ks, 1), pltpu.roll(dt_rows, half, 1)
    )
    dt_zone = (lane >= ks) & (lane < ks + half)
    w_own[...] = jnp.where(
        lane < ks, bc_rows, jnp.where(dt_zone & (row < 2 * heads), dt_rows, 0.0)
    ).astype(bf16)
    w_all[:, pl.ds(pl.multiple_of(me * LN, LN), LN)] = w_own[...]

    own_rows = pl.ds(pl.multiple_of(me * T, T), T)
    y_rows = pl.ds(pl.multiple_of(my * T, T), T)
    pl.semaphore_wait(
        barrier, (R - 1) + (F - 1)
    )

    def put(src, dst, phase, device):
        pltpu.make_async_remote_copy(
            src_ref=src,
            dst_ref=dst,
            send_sem=send_sem.at[phase],
            recv_sem=recv_sem.at[phase],
            device_id=device,
            device_id_type=MESH,
        ).start()

    def wait_bytes(ref, sem):
        pltpu.make_async_copy(ref, ref, sem).wait()

    own_lanes = pl.ds(pl.multiple_of(me * LN, LN), LN)
    w_bytes = wxz.at[pl.ds(0, (X - 1) * ks), :]
    o_bytes = w_ext.at[pl.ds(0, (X - 1) * ocols), :]

    for r in req_peers:
        put(w_own, w_all.at[:, own_lanes], 0, {"req": r})

    load(*OTHERS)

    own_block = pl.ds(pl.multiple_of(mx * LN, LN), ks)
    own_outs = pl.ds(
        pl.multiple_of(lax.div(mx, 2) * 2 * LN + lax.rem(mx, 2) * ocols, 16), ocols
    )
    tail = pad_in - inner
    for i in range(X):
        wxz[pl.ds(LN * i + ks, LN - ks), :] = jnp.zeros((LN - ks, 2 * inner), bf16)
    arrive("xw", "zw")
    wxz[own_block, pl.ds(0, inner)] = xw_ref[...]
    wxz[own_block, pl.ds(inner, inner)] = zw_ref[...]
    arrive("ow")
    w_ext[own_outs, pl.ds(0, inner)] = ow_ref[...]
    w_ext[own_outs, pl.ds(inner, tail)] = jnp.zeros((ocols, tail), bf16)
    rest = 2 * LN - 2 * ocols
    er = iota((rest, tail), 0)
    el = iota((rest, tail), 1)
    for i in range(per_row):
        top = pl.ds(2 * LN * i + 2 * ocols, rest)
        w_ext[top, pl.ds(0, inner)] = jnp.zeros((rest, inner), bf16)
        w_ext[top, pl.ds(inner, tail)] = ((er == el) & (el < 3)).astype(bf16)

    arrive("drafts")
    z_own[...] = jnp.zeros(z_own.shape, bf16)
    for j in range(R):
        start = ks * j
        base = start // LN * LN
        off = start - base
        if off + ks <= LN:
            window = drafts_ref[0, :, pl.ds(base, LN)].astype(f32)
            if off:
                window = pltpu.roll(window, LN - off, 1)
        else:
            window = drafts_ref[0, :, pl.ds(base, 2 * LN)].astype(f32)
            window = pltpu.roll(window, 2 * LN - off, 1)[:, :LN]
        a_buf[pl.ds(0, T), pl.ds(LN * j, LN)] = jnp.where(lane < ks, window, 0.0).astype(bf16)
        a_buf[pl.ds(T, T), pl.ds(LN * j, LN)] = jnp.where(
            dt_zone, pltpu.roll(window, ks, 1), 0.0
        ).astype(bf16)
        a_buf[pl.ds(2 * T, T), pl.ds(LN * j, LN)] = jnp.where(
            dt_zone, pltpu.roll(window, half, 1), 0.0
        ).astype(bf16)
    d_all[y_rows, :] = a_buf[pl.ds(0, T), pl.ds(pl.multiple_of(my * X * LN, X * LN), X * LN)]

    arrive("dt_bias", "decay", "cbs", "cxs", "sink_b", "sink_x")
    head_buf[...] = jnp.zeros(head_buf.shape, f32)
    head_buf[pl.ds(0, 1), pl.ds(0, heads)] = dt_bias_ref[...].reshape(1, heads)
    head_buf[pl.ds(1, 1), pl.ds(0, heads)] = decay_ref[...].reshape(1, heads)
    s_bc[...] = jnp.zeros(s_bc.shape, f32)
    s_bc[pl.ds(T - KC + 1, KC - 1), :] = cbs_ref[0].astype(f32)
    s_x[...] = jnp.zeros(s_x.shape, f32)
    s_x[pl.ds(T - KC + 1, KC - 1), :] = cxs_ref[0].astype(f32)
    bs_buf[...] = jnp.zeros(bs_buf.shape, f32)
    bs_buf[pl.ds(T, 4), :] = sink_b_ref[0].astype(f32)
    xs_buf[...] = jnp.zeros(xs_buf.shape, f32)
    xs_buf[pl.ds(T, 4), :] = sink_x_ref[0].astype(f32)
    arrive("cbb", "cbw", "cxb", "cxw", "gain", "ssm", "page_x", "page_b", "page_decay")

    wait_bytes(w_all.at[:, pl.ds(0, (R - 1) * LN)], recv_sem.at[0])
    z_own[:, pl.ds(0, 3 * T)] = nt(w_all[...], a_buf[...]).astype(bf16)
    z_rows = pl.ds(pl.multiple_of(mf * T, T), T)
    z_all[z_rows, :] = z_own[...]

    @pl.loop(0, F - 1)
    def _(i):
        put(z_own, z_all.at[z_rows, :], 2, {"fsdp": f_peer(i)})

    @pl.loop(1, X)
    def _(i):
        r = my * X + lax.rem(mx + i, X)
        put(wxz.at[own_block, :], wxz.at[own_block, :], 8, {"req": r})

    @pl.loop(0, Y - 1)
    def _(i):
        yy = y_peer(i)
        put(
            a_buf.at[pl.ds(0, T), pl.ds(pl.multiple_of(yy * X * LN, X * LN), X * LN)],
            d_all.at[y_rows, :],
            1,
            {"req": yy * X + mx},
        )

    er = iota((T, LN), 0)
    el = iota((T, LN), 1)
    proj = nt(a_buf[pl.ds(T, 2 * T), :], w_all[...])
    first = ((er == el) & (el < heads)).astype(f32)
    second = ((er == el + heads) & (el < heads)).astype(f32)
    dt_raw = jnp.dot(proj[:T], first, precision=EXACT, preferred_element_type=f32) + jnp.dot(
        proj[T:], second, precision=EXACT, preferred_element_type=f32
    )
    v = dt_raw + head_buf[pl.ds(0, 1), :]
    dtime = jnp.maximum(v, 0.0) + jnp.log1p(jnp.exp(-jnp.abs(v)))
    upto = (iota((T, T), 1) <= iota((T, T), 0)).astype(f32)
    cumul = -jnp.dot(
        upto, dtime * head_buf[pl.ds(1, 1), :], precision=EXACT, preferred_element_type=f32
    )
    hi, mid, low = pieces3(cumul)
    packed = hi + pltpu.roll(mid, 5, 1) + pltpu.roll(low, 10, 1)
    for step in (16, 32, 64):
        packed = packed + pltpu.roll(packed, step, 1)
    packed = jnp.where(lax.div(el, T) == lax.rem(er, 8), packed, 0.0)
    packed_low = jnp.sum(jnp.where(er < 8, packed, 0.0), axis=0, keepdims=True)
    packed_high = jnp.sum(jnp.where(er >= 8, packed, 0.0), axis=0, keepdims=True)
    row8 = iota((8, LN), 0)
    packed = jnp.where(row8 == 0, packed_low, jnp.where(row8 == 1, packed_high, 0.0))

    wait_bytes(z_all.at[pl.ds(0, (F - 1) * T), :], recv_sem.at[2])
    bc_raw = nt((iota((T, LN), 0) == iota((T, LN), 1)).astype(bf16), z_all[...])
    s_bc[pl.ds(T, T), :] = bc_raw
    acc = jnp.zeros((T, 2 * ns), f32) + cbb_ref[...].astype(f32).reshape(1, 2 * ns)
    for k in range(KC):
        acc = acc + cbw_ref[pl.ds(k, 1), :].astype(f32) * s_bc[pl.ds(T - KC + 1 + k, T), :]
    bc_act = silu(acc)
    b_mat = bc_act[:, :ns].astype(bf16)
    c_mat = bc_act[:, ns:].astype(bf16)
    if ns < LN:
        cc_own[...] = jnp.zeros(cc_own.shape, bf16)
    cc_own[pl.ds(0, T), pl.ds(0, ns)] = c_mat
    cc_own[pl.ds(T, CROWS - T), :] = packed[: CROWS - T].astype(bf16)
    cc_all[me] = cc_own[...]

    for r in req_peers:
        put(cc_own, cc_all.at[me], 3, {"req": r})

    eye_h = iota((heads, LN), 0) == iota((heads, LN), 1)

    @pl.loop(0, slots)
    def _(s):
        decays = page_decay_ref[s]
        least = jnp.min(decays, axis=1, keepdims=True)
        least_buf[s] = jnp.sum(jnp.where(eye_h, least, 0.0), axis=0, keepdims=True)
        factor = jnp.exp(least - decays)
        for h in range(heads):
            rows = pl.ds(h * HD, HD)
            faded = page_x_ref[s, rows, :].astype(f32) * factor[h : h + 1, :]
            state_buf[s, rows, :] = jnp.dot(
                faded.astype(bf16), page_b_ref[s], preferred_element_type=f32
            ).astype(bf16)


    wait_bytes(d_all.at[pl.ds(0, (Y - 1) * T), :], recv_sem.at[1])
    wait_bytes(w_bytes, recv_sem.at[8])
    xz_send[...] = jnp.dot(d_all[...], wxz[...], preferred_element_type=f32).astype(bf16)
    xz_recv[my] = xz_send[y_rows, :]

    @pl.loop(0, Y - 1)
    def _(i):
        yy = y_peer(i)
        put(
            xz_send.at[pl.ds(pl.multiple_of(yy * T, T), T), :],
            xz_recv.at[my],
            4,
            {"req": yy * X + mx},
        )

    @pl.loop(1, X)
    def _(i):
        r = my * X + lax.rem(mx + i, X)
        put(w_ext.at[own_outs, :], w_ext.at[own_outs, :], 9, {"req": r})

    arrive("slot_req", "slot_page", "page_count", "owner_row", "accepted")
    rows_of = []
    live_of = []
    for s in range(slots):
        req = slot_req_ref[s]
        guarded = jnp.maximum(req, 0)
        live_of.append((req >= 0) & (slot_page_ref[s] < page_count_ref[guarded]))
        rows_of.append(owner_row_ref[guarded])
    by_lane = jnp.zeros((1, slots * T), jnp.int32)
    live_sub = jnp.zeros((slots * T, 1), jnp.int32)
    for s in range(slots):
        in_sub = lax.div(iota((slots * T, 1), 0), T) == s
        in_lane = lax.div(iota((1, slots * T), 1), T) == s
        live_sub = jnp.where(in_sub, live_of[s].astype(jnp.int32), live_sub)
        by_lane = jnp.where(
            in_lane, jnp.where(live_of[s], rows_of[s], -(1 << 20)), by_lane
        )
    at = lax.rem(iota((1, slots * T), 1), T)
    tall_sub = iota((R * 8, slots * T), 0)
    scatter_low = ((tall_sub == 8 * by_lane + at) & (at < 8)).astype(bf16)
    scatter_high = ((tall_sub == 8 * by_lane + at - 8) & (at >= 8)).astype(bf16)

    head_lane = lax.div(iota((T, inner), 1), HD)

    def own_heads(stacked):
        out = jnp.where(head_lane == 0, stacked[0:T], 0.0)
        for h in range(1, heads):
            out = jnp.where(head_lane == h, stacked[h * T : (h + 1) * T], out)
        return out

    wait_bytes(cc_all.at[pl.ds(0, R - 1)], recv_sem.at[3])
    group = lax.div(lane, T) == lax.rem(row, 8)
    queries = []
    fades = []
    for s in range(slots):
        block = cc_all[rows_of[s]]
        queries.append(block[:T, :ns])
        folded = block[T:].astype(f32)
        folded = jnp.where(group, jnp.where(row < 8, folded[0:1], folded[1:2]), 0.0)
        for step in (64, 32, 16):
            folded = folded + pltpu.roll(folded, step, 1)
        cum = folded + pltpu.roll(folded, LN - 5, 1) + pltpu.roll(folded, LN - 10, 1)
        fades.append(jnp.exp(cum - least_buf[s]))

    cut = 2 * HD
    for first_head, send, recv, phase in ((0, pa_send, pa_recv, 5), (2, pb_send, pb_recv, 10)):
        lanes = cut if first_head == 0 else inner - cut
        part = pl.ds(first_head * HD, lanes)
        lane_head = lax.div(iota((T, lanes), 1), HD) + first_head
        chosen = []
        for s in range(slots):
            factor = fades[s]
            spread = jnp.zeros((T, lanes), f32)
            for h in range(first_head, first_head + lanes // HD):
                spread = jnp.where(lane_head == h, factor[:, h : h + 1], spread)
            chosen.append(nt(queries[s], state_buf[s, part, :]) * spread)
        kept = jnp.where(live_sub != 0, jnp.concatenate(chosen, axis=0), 0.0).astype(bf16)
        low = jnp.dot(scatter_low, kept, preferred_element_type=f32)
        high = jnp.dot(scatter_high, kept, preferred_element_type=f32)
        send[:, :, pl.ds(0, lanes)] = low.astype(bf16).reshape(R, 8, lanes)
        send[:, :, pl.ds(lanes, lanes)] = high.astype(bf16).reshape(R, 8, lanes)
        recv[me] = send[me]

        for r in req_peers:
            put(send.at[r], recv.at[me], phase, {"req": r})

    wait_bytes(xz_recv.at[pl.ds(0, Y - 1)], recv_sem.at[4])
    xz = sum_blocks(xz_recv)
    x_raw = xz[:, :inner].astype(bf16).astype(f32)
    z_raw = xz[:, inner:].astype(bf16).astype(f32)
    s_x[pl.ds(T, T), :] = x_raw
    acc = jnp.zeros((T, inner), f32) + cxb_ref[...].astype(f32).reshape(1, inner)
    for k in range(KC):
        acc = acc + cxw_ref[pl.ds(k, 1), :].astype(f32) * s_x[pl.ds(T - KC + 1 + k, T), :]
    x_act = silu(acc).astype(bf16).astype(f32)
    xs_buf[pl.ds(0, T), :] = x_act
    bs_buf[pl.ds(0, T), :] = b_mat.astype(f32)
    scores = nt(c_mat, bs_buf[...].astype(bf16))
    zeros_t = jnp.zeros((T, LN), f32)
    eye8 = (iota((8, LN), 0) == iota((8, LN), 1)).astype(f32)
    cumul_t = nt(eye8, jnp.concatenate([cumul, zeros_t], axis=0), EXACT)
    dtime_t = nt(eye8, jnp.concatenate([dtime, zeros_t], axis=0), EXACT)
    at = iota((T, 2 * T), 0)
    au = iota((T, 2 * T), 1)
    for h in range(heads):
        spread = jnp.where(au <= at, cumul[:, h : h + 1] - cumul_t[h : h + 1, :], 0.0)
        factor = jnp.exp(spread) * dtime_t[h : h + 1, :]
        factor = jnp.where(au >= T, 1.0, jnp.where(au <= at, factor, 0.0))
        w5[pl.ds(h * T, T), pl.ds(0, 2 * T)] = (scores * factor).astype(bf16)
    local = own_heads(
        jnp.dot(
            w5[:, pl.ds(0, 2 * T)], xs_buf[...].astype(bf16), preferred_element_type=f32
        )
    )

    taken = accepted_ref[...]
    at = iota((T, LN), 0)
    last = jnp.sum(jnp.where(at == taken - 1, cumul, 0.0), axis=0, keepdims=True)
    spread = jnp.where(at < taken, last - cumul, 0.0)
    coeff = jnp.where(at < taken, jnp.exp(spread) * dtime, 0.0)
    coeff_x = jnp.zeros((T, inner), f32)
    for h in range(heads):
        coeff_x = jnp.where(head_lane == h, coeff[:, h : h + 1], coeff_x)
    y = coeff_x * x_act
    y_hi = y.astype(bf16).astype(f32)
    y2 = jnp.concatenate([y_hi, y - y_hi], axis=0).astype(bf16)
    b2 = jnp.concatenate([b_mat, b_mat], axis=0)
    fresh = lax.dot_general(
        y2, b2, (((0,), (0,)), ((), ())), preferred_element_type=f32
    )
    keep = jnp.exp(last)
    for h in range(heads):
        state_ref[0, h] = keep[:, h : h + 1] * ssm_ref[0, h] + fresh[h * HD : (h + 1) * HD]
    tail_pick = (
        iota((8, 2 * T), 1) == T - KC + 1 + taken + iota((8, 2 * T), 0)
    ).astype(bf16)
    ncx = jnp.dot(tail_pick, s_x[...].astype(bf16), preferred_element_type=f32)
    ncx_ref[0] = ncx[: KC - 1].astype(bf16)
    ncb = jnp.dot(tail_pick, s_bc[...].astype(bf16), preferred_element_type=f32)
    ncb_ref[0] = ncb[: KC - 1].astype(bf16)
    for store in stores[1:]:
        store.start()
    gate = silu(z_raw)

    parts = []
    for recv, phase in ((pa_recv, 5), (pb_recv, 10)):
        wait_bytes(recv.at[pl.ds(0, R - 1)], recv_sem.at[phase])
        part = sum_blocks(recv)
        lanes = part.shape[1] // 2
        parts.append(jnp.concatenate([part[:, :lanes], part[:, lanes:]], axis=0))
    page_sum = jnp.concatenate(parts, axis=1)
    gated = (page_sum + local) * gate
    squares = jnp.sum(gated * gated, axis=1, keepdims=True)
    hi, mid, low = pieces3(squares)
    el = iota((T, tail), 1)
    g_own[:, pl.ds(0, inner)] = (gated * gain_ref[...].astype(f32).reshape(1, inner)).astype(bf16)
    g_own[:, pl.ds(inner, tail)] = jnp.where(
        el == 0, hi, jnp.where(el == 1, mid, jnp.where(el == 2, low, 0.0))
    ).astype(bf16)
    g_all[y_rows, :] = g_own[...]

    @pl.loop(0, Y - 1)
    def _(i):
        put(g_own, g_all.at[y_rows, :], 6, {"req": y_peer(i) * X + mx})

    wait_bytes(o_bytes, recv_sem.at[9])
    wait_bytes(g_all.at[pl.ds(0, (Y - 1) * T), :], recv_sem.at[6])
    f_send[...] = nt(g_all[...], w_ext[...]).astype(bf16)

    for b in range(per_row):
        lanes = pl.ds(2 * LN * b, 2 * LN)
        target = per_row * my + b

        @pl.when(target == mf)
        def _():
            f_recv[mf] = f_send[y_rows, lanes]

        @pl.when(target != mf)
        def _():
            put(f_send.at[y_rows, lanes], f_recv.at[mf], 7, {"fsdp": target})

        @pl.loop(0, Y - 1)
        def _(i):
            yy = y_peer(i)
            put(
                f_send.at[pl.ds(pl.multiple_of(yy * T, T), T), lanes],
                f_recv.at[mf],
                7,
                {"req": yy * X + mx, "fsdp": target},
            )

    @pl.when(is_self)
    def _():
        wait_bytes(f_recv.at[pl.ds(0, F - 1)], recv_sem.at[7])

    @pl.when(jnp.logical_not(is_self))
    def _():
        wait_bytes(f_recv, recv_sem.at[7])

    out = sum_blocks(f_recv)
    wide = 2 * ocols
    total_squares = (
        out[:, wide : wide + 1] + out[:, wide + 1 : wide + 2] + out[:, wide + 2 : wide + 3]
    )
    scale = lax.rsqrt(total_squares / total_inner + EPSILON)
    mixed_ref[0] = (out * scale)[:, :wide].astype(bf16)
    stores[0].start()

    wait_bytes(w_all.at[:, pl.ds(0, (R - 1) * LN)], send_sem.at[0])
    wait_bytes(d_all.at[pl.ds(0, (Y - 1) * T), :], send_sem.at[1])
    wait_bytes(z_all.at[pl.ds(0, (F - 1) * T), :], send_sem.at[2])
    wait_bytes(cc_all.at[pl.ds(0, R - 1)], send_sem.at[3])
    wait_bytes(xz_recv.at[pl.ds(0, Y - 1)], send_sem.at[4])
    wait_bytes(w_bytes, send_sem.at[8])
    wait_bytes(o_bytes, send_sem.at[9])
    wait_bytes(pa_recv.at[pl.ds(0, R - 1)], send_sem.at[5])
    wait_bytes(pb_recv.at[pl.ds(0, R - 1)], send_sem.at[10])
    wait_bytes(g_all.at[pl.ds(0, (Y - 1) * T), :], send_sem.at[6])

    @pl.when(is_self)
    def _():
        wait_bytes(f_recv.at[pl.ds(0, F - 1)], send_sem.at[7])

    @pl.when(jnp.logical_not(is_self))
    def _():
        wait_bytes(f_recv, send_sem.at[7])


def hand_over(*refs):
    held, sem = refs[8:12], refs[12]
    reads = [pltpu.make_async_copy(refs[i], held[i], sem.at[i]) for i in range(4)]
    writes = [pltpu.make_async_copy(held[i], refs[4 + i], sem.at[4 + i]) for i in range(4)]
    for read in reads:
        read.start()
    for read, write in zip(reads, writes):
        read.wait()
        write.start()
    for write in writes:
        write.wait()


def per_device(
    R,
    F,
    drafts,
    x_weight,
    z_weight,
    bc_weight,
    dt_weight,
    dt_bias,
    decay_rate,
    conv_x_weight,
    conv_x_bias,
    conv_bc_weight,
    conv_bc_bias,
    norm_gain,
    out_weight,
    conv_x_state,
    conv_bc_state,
    ssm_state,
    sink_x,
    sink_b,
    page_x,
    page_b,
    page_decay,
    slot_req,
    slot_page,
    page_count,
    accepted,
    owner_row,
):
    inner = x_weight.shape[1]
    ns = bc_weight.shape[1] // 2
    slots, page, _ = page_x.shape
    heads = dt_weight.shape[1]
    ocols = out_weight.shape[1]
    pad_in = -(-inner // LN) * LN
    Y = R // X
    shape = jax.ShapeDtypeStruct
    operands = (
        drafts,
        x_weight,
        z_weight,
        bc_weight,
        dt_weight.T,
        dt_bias,
        decay_rate,
        conv_x_weight,
        conv_x_bias,
        conv_bc_weight,
        conv_bc_bias,
        norm_gain,
        out_weight.T,
        conv_x_state,
        conv_bc_state,
        ssm_state,
        sink_x,
        sink_b,
        jnp.swapaxes(page_x, 1, 2),
        page_b,
        page_decay,
        slot_req,
        slot_page,
        page_count,
        accepted.reshape(1, 1),
        owner_row,
    )
    out_shapes = (
        shape((1, T, 2 * ocols), bf16),
        shape(ssm_state.shape, f32),
        shape(conv_x_state.shape, bf16),
        shape(conv_bc_state.shape, bf16),
    )
    held = [
        (pltpu.SMEM if name in SCALARS else pltpu.VMEM)(a.shape, a.dtype)
        for name, a in zip(NAMES, operands)
    ]
    scratch = held + [
        pltpu.VMEM((T, LN), f32),
        pltpu.VMEM((3 * T, R * LN), bf16),
        pltpu.VMEM((T, LN), bf16),
        pltpu.VMEM((T, R * LN), bf16),
        pltpu.VMEM((Y * T, X * LN), bf16),
        pltpu.VMEM((X * LN, 2 * inner), bf16),
        pltpu.VMEM((Y * T, 2 * inner), bf16),
        pltpu.VMEM((Y, T, 2 * inner), bf16),
        pltpu.VMEM((T, LN), bf16),
        pltpu.VMEM((F * T, LN), bf16),
        pltpu.VMEM((8, LN), f32),
        pltpu.VMEM((2 * T, 2 * ns), f32),
        pltpu.VMEM((CROWS, LN), bf16),
        pltpu.VMEM((R, CROWS, LN), bf16),
        pltpu.VMEM((slots, inner, ns), bf16),
        pltpu.VMEM((slots, 1, LN), f32),
        pltpu.VMEM((heads * T, page), bf16),
        pltpu.VMEM((R, 8, 4 * HD), bf16),
        pltpu.VMEM((R, 8, 4 * HD), bf16),
        pltpu.VMEM((R, 8, 2 * inner - 4 * HD), bf16),
        pltpu.VMEM((R, 8, 2 * inner - 4 * HD), bf16),
        pltpu.VMEM((2 * T, inner), f32),
        pltpu.VMEM((2 * T, inner), f32),
        pltpu.VMEM((2 * T, ns), f32),
        pltpu.VMEM((T, pad_in), bf16),
        pltpu.VMEM((Y * T, pad_in), bf16),
        pltpu.VMEM((X * LN, pad_in), bf16),
        pltpu.VMEM((Y * T, X * LN), bf16),
        pltpu.VMEM((F, T, 2 * LN), bf16),
        pltpu.SemaphoreType.DMA((11,)),
        pltpu.SemaphoreType.DMA((11,)),
        *(pltpu.VMEM(a.shape, a.dtype) for a in out_shapes),
        pltpu.SemaphoreType.DMA((26,)),
        pltpu.SemaphoreType.DMA((4,)),
    ]
    results = pl.pallas_call(
        functools.partial(kernel, R, F),
        out_shape=out_shapes,
        in_specs=[pl.BlockSpec(memory_space=pltpu.HBM)] * 26,
        out_specs=(pl.BlockSpec(memory_space=pltpu.HBM),) * 4,
        scratch_shapes=scratch,
        compiler_params=pltpu.CompilerParams(
            collective_id=0, has_side_effects=True
        ),
        name="mixer",
    )(*operands)
    hbm = pl.BlockSpec(memory_space=pltpu.HBM)
    return pl.pallas_call(
        hand_over,
        out_shape=tuple(shape(a.shape, a.dtype) for a in results),
        in_specs=[hbm] * 4,
        out_specs=(hbm,) * 4,
        scratch_shapes=[pltpu.VMEM(a.shape, a.dtype) for a in results]
        + [pltpu.SemaphoreType.DMA((8,))],
        name="hand_over",
    )(*results)


def solution(mesh):
    in_specs = (
        P("req", None, None),
        P("req", "fsdp"),
        P("req", "fsdp"),
        P("req", None),
        P("req", "fsdp"),
        P("fsdp"),
        P("fsdp"),
        P(None, "fsdp"),
        P("fsdp"),
        P(),
        P(),
        P("fsdp"),
        P("fsdp", "req"),
        P("req", None, "fsdp"),
        P("req", None, None),
        P("req", "fsdp", None, None),
        P("req", None, "fsdp"),
        P("req", None, None),
        P("req", None, "fsdp"),
        P("req", None, None),
        P("req", "fsdp", None),
        P("req"),
        P("req"),
        P(),
        P("req"),
        P(),
    )
    out_specs = (
        P("req", None, "fsdp"),
        P("req", "fsdp", None, None),
        P("req", None, "fsdp"),
        P("req", None, None),
    )
    return jax.shard_map(
        functools.partial(per_device, mesh.shape["req"], mesh.shape["fsdp"]),
        mesh=mesh,
        in_specs=in_specs,
        out_specs=out_specs,
        check_vma=False,
    )
```
